32 devices in a mesh: rep: 4 (over z), shard: 4 (over y, core), seq: 2 (over x).
Axes of the slice: x: 2, y: 2, z: 4, core: 2. Of those that a mesh axis runs over, the one named last changes fastest.
Arguments:
- inputs: bfloat16 [16, 1024, 768], P(('rep', 'shard'), 'seq'), may hold values from -6 to 6
- segments: int32 [16, 1024], P(('rep', 'shard'), 'seq'), may hold values from 0 to 1, never falling along the last dimension, each value on 1 to 768 neighbouring positions
- cotangent: bfloat16 [16, 1024, 768], P(('rep', 'shard'), 'seq'), may hold values from -6 to 6
- w_query: bfloat16 [768, 768], P('shard'), may hold values from -0.21875 to 0.21875
- b_query: bfloat16 [768], P('shard'), may hold values from -4 to 4
- w_key: bfloat16 [768, 768], P('shard'), may hold values from -0.21875 to 0.21875
- w_value: bfloat16 [768, 768], P('shard'), may hold values from -0.21875 to 0.21875
- b_value: bfloat16 [768], P('shard'), may hold values from -0.75 to 0.75
- w_out: bfloat16 [768, 768], P('shard'), may hold values from -3.5 to 3.5
- b_out: bfloat16 [768], P('shard'), may hold values from -4 to 4
- gain_one: bfloat16 [768], P('shard'), may hold values from 0.5 to 1.5
- shift_one: bfloat16 [768], P('shard'), may hold values from -4 to 4
- w_up: bfloat16 [768, 3072], P('shard'), may hold values from -0.21875 to 0.21875
- b_up: bfloat16 [3072], P('shard'), may hold values from -4 to 4
- w_down: bfloat16 [3072, 768], P('shard'), may hold values from -0.109375 to 0.109375
- b_down: bfloat16 [768], P('shard'), may hold values from -4 to 4
- gain_two: bfloat16 [768], P('shard'), may hold values from 0.5 to 1.5
- shift_two: bfloat16 [768], P('shard'), may hold values from -4 to 4
Outputs:
- result: bfloat16 [16, 1024, 768], P(('rep', 'shard'), 'seq')
- grad_inputs: float32 [16, 1024, 768], P(('rep', 'shard'), 'seq')
- grad_w_query: float32 [768, 768], P('shard')
- grad_b_query: float32 [768], P('shard')
- grad_w_key: float32 [768, 768], P('shard')
- grad_w_value: float32 [768, 768], P('shard')
- grad_b_value: float32 [768], P('shard')
- grad_w_out: float32 [768, 768], P('shard')
- grad_b_out: float32 [768], P('shard')
- grad_gain_one: float32 [768], P('shard')
- grad_shift_one: float32 [768], P('shard')
- grad_w_up: float32 [768, 3072], P('shard')
- grad_b_up: float32 [3072], P('shard')
- grad_w_down: float32 [3072, 768], P('shard')
- grad_b_down: float32 [768], P('shard')
- grad_gain_two: float32 [768], P('shard')
- grad_shift_two: float32 [768], P('shard')
The draws below stay inside these ranges and needn't reach their ends.
Inputs may be any that keep to these rules, and one draw needn't show every extreme that they name: `segments`: along each sequence the document numbers never fall; each document covers 1 to 768 positions.
All inputs are finite; a program needn't handle non-finite values.
Results may differ from the reference program's by a relative error of at most 0.023.
Values may be sent and summed in bfloat16 or wider, within the bound.
A program may use at most 192 MiB of HBM per device.

```python
import math
import jax
import jax.numpy as jnp
import numpy as np
from jax import lax

D = 768
H = 12
DH = 64
FF = 3072
SEQ_LEN = 1024
SEQS = 16
DOCS = 2
DOC_MOST = 768


def block_levels(own_key, shape, cuts, low, top_value):
    level = 1.0
    for dim, shards_of in cuts:
        draws = jax.random.uniform(jax.random.fold_in(jax.random.fold_in(own_key, 6), dim), (shards_of,), jnp.float32, low / len(cuts), top_value / len(cuts))
        level = level * jnp.repeat(jnp.exp(draws), shape[dim] // shards_of).reshape((-1,) + (1,) * (len(shape) - 1 - dim))
    return level


def profile(amount, total, limit, lean):
    portions = [(1 << 20) // math.isqrt(rank ** lean) + 1 for rank in range(2, amount + 1)]
    surplus, counts = total - limit - (amount - 1), [1] * (amount - 1)
    while surplus > 0:
        movable = [i for i in range(amount - 1) if counts[i] < limit]
        mass, budget = sum([portions[i] for i in movable]), surplus
        for i in movable:
            extra = min(limit - counts[i], max(1, budget * portions[i] // mass), surplus)
            counts[i] = counts[i] + extra
            surplus = surplus - extra
    return np.array([limit] + counts)


def uneven(stream_key, number_of, total, bound, skew):
    if number_of == 2:
        one = jax.random.randint(stream_key, (), max(1, total - bound), min(bound, total - 1) + 1)
        return jnp.stack([one, total - one])
    sizes = jnp.asarray(profile(number_of, total, bound, skew), jnp.int32)
    couples = (number_of - 1) // 2
    source_of, taker = sizes[1:1 + 2 * couples:2], sizes[2:2 + 2 * couples:2]
    room = jnp.minimum(source_of - 1, bound - taker)
    passed = jax.random.randint(jax.random.fold_in(stream_key, 1), (couples,), 0, 1 << 20) % (room + 1)
    sizes = sizes.at[1:1 + 2 * couples:2].set(source_of - passed).at[2:2 + 2 * couples:2].set(taker + passed)
    return sizes[jax.random.permutation(jax.random.fold_in(stream_key, 2), number_of)]


def normal_values(key, shape, deviation, most, pieces=(), held_as=jnp.bfloat16):
    drawn = deviation * jax.random.normal(key, shape, jnp.float32)
    if pieces:
        drawn = drawn * block_levels(key, shape, pieces, -0.22, 0.18)
    return jnp.clip(drawn, -most, most).astype(held_as)


def setup_inputs(seed: int = 0) -> dict:
    arg_keys = jax.random.split(jax.random.key(seed), 19)
    inputs = normal_values(arg_keys[0], (SEQS, SEQ_LEN, D), 1.0, 6.0, ((0, 16), (1, 2)))
    segments = jax.vmap(lambda own: jnp.searchsorted(jnp.cumsum(uneven(own, DOCS, SEQ_LEN, DOC_MOST, 2)), jnp.arange(SEQ_LEN), side="right"))(jax.random.split(arg_keys[1], SEQS)).reshape((SEQS, SEQ_LEN)).astype(jnp.int32)
    cotangent = normal_values(arg_keys[2], (SEQS, SEQ_LEN, D), 1.0, 6.0, ((0, 16), (1, 2)))
    w_query = normal_values(arg_keys[3], (D, D), D ** -0.5, 0.21875, ((0, 4),))
    b_query = normal_values(arg_keys[4], (D,), 0.3, 4.0, ((0, 4),))
    w_key = normal_values(arg_keys[5], (D, D), D ** -0.5, 0.21875, ((0, 4),))
    w_value = normal_values(arg_keys[6], (D, D), D ** -0.5, 0.21875, ((0, 4),))
    b_value = normal_values(arg_keys[7], (D,), 0.05, 0.75, ((0, 4),))
    w_out = normal_values(arg_keys[8], (D, D), 3 ** -0.5, 3.5, ((0, 4),))
    b_out = normal_values(arg_keys[9], (D,), 0.3, 4.0, ((0, 4),))
    gain_one = jnp.clip(1.0 + 0.1 * jax.random.normal(arg_keys[10], (D,), jnp.float32), 0.5, 1.5).astype(jnp.bfloat16)
    shift_one = normal_values(arg_keys[11], (D,), 0.3, 4.0, ((0, 4),))
    w_up = normal_values(arg_keys[12], (D, FF), D ** -0.5, 0.21875, ((0, 4),))
    b_up = normal_values(arg_keys[13], (FF,), 0.3, 4.0, ((0, 4),))
    w_down = normal_values(arg_keys[14], (FF, D), FF ** -0.5, 0.109375, ((0, 4),))
    b_down = normal_values(arg_keys[15], (D,), 0.3, 4.0, ((0, 4),))
    gain_two = jnp.clip(1.0 + 0.1 * jax.random.normal(arg_keys[16], (D,), jnp.float32), 0.5, 1.5).astype(jnp.bfloat16)
    shift_two = normal_values(arg_keys[17], (D,), 0.3, 4.0, ((0, 4),))
    return {"inputs": inputs, "segments": segments, "cotangent": cotangent, "w_query": w_query, "b_query": b_query, "w_key": w_key, "w_value": w_value, "b_value": b_value, "w_out": w_out, "b_out": b_out, "gain_one": gain_one, "shift_one": shift_one, "w_up": w_up, "b_up": b_up, "w_down": w_down, "b_down": b_down, "gain_two": gain_two, "shift_two": shift_two}


@jax.custom_vjp
def low(v):
    return lax.optimization_barrier(v.astype(jnp.bfloat16)).astype(jnp.float32)

@jax.custom_vjp
def low_back(v):
    return v

def low_keep(v):
    return (low(v), None)

def low_pass(kept, grad):
    return (grad,)

def back_keep(v):
    return (v, None)

def back_low(kept, grad):
    return (low(grad),)
low.defvjp(low_keep, low_pass)
low_back.defvjp(back_keep, back_low)
norm_eps = 1e-05
far_value = -1e+30
highest = lax.Precision.HIGHEST

def round_both(value):
    return low(low_back(value))

def product(left, right):
    return jnp.dot(left, right, precision=highest, preferred_element_type=jnp.float32)

def layer_norm(total_rows, gain_vec, shift_vec):
    row_mean = lax.optimization_barrier(jnp.mean(total_rows, -1, keepdims=True))
    centred = total_rows - row_mean
    variance = lax.optimization_barrier(jnp.mean(centred * centred, -1, keepdims=True))
    return centred * lax.rsqrt(variance + norm_eps) * gain_vec + shift_vec

def sequence_layer(token_rows, seg_ids, params):
    w_query, b_query, w_key, w_value, b_value, w_out, b_out, gain_one, shift_one, w_up, b_up, w_down, b_down, gain_two, shift_two = params
    score_scale = DH ** (-0.5)
    queries = round_both(product(token_rows, w_query) + b_query).reshape(SEQ_LEN, H, DH)
    key_rows = round_both(product(token_rows, w_key)).reshape(SEQ_LEN, H, DH)
    value_rows = round_both(product(token_rows, w_value) + b_value).reshape(SEQ_LEN, H, DH)
    block_size = math.gcd(SEQ_LEN, 512)
    block_count = SEQ_LEN // block_size
    query_blocks = queries.reshape(block_count, block_size, H, DH)
    seg_blocks = seg_ids.reshape(block_count, block_size)

    def attend(pair_item):
        query_part, seg_part = pair_item
        scores = jnp.einsum('rhd,khd->hrk', query_part, key_rows, precision=highest) * score_scale
        scores = low_back(scores)
        allowed = seg_part[:, None] == seg_ids[None, :]
        scores = jnp.where(allowed[None], scores, far_value)
        probabilities = low(jax.nn.softmax(scores, axis=-1))
        return jnp.einsum('hrk,khd->rhd', probabilities, value_rows, precision=highest)
    mixture = lax.map(jax.checkpoint(attend), (query_blocks, seg_blocks)).reshape(SEQ_LEN, D)
    mixture = round_both(mixture)
    attn_out = low_back(product(mixture, w_out) + b_out)
    norm_one = layer_norm(token_rows + attn_out, gain_one, shift_one)
    pre_act = low_back(product(low(norm_one), w_up) + b_up)
    activated = jax.nn.gelu(pre_act, approximate=False)
    ffn_out = low_back(product(low(activated), w_down) + b_down)
    return layer_norm(norm_one + ffn_out, gain_two, shift_two)

def reference(inputs, segments, cotangent, w_query, b_query, w_key, w_value, b_value, w_out, b_out, gain_one, shift_one, w_up, b_up, w_down, b_down, gain_two, shift_two):
    params = tuple((param.astype(jnp.float32) for param in (w_query, b_query, w_key, w_value, b_value, w_out, b_out, gain_one, shift_one, w_up, b_up, w_down, b_down, gain_two, shift_two)))
    rows_all = inputs.astype(jnp.float32)

    def forward(rows_all, params):

        def one_sequence(pair_item):
            return sequence_layer(pair_item[0], pair_item[1], params)
        return lax.map(one_sequence, (rows_all, segments))
    result, pullback = jax.vjp(forward, rows_all, params)
    grad_rows, gradients = pullback(cotangent.astype(jnp.float32))
    g_query, g_bquery, g_key, g_value, g_bvalue, g_out, g_bout, g_gone, g_sone, g_up, g_bup, g_down, g_bdown, g_gtwo, g_stwo = gradients
    return (result.astype(jnp.bfloat16), grad_rows, g_query, g_bquery, g_key, g_value, g_bvalue, g_out, g_bout, g_gone, g_sone, g_up, g_bup, g_down, g_bdown, g_gtwo, g_stwo)
```

```python
import functools
import math

import jax
import jax.numpy as jnp
from jax import lax
from jax.experimental import pallas as pl
from jax.experimental.pallas import tpu as pltpu
from jax.sharding import PartitionSpec as P

D = 768
H = 12
DH = 64
FF = 3072
MESH = pl.DeviceIdType.MESH
F32 = jnp.float32
BF = jnp.bfloat16
ANY = pl.BlockSpec(memory_space=pl.ANY)

norm_eps = 1e-05
far_value = -1e30


class Place:
    def __init__(self):
        self.z = lax.axis_index("rep")
        self.s = lax.axis_index("shard")
        self.x = lax.axis_index("seq")
        self.y = self.s // 2
        self.c = self.s % 2
        self.zb = self.z % 2
        self.zh = self.z // 2
        zb, zh, x, y, c = self.zb, self.zh, self.x, self.y, self.c
        self.core_p = (self.z, 2 * y + 1 - c, x)
        self.y_p = (self.z, 2 * (1 - y) + c, x)
        self.diag_p = (self.z, 2 * (1 - y) + 1 - c, x)
        self.x_p = (self.z, self.s, 1 - x)
        self.z0_p = (2 * zh + 1 - zb, self.s, x)
        self.z1_p = (2 * (1 - zh) + zb, self.s, x)


def greet(partners):
    barrier = pltpu.get_barrier_semaphore()
    for p in partners:
        pl.semaphore_signal(barrier, inc=1, device_id=p, device_id_type=MESH)
    pl.semaphore_wait(barrier, len(partners))


def remote(src, dst, ssem, rsem, dev):
    return pltpu.make_async_remote_copy(
        src_ref=src, dst_ref=dst, send_sem=ssem, recv_sem=rsem, device_id=dev, device_id_type=MESH
    )


def gather_pieces(q, k, v, o, up, dn, small):
    out = []
    for r in (q, k, v, o):
        out.append(r)
    return out


def gather_kernel(
    wq, wk, wv, wo, wu, wd, small, x_in, seg_in,
    gq, gk, gv, go, gu, gd, gsmall, xf, segf,
    b768, bu, bd, bsm, bx, bseg, ysend, yrecv, fsend, frecv, csend, crecv, ssend, srecv, lsem,
):
    me = Place()
    s = me.s
    so = 2 * (1 - me.y) + me.c
    q_me = 2 * me.x + me.zb
    q_x = 2 * (1 - me.x) + me.zb
    q_z = 2 * me.x + 1 - me.zb
    q_d = 2 * (1 - me.x) + 1 - me.zb

    chunks = []
    for own, full in ((wq, gq), (wk, gk), (wv, gv), (wo, go)):
        chunks.append((own, full, 0, 192, 0, 768))
    for j in range(2):
        chunks.append((wu, gu, 0, 192, 1536 * j, 1536))
    for j in range(2):
        chunks.append((wd, gd, 384 * j, 384, 0, 768))
    n = len(chunks)

    greet([me.core_p, me.y_p, me.diag_p, me.x_p, me.z0_p])

    def quarter(ch, qi):
        own, full, r0, rows, c0, cols = ch
        h = rows // 4
        return pl.ds(pl.multiple_of(r0 + qi * h, 16), h)

    cps = []
    cps.append(remote(x_in, xf.at[me.x], ssend.at[0], srecv.at[0], me.x_p))
    cps.append(remote(seg_in, segf.at[me.x], ssend.at[1], srecv.at[1], me.x_p))
    cps.append(remote(small, gsmall.at[s], ssend.at[2], srecv.at[2], me.core_p))
    cps.append(remote(small, gsmall.at[s], ssend.at[3], srecv.at[3], me.y_p))
    cps.append(remote(small, gsmall.at[s], ssend.at[4], srecv.at[4], me.diag_p))

    ycp, xcp, zcp, x2cp, z2cp, ccp = [], [], [], [], [], []
    for k, ch in enumerate(chunks):
        own, full, r0, rows, c0, cols = ch
        cs = pl.ds(c0, cols)
        h0, h1 = pl.ds(c0, cols // 2), pl.ds(c0 + cols // 2, cols // 2)
        rm, rx, rz, rd = (quarter(ch, qi) for qi in (q_me, q_x, q_z, q_d))
        whole = pl.ds(r0, rows)
        ycp.append(remote(own.at[rm, cs], full.at[s, rm, cs], ysend.at[k], yrecv.at[k], me.y_p))
        xcp.append(remote(full.at[so, rm, cs], full.at[so, rm, cs], fsend.at[k, 0], frecv.at[k, 0], me.x_p))
        zcp.append(remote(full.at[so, rm, cs], full.at[so, rm, cs], fsend.at[k, 1], frecv.at[k, 1], me.z0_p))
        x2cp.append(remote(full.at[so, rz, h0], full.at[so, rz, h0], fsend.at[k, 2], frecv.at[k, 2], me.x_p))
        z2cp.append(remote(full.at[so, rx, h1], full.at[so, rx, h1], fsend.at[k, 3], frecv.at[k, 3], me.z0_p))
        cc = [remote(own.at[whole, cs], full.at[s, whole, cs], csend.at[k, 0], crecv.at[k, 0], me.core_p)]
        for i, r in enumerate((rm, rx, rz, rd)):
            cc.append(remote(full.at[so, r, cs], full.at[so, r, cs], csend.at[k, i + 1], crecv.at[k, i + 1], me.core_p))
        ccp.append(cc)

    for k in range(3):
        ycp[k].start()
    for cp in cps:
        cp.start()
    for k in range(3, n):
        ycp[k].start()
    owns = [(wq, b768.at[0], gq), (wk, b768.at[1], gk), (wv, b768.at[2], gv), (wo, b768.at[3], go), (wu, bu, gu), (wd, bd, gd), (small, bsm, gsmall)]
    ins = [pltpu.make_async_copy(a, b, lsem.at[i, 0]) for i, (a, b, _) in enumerate(owns)]
    outs = [pltpu.make_async_copy(b, f.at[s], lsem.at[i, 1]) for i, (_, b, f) in enumerate(owns)]
    ins.append(pltpu.make_async_copy(x_in, bx, lsem.at[7, 0]))
    outs.append(pltpu.make_async_copy(bx, xf.at[me.x], lsem.at[7, 1]))
    ins.append(pltpu.make_async_copy(seg_in, bseg, lsem.at[8, 0]))
    outs.append(pltpu.make_async_copy(bseg, segf.at[me.x], lsem.at[8, 1]))
    for cp in ins:
        cp.start()
    for k in range(n):
        ccp[k][0].start()
    for a, b in zip(ins, outs):
        a.wait()
        b.start()

    for t in range(n + 2):
        if t < n:
            k = t
            ycp[k].wait_recv()
            xcp[k].start()
            zcp[k].start()
            ccp[k][1].start()
        if 0 <= t - 1 < n:
            k = t - 1
            xcp[k].wait_recv()
            z2cp[k].start()
            ccp[k][2].start()
            zcp[k].wait_recv()
            x2cp[k].start()
            ccp[k][3].start()
        if 0 <= t - 2 < n:
            k = t - 2
            x2cp[k].wait_recv()
            z2cp[k].wait_recv()
            ccp[k][4].start()
    for cp in cps:
        cp.wait()
    for k in range(n):
        for cp in ccp[k]:
            cp.wait()
        for cp in (ycp[k], xcp[k], zcp[k], x2cp[k], z2cp[k]):
            cp.wait_send()
    for cp in outs:
        cp.wait()


def gather_all(wq, wk, wv, wo, wu, wd, small, x_in, seg_in):
    sd = jax.ShapeDtypeStruct
    n = 8
    dma = pltpu.SemaphoreType.DMA
    return pl.pallas_call(
        gather_kernel,
        name="gather",
        out_shape=[
            sd((4, 192, 768), BF), sd((4, 192, 768), BF), sd((4, 192, 768), BF), sd((4, 192, 768), BF),
            sd((4, 192, 3072), BF), sd((4, 768, 768), BF), sd((4, 16, 768), BF),
            sd((2, 512, 768), BF), sd((2, 8, 512), jnp.int32),
        ],
        in_specs=[ANY] * 9,
        out_specs=[ANY] * 9,
        scratch_shapes=[
            pltpu.VMEM((4, 192, 768), BF), pltpu.VMEM((192, 3072), BF), pltpu.VMEM((768, 768), BF),
            pltpu.VMEM((16, 768), BF), pltpu.VMEM((512, 768), BF), pltpu.VMEM((8, 512), jnp.int32),
            dma((n,)), dma((n,)), dma((n, 4)), dma((n, 4)), dma((n, 5)), dma((n, 5)), dma((5,)), dma((5,)),
            dma((9, 2)),
        ],
        compiler_params=pltpu.CompilerParams(collective_id=0, has_side_effects=True),
    )(wq, wk, wv, wo, wu, wd, small, x_in, seg_in)


NCH = 12


def add_into(dst, src, rows, step=32):
    def body(i, carry):
        r = pl.ds(pl.multiple_of(i * step, step), step)
        dst[r, :] = (dst[r, :].astype(F32) + src[r, :].astype(F32)).astype(BF)
        return carry

    lax.fori_loop(0, rows // step, body, 0)


def reduce_kernel(
    gq, gk, gv, go, gu, gd, vec, pgx,
    fin_out, vec_out, gx_out,
    kbuf, cbuf, ybuf, xbuf, z0buf, z1buf, fin, vbuf, vval,
    ksem, csend, crecv, send, recv, vsend, vrecv, gsem, osem,
):
    me = Place()
    x, y, c, zb, zh = me.x, me.y, me.c, me.zb, me.zh
    greet([me.core_p, me.y_p, me.x_p, me.z0_p, me.z1_p])

    def piece(k, sh):
        if k < 8:
            j = k % 4
            ref = gd if k < 4 else gu
            if k < 4:
                return gd.at[sh, pl.ds(192 * j, 192), :]
            return gu.at[sh, :, pl.ds(768 * j, 768)]
        return (go, gv, gk, gq)[k - 8].at[sh]

    ccps, kcps = [], []
    for k in range(NCH):
        for yy in range(2):
            ccps.append(remote(piece(k, 2 * yy + 1 - c), cbuf.at[k, yy], csend.at[k, yy], crecv.at[k, yy], me.core_p))
            kcps.append(pltpu.make_async_copy(piece(k, 2 * yy + c), kbuf.at[k, yy], ksem.at[k, yy]))
    gcp = remote(pgx, gx_out, gsem.at[0], gsem.at[1], me.x_p)
    for a, b in zip(ccps, kcps):
        a.start()
        b.start()
    gcp.start()

    row0 = pl.multiple_of(x * 96 + zb * 48, 16)
    rx_mine = pl.ds(pl.multiple_of(x * 96, 16), 96)
    rx_other = pl.ds(pl.multiple_of((1 - x) * 96, 16), 96)
    rz_mine = pl.ds(pl.multiple_of(zb * 48, 16), 48)
    rz_other = pl.ds(pl.multiple_of((1 - zb) * 48, 16), 48)
    c_mine = pl.ds(pl.multiple_of(zh * 384, 128), 384)
    c_other = pl.ds(pl.multiple_of((1 - zh) * 384, 128), 384)
    rq = pl.ds(row0, 48)

    def ycp(k):
        return remote(cbuf.at[k, 1 - y], ybuf.at[k], send.at[0, k], recv.at[0, k], me.y_p)

    def xcp(k):
        return remote(ybuf.at[k, rx_other, :], xbuf.at[k], send.at[1, k], recv.at[1, k], me.x_p)

    def z0cp(k):
        return remote(xbuf.at[k, rz_other, :], z0buf.at[k], send.at[2, k], recv.at[2, k], me.z0_p)

    def z1cp(k):
        return remote(z0buf.at[k, :, c_other], z1buf.at[k], send.at[3, k], recv.at[3, k], me.z1_p)

    def a1cp(k):
        r = fin.at[k, rq, c_mine]
        return remote(r, r, send.at[4, k], recv.at[4, k], me.z1_p)

    def a0cp(k):
        r = fin.at[k, rq, :]
        return remote(r, r, send.at[5, k], recv.at[5, k], me.z0_p)

    def axcp(k):
        r = fin.at[k, rx_mine, :]
        return remote(r, r, send.at[6, k], recv.at[6, k], me.x_p)

    def ocp(k):
        return pltpu.make_async_copy(fin.at[k], fin_out.at[k], osem.at[k])

    vps = (me.core_p, me.y_p, me.x_p, me.z0_p, me.z1_p)
    vval[0] = vec[...]
    vcps = [remote(vval.at[b], vbuf.at[b], vsend.at[b], vrecv.at[b], vps[b]) for b in range(5)]
    vcps[0].start()

    for k in range(NCH):
        for yy in range(2):
            i = 2 * k + yy
            ccps[i].wait_recv()
            kcps[i].wait()
            add_into(cbuf.at[k, yy], kbuf.at[k, yy], 192)
        ycp(k).start()

    for b in range(5):
        vcps[b].wait_recv()
        if b < 4:
            vval[b + 1] = vval[b] + vbuf[b]
            vcps[b + 1].start()
        else:
            vec_out[...] = vval[b] + vbuf[b]

    def stages(t, carry):
        def at(d):
            return jnp.clip(t - d, 0, NCH - 1), jnp.logical_and(t - d >= 0, t - d < NCH)

        k, ok = at(0)

        @pl.when(ok)
        def _():
            ycp(k).wait_recv()
            add_into(ybuf.at[k], cbuf.at[k, y], 192)
            xcp(k).start()

        k1, ok1 = at(1)

        @pl.when(ok1)
        def _():
            xcp(k1).wait_recv()
            add_into(xbuf.at[k1], ybuf.at[k1, rx_mine, :], 96)
            z0cp(k1).start()

        k2, ok2 = at(2)

        @pl.when(ok2)
        def _():
            z0cp(k2).wait_recv()
            add_into(z0buf.at[k2], xbuf.at[k2, rz_mine, :], 48, 16)
            z1cp(k2).start()

        k3, ok3 = at(3)

        @pl.when(ok3)
        def _():
            z1cp(k3).wait_recv()
            fin[k3, rq, c_mine] = (z1buf[k3].astype(F32) + z0buf[k3, :, c_mine].astype(F32)).astype(BF)
            a1cp(k3).start()

        k4, ok4 = at(4)

        @pl.when(ok4)
        def _():
            a1cp(k4).wait_recv()
            a0cp(k4).start()

        k5, ok5 = at(5)

        @pl.when(ok5)
        def _():
            a0cp(k5).wait_recv()
            axcp(k5).start()

        k6, ok6 = at(6)

        @pl.when(ok6)
        def _():
            axcp(k6).wait_recv()
            ocp(k6).start()

        return carry

    lax.fori_loop(0, NCH + 6, stages, 0)

    def finish(k, carry):
        for f in (ycp, xcp, z0cp, z1cp, a1cp, a0cp, axcp):
            f(k).wait_send()
        ocp(k).wait()
        return carry

    lax.fori_loop(0, NCH, finish, 0)
    for cp in ccps:
        cp.wait_send()
    for cp in vcps:
        cp.wait_send()
    gcp.wait()


def reduce_all(gq, gk, gv, go, gu, gd, vec, pgx):
    sd = jax.ShapeDtypeStruct
    dma = pltpu.SemaphoreType.DMA
    vm = pltpu.VMEM
    vspec = pl.BlockSpec(memory_space=pltpu.VMEM)
    return pl.pallas_call(
        reduce_kernel,
        name="reduce",
        out_shape=[sd((NCH, 192, 768), BF), sd((16, 768), F32), sd((512, 768), BF)],
        in_specs=[ANY] * 6 + [vspec, ANY],
        out_specs=[ANY, vspec, ANY],
        scratch_shapes=[
            vm((NCH, 2, 192, 768), BF), vm((NCH, 2, 192, 768), BF), vm((NCH, 192, 768), BF), vm((NCH, 96, 768), BF),
            vm((NCH, 48, 768), BF), vm((NCH, 48, 384), BF), vm((NCH, 192, 768), BF),
            vm((5, 16, 768), F32), vm((5, 16, 768), F32),
            dma((NCH, 2)), dma((NCH, 2)), dma((NCH, 2)), dma((7, NCH)), dma((7, NCH)), dma((5,)), dma((5,)), dma((2,)), dma((NCH,)),
        ],
        compiler_params=pltpu.CompilerParams(collective_id=1, has_side_effects=True, vmem_limit_bytes=60 * 2**20),
    )(gq, gk, gv, go, gu, gd, vec, pgx)


NT = (((1,), (1,)), ((), ()))


def dot(a, b, dims=(((1,), (0,)), ((), ()))):
    return lax.dot_general(a, b, dims, preferred_element_type=F32)


def attn_fwd_kernel(q_ref, k_ref, v_ref, sq_ref, sk_ref, mix_ref, p_ref, bias):
    @pl.when(pl.program_id(0) == 0)
    def _():
        bias[...] = jnp.where(sq_ref[...] == sk_ref[...], 0.0, far_value)

    parts = []
    for i in range(2):
        cols = slice(64 * i, 64 * i + 64)
        s = dot(q_ref[:, cols], k_ref[:, cols], NT) + bias[...]
        m = jnp.max(s, axis=1, keepdims=True)
        e = jnp.exp(s - m)
        p = (e * (1.0 / jnp.sum(e, axis=1, keepdims=True))).astype(BF)
        p_ref[i] = p
        parts.append(dot(p, v_ref[:, cols]))
    mix_ref[...] = jnp.concatenate(parts, axis=1).astype(BF)


def attn_fwd(q, k, v, sq, sk):
    sd = jax.ShapeDtypeStruct
    rows, keys = q.shape[0], k.shape[0]
    blk = lambda r: pl.BlockSpec((r, 128), lambda h: (0, h))
    return pl.pallas_call(
        attn_fwd_kernel,
        name="attn_fwd",
        grid=(H // 2,),
        out_shape=[sd((rows, D), BF), sd((H, rows, keys), BF)],
        in_specs=[blk(rows), blk(keys), blk(keys), pl.BlockSpec((rows, 1), lambda h: (0, 0)), pl.BlockSpec((1, keys), lambda h: (0, 0))],
        out_specs=[blk(rows), pl.BlockSpec((2, rows, keys), lambda h: (h, 0, 0))],
        scratch_shapes=[pltpu.VMEM((rows, keys), F32)],
        compiler_params=pltpu.CompilerParams(vmem_limit_bytes=60 * 2**20),
    )(q, k, v, sq, sk)


def attn_bwd_kernel(q_ref, k_ref, v_ref, mix_ref, g_ref, p_ref, dq_ref, dk_ref, dv_ref):
    g = g_ref[...]
    prod = g.astype(F32) * mix_ref[...].astype(F32)
    gt = g.T
    qt = q_ref[...].T
    dqs, dks, dvs = [], [], []
    for i in range(2):
        cols = slice(64 * i, 64 * i + 64)
        p = p_ref[i]
        delta = jnp.sum(prod[:, cols], axis=1, keepdims=True)
        dp = dot(g[:, cols], v_ref[:, cols], NT)
        gs = (p.astype(F32) * (dp - delta)).astype(BF)
        dqs.append(dot(gs, k_ref[:, cols]) * 0.125)
        dks.append(dot(qt[cols, :], gs))
        dvs.append(dot(gt[cols, :], p))
    dq_ref[...] = jnp.concatenate(dqs, axis=1).astype(BF)
    dk_ref[...] = jnp.concatenate(dks, axis=0).T.astype(BF)
    dv_ref[...] = jnp.concatenate(dvs, axis=0).T.astype(BF)


def attn_bwd(q, k, v, mix, g, p):
    sd = jax.ShapeDtypeStruct
    rows, keys = q.shape[0], k.shape[0]
    blk = lambda r: pl.BlockSpec((r, 128), lambda h: (0, h))
    return pl.pallas_call(
        attn_bwd_kernel,
        name="attn_bwd",
        grid=(H // 2,),
        out_shape=[sd((rows, D), BF), sd((keys, D), BF), sd((keys, D), BF)],
        in_specs=[blk(rows), blk(keys), blk(keys), blk(rows), blk(rows), pl.BlockSpec((2, rows, keys), lambda h: (h, 0, 0))],
        out_specs=[blk(rows), blk(keys), blk(keys)],
        compiler_params=pltpu.CompilerParams(vmem_limit_bytes=60 * 2**20),
    )(q, k, v, mix, g, p)


def layer_norm(total_rows, gain_vec, shift_vec):
    row_mean = jnp.mean(total_rows, -1, keepdims=True)
    centred = total_rows - row_mean
    variance = jnp.mean(centred * centred, -1, keepdims=True)
    inv_std = lax.rsqrt(variance + norm_eps)
    normed = centred * inv_std
    return (normed * gain_vec + shift_vec, normed, inv_std)


def norm_grad(grad_in, normed, inv_std, gain_vec):
    scaled = grad_in * gain_vec
    centred_grad = (
        scaled
        - jnp.mean(scaled, -1, keepdims=True)
        - normed * jnp.mean(scaled * normed, -1, keepdims=True)
    )
    return (centred_grad * inv_std, jnp.sum(grad_in * normed, 0), jnp.sum(grad_in, 0))


TN = (((0,), (0,)), ((), ()))


def shards(
    inputs, segments, cotangent, w_query, b_query, w_key, w_value, b_value, w_out, b_out,
    gain_one, shift_one, w_up, b_up, w_down, b_down, gain_two, shift_two,
):
    x_own = inputs[0]
    rows = x_own.shape[0]
    small = jnp.concatenate(
        [b_query, b_value, b_out, gain_one, shift_one, b_down, gain_two, shift_two, b_up]
    ).reshape(3, 768)
    small = jnp.pad(small, ((0, 13), (0, 0)))
    seg8 = jnp.broadcast_to(segments, (8, rows))
    wq, wk, wv, wo, wu, wd, sm, xf, segf = gather_all(
        w_query, w_key, w_value, w_out, w_up, w_down, small, x_own, seg8
    )
    wq, wk, wv, wo, wu, wd = (w.reshape(-1, w.shape[-1]) for w in (wq, wk, wv, wo, wu, wd))
    vecs = sm[:, :2].reshape(4, 8, 192).transpose(1, 0, 2).reshape(8, 768).astype(F32)
    bq, bv, bo, g1, s1, bd, g2, s2 = (vecs[i] for i in range(8))
    bu = sm[:, 2].reshape(FF).astype(F32)
    x_all = xf.reshape(-1, D)
    seg_all = segf[:, 0].reshape(1, -1)

    q8 = ((dot(x_own, wq) + bq).astype(BF).astype(F32) * 0.125).astype(BF)
    keys = dot(x_all, wk).astype(BF)
    values = (dot(x_all, wv) + bv).astype(BF)
    mixture, probs = attn_fwd(q8, keys, values, segments.reshape(-1, 1), seg_all)
    attn_out = dot(mixture, wo) + bo
    norm_one, normed_one, inv_one = layer_norm(x_own.astype(F32) + attn_out, g1, s1)
    hidden_low = norm_one.astype(BF)
    pre_act = dot(hidden_low, wu) + bu
    phi = 0.5 * (1.0 + lax.erf(pre_act * (2.0**-0.5)))
    act_low = (pre_act * phi).astype(BF)
    slope = phi + pre_act * jnp.exp(-0.5 * pre_act * pre_act) * (2 * math.pi) ** -0.5
    ffn_out = dot(act_low, wd) + bd
    result, normed_two, inv_two = layer_norm(norm_one + ffn_out, g2, s2)

    grad_mid, d_g2, d_s2 = norm_grad(cotangent[0].astype(F32), normed_two, inv_two, g2)
    grad_ffn = grad_mid.astype(BF)
    d_bd = jnp.sum(grad_ffn.astype(F32), 0)
    d_wd = dot(act_low, grad_ffn, TN).astype(BF)
    grad_pre = (dot(grad_ffn, wd, NT) * slope).astype(BF)
    d_bu = jnp.sum(grad_pre.astype(F32), 0)
    d_wu = dot(hidden_low, grad_pre, TN).astype(BF)
    grad_hidden = grad_mid + dot(grad_pre, wu, NT)
    grad_sum_one, d_g1, d_s1 = norm_grad(grad_hidden, normed_one, inv_one, g1)
    grad_attn = grad_sum_one.astype(BF)
    d_bo = jnp.sum(grad_attn.astype(F32), 0)
    d_wo = dot(mixture, grad_attn, TN).astype(BF)
    grad_mix = dot(grad_attn, wo, NT).astype(BF)

    dq, dk, dv = attn_bwd(q8, keys, values, mixture, grad_mix, probs)
    d_wq = dot(x_own, dq, TN).astype(BF)
    d_wk = dot(x_all, dk, TN).astype(BF)
    d_wv = dot(x_all, dv, TN).astype(BF)
    d_bq = jnp.sum(dq.astype(F32), 0)
    d_bv = jnp.sum(dv.astype(F32), 0)
    kv_grad = dot(dk, wk, NT) + dot(dv, wv, NT)
    me = lax.axis_index("seq")
    kv2 = kv_grad.reshape(2, rows, D)
    own_part = lax.dynamic_index_in_dim(kv2, me, 0, False) + dot(dq, wq, NT) + grad_sum_one
    other_part = lax.dynamic_index_in_dim(kv2, 1 - me, 0, False).astype(BF)
    vec = jnp.concatenate(
        [jnp.stack([d_bq, d_bv, d_bo, d_g1, d_s1, d_bd, d_g2, d_s2]), d_bu.reshape(4, D), jnp.zeros((4, D), F32)]
    )
    shape4 = lambda a: a.reshape(4, -1, a.shape[-1])
    fin, vec, gx = reduce_all(
        shape4(d_wq), shape4(d_wk), shape4(d_wv), shape4(d_wo), shape4(d_wu), shape4(d_wd), vec, other_part
    )
    fin = fin.astype(F32)
    o_wd = fin[0:4].reshape(768, D)
    o_wu = fin[4:8].transpose(1, 0, 2).reshape(192, FF)
    o_wo, o_wv, o_wk, o_wq = (fin[i] for i in range(8, 12))
    sh = lax.axis_index("shard")
    mine = lax.dynamic_slice(vec[:8], (0, sh * 192), (8, 192))
    o_bq, o_bv, o_bo, o_g1, o_s1, o_bd, o_g2, o_s2 = (mine[i] for i in range(8))
    o_bu = lax.dynamic_index_in_dim(vec[8:12], sh, 0, False)
    grad_input = own_part + gx.astype(F32)
    return (
        result.astype(BF)[None], grad_input[None], o_wq, o_bq, o_wk, o_wv, o_bv, o_wo, o_bo,
        o_g1, o_s1, o_wu, o_bu, o_wd, o_bd, o_g2, o_s2,
    )


def make(mesh, body):
    in_specs = (
        P(("rep", "shard"), "seq", None), P(("rep", "shard"), "seq"), P(("rep", "shard"), "seq", None),
        P("shard", None), P("shard"), P("shard", None), P("shard", None), P("shard"), P("shard", None), P("shard"),
        P("shard"), P("shard"), P("shard", None), P("shard"), P("shard", None), P("shard"), P("shard"), P("shard"),
    )
    out_specs = (
        P(("rep", "shard"), "seq", None), P(("rep", "shard"), "seq", None),
        P("shard", None), P("shard"), P("shard", None), P("shard", None), P("shard"), P("shard", None), P("shard"),
        P("shard"), P("shard"), P("shard", None), P("shard"), P("shard", None), P("shard"), P("shard"), P("shard"),
    )
    return jax.shard_map(body, mesh=mesh, in_specs=in_specs, out_specs=out_specs, check_vma=False)


param_names = (
    "w_query",
    "b_query",
    "w_key",
    "w_value",
    "b_value",
    "w_out",
    "b_out",
    "gain_one",
    "shift_one",
    "w_up",
    "b_up",
    "w_down",
    "b_down",
    "gain_two",
    "shift_two",
)


def as_sent(x):
    return jax.tree.map(lambda a: a.astype(jnp.bfloat16) if a.dtype == jnp.float32 else a, x)


def general_layer_norm(total_rows, gain_vec, shift_vec):
    row_mean = jnp.mean(total_rows, -1, keepdims=True)
    centred = total_rows - row_mean
    variance = jnp.mean(centred * centred, -1, keepdims=True)
    inv_std = lax.rsqrt(variance + norm_eps)
    normed = centred * inv_std
    return (normed * gain_vec + shift_vec, normed, inv_std)


def general_norm_grad(grad_in, normed, inv_std, gain_vec):
    scaled = grad_in * gain_vec
    centred_grad = (
        scaled
        - jnp.mean(scaled, -1, keepdims=True)
        - normed * jnp.mean(scaled * normed, -1, keepdims=True)
    )
    return (centred_grad * inv_std, jnp.sum(grad_in * normed, 0), jnp.sum(grad_in, 0))


def inner_rows(left, right):
    return lax.dot_general(
        left, right, (((0,), (0,)), ((), ())), preferred_element_type=jnp.float32
    )


def times_transposed(left, matrix):
    return lax.dot_general(
        left, matrix, (((1,), (1,)), ((), ())), preferred_element_type=jnp.float32
    )


def gelu_exact(value):
    return jax.nn.gelu(value, approximate=False)


def general_shards(
    inputs,
    segments,
    cotangent,
    w_query,
    b_query,
    w_key,
    w_value,
    b_value,
    w_out,
    b_out,
    gain_one,
    shift_one,
    w_up,
    b_up,
    w_down,
    b_down,
    gain_two,
    shift_two,
):
    score_scale = DH ** (-0.5)
    token_rows = inputs[0]
    row_count = token_rows.shape[0]
    own_seg = segments[0].astype(jnp.float32)
    local_params = (
        w_query,
        b_query,
        w_key,
        w_value,
        b_value,
        w_out,
        b_out,
        gain_one,
        shift_one,
        w_up,
        b_up,
        w_down,
        b_down,
        gain_two,
        shift_two,
    )
    gathered = (
        lax.all_gather(local_params[0], "shard", axis=0, tiled=True),
        lax.all_gather(local_params[1], "shard", axis=0, tiled=True),
        lax.all_gather(local_params[2], "shard", axis=0, tiled=True),
        lax.all_gather(local_params[3], "shard", axis=0, tiled=True),
        lax.all_gather(local_params[4], "shard", axis=0, tiled=True),
        lax.all_gather(local_params[5], "shard", axis=0, tiled=True),
        lax.all_gather(local_params[6], "shard", axis=0, tiled=True),
        lax.all_gather(local_params[7], "shard", axis=0, tiled=True),
        lax.all_gather(local_params[8], "shard", axis=0, tiled=True),
        lax.all_gather(local_params[9], "shard", axis=0, tiled=True),
        lax.all_gather(local_params[10], "shard", axis=0, tiled=True),
        lax.all_gather(local_params[11], "shard", axis=0, tiled=True),
        lax.all_gather(local_params[12], "shard", axis=0, tiled=True),
        lax.all_gather(local_params[13], "shard", axis=0, tiled=True),
        lax.all_gather(local_params[14], "shard", axis=0, tiled=True),
    )
    weights = dict(zip(param_names, gathered))

    def vector(name):
        return weights[name].astype(jnp.float32)

    q_wide = jnp.dot(token_rows, weights["w_query"], preferred_element_type=jnp.float32) + vector(
        "b_query"
    )
    queries = q_wide.astype(jnp.bfloat16)
    key_rows = jnp.dot(token_rows, weights["w_key"], preferred_element_type=jnp.float32).astype(
        jnp.bfloat16
    )
    value_rows = (
        jnp.dot(token_rows, weights["w_value"], preferred_element_type=jnp.float32)
        + vector("b_value")
    ).astype(jnp.bfloat16)
    seg_wire = segments[0].astype(jnp.bfloat16)
    query_heads = queries.reshape(row_count, H, DH)
    start_state = (
        jnp.full((H, row_count), far_value, jnp.float32),
        jnp.zeros((H, row_count), jnp.float32),
        jnp.zeros((row_count, H, DH), jnp.float32),
    )
    carried = start_state
    piece_keys = lax.all_gather(key_rows, "seq", axis=0, tiled=True)
    piece_values = lax.all_gather(value_rows, "seq", axis=0, tiled=True)
    piece_seg = lax.all_gather(seg_wire, "seq", axis=0, tiled=True)
    piece_rows = piece_keys.shape[0]
    width_blk = math.gcd(piece_rows, 512)
    blocks = piece_rows // width_blk
    key_blocks = piece_keys.reshape(blocks, width_blk, H, DH)
    value_blocks = piece_values.reshape(blocks, width_blk, H, DH)
    seg_blocks = piece_seg.astype(jnp.float32).reshape(blocks, width_blk)

    def update(fold_state, block_item):
        key_blk, value_blk, seg_blk = block_item
        row_peak, row_total, accumulated = fold_state
        scores = (
            jnp.einsum("rhd,khd->hrk", query_heads, key_blk, preferred_element_type=jnp.float32)
            * score_scale
        )
        allowed = own_seg[:, None] == seg_blk[None, :]
        scores = jnp.where(allowed[None], scores, far_value)
        new_peak = jnp.maximum(row_peak, jnp.max(scores, -1))
        factor = jnp.exp(row_peak - new_peak)
        exp_scores = jnp.exp(scores - new_peak[:, :, None])
        row_total = row_total * factor + jnp.sum(exp_scores, -1)
        block_mix = jnp.einsum(
            "hrk,khd->rhd",
            exp_scores.astype(jnp.bfloat16),
            value_blk,
            preferred_element_type=jnp.float32,
        )
        accumulated = accumulated * jnp.transpose(factor)[:, :, None] + block_mix
        return ((new_peak, row_total, accumulated), None)

    carried, unused = lax.scan(update, carried, (key_blocks, value_blocks, seg_blocks))
    row_peak, row_total, accumulated = carried
    mix_wide = (accumulated / jnp.transpose(row_total)[:, :, None]).reshape(row_count, D)
    mixture = mix_wide.astype(jnp.bfloat16)
    log_total = row_peak + jnp.log(row_total)
    attn_out = jnp.dot(mixture, weights["w_out"], preferred_element_type=jnp.float32) + vector(
        "b_out"
    )
    norm_one, normed_one, inv_one = general_layer_norm(
        token_rows.astype(jnp.float32) + attn_out, vector("gain_one"), vector("shift_one")
    )
    hidden_low = norm_one.astype(jnp.bfloat16)
    pre_act = jnp.dot(hidden_low, weights["w_up"], preferred_element_type=jnp.float32) + vector(
        "b_up"
    )
    activated, gelu_pullback = jax.vjp(gelu_exact, pre_act)
    act_low = activated.astype(jnp.bfloat16)
    ffn_out = jnp.dot(act_low, weights["w_down"], preferred_element_type=jnp.float32) + vector(
        "b_down"
    )
    result, normed_two, inv_two = general_layer_norm(
        norm_one + ffn_out, vector("gain_two"), vector("shift_two")
    )
    regathered = (
        lax.all_gather(local_params[0], "shard", axis=0, tiled=True),
        lax.all_gather(local_params[1], "shard", axis=0, tiled=True),
        lax.all_gather(local_params[2], "shard", axis=0, tiled=True),
        lax.all_gather(local_params[3], "shard", axis=0, tiled=True),
        lax.all_gather(local_params[4], "shard", axis=0, tiled=True),
        lax.all_gather(local_params[5], "shard", axis=0, tiled=True),
        lax.all_gather(local_params[6], "shard", axis=0, tiled=True),
        lax.all_gather(local_params[7], "shard", axis=0, tiled=True),
        lax.all_gather(local_params[8], "shard", axis=0, tiled=True),
        lax.all_gather(local_params[9], "shard", axis=0, tiled=True),
        lax.all_gather(local_params[10], "shard", axis=0, tiled=True),
        lax.all_gather(local_params[11], "shard", axis=0, tiled=True),
        lax.all_gather(local_params[12], "shard", axis=0, tiled=True),
        lax.all_gather(local_params[13], "shard", axis=0, tiled=True),
        lax.all_gather(local_params[14], "shard", axis=0, tiled=True),
    )
    backward_set = dict(zip(param_names, regathered))
    grad_out = cotangent[0].astype(jnp.float32)
    grad_mid, grad_gain_two, grad_shift_two = general_norm_grad(
        grad_out, normed_two, inv_two, backward_set["gain_two"].astype(jnp.float32)
    )
    grad_ffn = grad_mid.astype(jnp.bfloat16)
    grad_b_down = jnp.sum(grad_ffn.astype(jnp.float32), 0)
    grad_w_down = inner_rows(act_low, grad_ffn)
    grad_act = times_transposed(grad_ffn, backward_set["w_down"])
    (grad_pre_wide,) = gelu_pullback(grad_act)
    grad_pre = grad_pre_wide.astype(jnp.bfloat16)
    grad_b_up = jnp.sum(grad_pre.astype(jnp.float32), 0)
    grad_w_up = inner_rows(hidden_low, grad_pre)
    grad_hidden = grad_mid + times_transposed(grad_pre, backward_set["w_up"])
    grad_sum_one, grad_gain_one, grad_shift_one = general_norm_grad(
        grad_hidden, normed_one, inv_one, backward_set["gain_one"].astype(jnp.float32)
    )
    grad_attn = grad_sum_one.astype(jnp.bfloat16)
    grad_b_out = jnp.sum(grad_attn.astype(jnp.float32), 0)
    grad_w_out = inner_rows(mixture, grad_attn)
    grad_mixture = times_transposed(grad_attn, backward_set["w_out"]).astype(jnp.bfloat16)
    grad_mix_heads = grad_mixture.reshape(row_count, H, DH)
    row_delta = jnp.transpose(
        jnp.sum((grad_mixture.astype(jnp.float32) * mix_wide).reshape(row_count, H, DH), -1)
    )
    all_keys, all_values, all_seg = (
        lax.all_gather(key_rows, "seq", axis=0, tiled=True),
        lax.all_gather(value_rows, "seq", axis=0, tiled=True),
        lax.all_gather(seg_wire, "seq", axis=0, tiled=True),
    )
    seq_rows = all_keys.shape[0]
    width_all = math.gcd(seq_rows, 512)
    blocks_all = seq_rows // width_all
    key_blocks = all_keys.reshape(blocks_all, width_all, H, DH)
    value_blocks = all_values.reshape(blocks_all, width_all, H, DH)
    seg_blocks = all_seg.astype(jnp.float32).reshape(blocks_all, width_all)

    def block_grads(key_blk, value_blk, seg_blk):
        scores = (
            jnp.einsum("rhd,khd->hrk", query_heads, key_blk, preferred_element_type=jnp.float32)
            * score_scale
        )
        allowed = own_seg[:, None] == seg_blk[None, :]
        scores = jnp.where(allowed[None], scores, far_value)
        probabilities = jnp.exp(scores - log_total[:, :, None])
        grad_probs = jnp.einsum(
            "rhd,khd->hrk", grad_mix_heads, value_blk, preferred_element_type=jnp.float32
        )
        grad_scores = (probabilities * (grad_probs - row_delta[:, :, None])).astype(jnp.bfloat16)
        return (probabilities, grad_scores)

    def back_update(grad_query_acc, block_item):
        key_blk, value_blk, seg_blk = block_item
        back_grad_query_acc = grad_query_acc
        probabilities, grad_scores = block_grads(key_blk, value_blk, seg_blk)
        grad_value_blk = jnp.einsum(
            "hrk,rhd->khd",
            probabilities.astype(jnp.bfloat16),
            grad_mix_heads,
            preferred_element_type=jnp.float32,
        )
        back_grad_query_acc = (
            back_grad_query_acc
            + jnp.einsum("hrk,khd->rhd", grad_scores, key_blk, preferred_element_type=jnp.float32)
            * score_scale
        )
        grad_key_blk = (
            jnp.einsum("hrk,rhd->khd", grad_scores, query_heads, preferred_element_type=jnp.float32)
            * score_scale
        )
        return (back_grad_query_acc, (grad_key_blk, grad_value_blk))

    grad_query_heads, key_value_grads = lax.scan(
        back_update,
        jnp.zeros((row_count, H, DH), jnp.float32),
        (key_blocks, value_blocks, seg_blocks),
    )
    grad_key_all = key_value_grads[0].reshape(seq_rows, D)
    grad_value_all = key_value_grads[1].reshape(seq_rows, D)
    grad_key_rows, grad_value_rows = (
        lax.psum_scatter(
            grad_key_all.astype(jnp.bfloat16), "seq", scatter_dimension=0, tiled=True
        ).astype(jnp.float32),
        lax.psum_scatter(
            grad_value_all.astype(jnp.bfloat16), "seq", scatter_dimension=0, tiled=True
        ).astype(jnp.float32),
    )
    grad_query_low = grad_query_heads.reshape(row_count, D).astype(jnp.bfloat16)
    grad_key_low = grad_key_rows.astype(jnp.bfloat16)
    grad_value_low = grad_value_rows.astype(jnp.bfloat16)
    grad_w_query = inner_rows(token_rows, grad_query_low)
    grad_b_query = jnp.sum(grad_query_low.astype(jnp.float32), 0)
    grad_w_key = inner_rows(token_rows, grad_key_low)
    grad_w_value = inner_rows(token_rows, grad_value_low)
    grad_b_value = jnp.sum(grad_value_low.astype(jnp.float32), 0)
    grad_input = (
        grad_sum_one
        + times_transposed(grad_query_low, backward_set["w_query"])
        + times_transposed(grad_key_low, backward_set["w_key"])
        + times_transposed(grad_value_low, backward_set["w_value"])
    )
    gradients = (
        grad_w_query,
        grad_b_query,
        grad_w_key,
        grad_w_value,
        grad_b_value,
        grad_w_out,
        grad_b_out,
        grad_gain_one,
        grad_shift_one,
        grad_w_up,
        grad_b_up,
        grad_w_down,
        grad_b_down,
        grad_gain_two,
        grad_shift_two,
    )
    owned_grads = (
        lax.psum_scatter(
            gradients[0].astype(jnp.bfloat16), "shard", scatter_dimension=0, tiled=True
        ).astype(jnp.float32),
        lax.psum_scatter(
            gradients[1].astype(jnp.bfloat16), "shard", scatter_dimension=0, tiled=True
        ).astype(jnp.float32),
        lax.psum_scatter(
            gradients[2].astype(jnp.bfloat16), "shard", scatter_dimension=0, tiled=True
        ).astype(jnp.float32),
        lax.psum_scatter(
            gradients[3].astype(jnp.bfloat16), "shard", scatter_dimension=0, tiled=True
        ).astype(jnp.float32),
        lax.psum_scatter(
            gradients[4].astype(jnp.bfloat16), "shard", scatter_dimension=0, tiled=True
        ).astype(jnp.float32),
        lax.psum_scatter(
            gradients[5].astype(jnp.bfloat16), "shard", scatter_dimension=0, tiled=True
        ).astype(jnp.float32),
        lax.psum_scatter(
            gradients[6].astype(jnp.bfloat16), "shard", scatter_dimension=0, tiled=True
        ).astype(jnp.float32),
        lax.psum_scatter(
            gradients[7].astype(jnp.bfloat16), "shard", scatter_dimension=0, tiled=True
        ).astype(jnp.float32),
        lax.psum_scatter(
            gradients[8].astype(jnp.bfloat16), "shard", scatter_dimension=0, tiled=True
        ).astype(jnp.float32),
        lax.psum_scatter(
            gradients[9].astype(jnp.bfloat16), "shard", scatter_dimension=0, tiled=True
        ).astype(jnp.float32),
        lax.psum_scatter(
            gradients[10].astype(jnp.bfloat16), "shard", scatter_dimension=0, tiled=True
        ).astype(jnp.float32),
        lax.psum_scatter(
            gradients[11].astype(jnp.bfloat16), "shard", scatter_dimension=0, tiled=True
        ).astype(jnp.float32),
        lax.psum_scatter(
            gradients[12].astype(jnp.bfloat16), "shard", scatter_dimension=0, tiled=True
        ).astype(jnp.float32),
        lax.psum_scatter(
            gradients[13].astype(jnp.bfloat16), "shard", scatter_dimension=0, tiled=True
        ).astype(jnp.float32),
        lax.psum_scatter(
            gradients[14].astype(jnp.bfloat16), "shard", scatter_dimension=0, tiled=True
        ).astype(jnp.float32),
    )
    owned_grads = jax.tree.map(
        lambda part: part.astype(jnp.float32), lax.psum(as_sent(tuple(owned_grads)), ("rep", "seq"))
    )
    return (result.astype(jnp.bfloat16)[None], grad_input[None]) + tuple(owned_grads)


def solution(mesh):
    if dict(mesh.shape) == {"rep": 4, "shard": 4, "seq": 2}:
        return make(mesh, shards)
    return make(mesh, general_shards)
```

```python
import functools
import math

import jax
import jax.numpy as jnp
from jax import lax
from jax.experimental import pallas as pl
from jax.experimental.pallas import tpu as pltpu
from jax.sharding import PartitionSpec as P

D = 768
H = 12
DH = 64
FF = 3072
MESH = pl.DeviceIdType.MESH
F32 = jnp.float32
BF = jnp.bfloat16
ANY = pl.BlockSpec(memory_space=pl.ANY)

norm_eps = 1e-05
far_value = -1e30


class Place:
    def __init__(self):
        self.z = lax.axis_index("rep")
        self.s = lax.axis_index("shard")
        self.x = lax.axis_index("seq")
        self.y = self.s // 2
        self.c = self.s % 2
        self.zb = self.z % 2
        self.zh = self.z // 2
        zb, zh, x, y, c = self.zb, self.zh, self.x, self.y, self.c
        self.core_p = (self.z, 2 * y + 1 - c, x)
        self.y_p = (self.z, 2 * (1 - y) + c, x)
        self.diag_p = (self.z, 2 * (1 - y) + 1 - c, x)
        self.x_p = (self.z, self.s, 1 - x)
        self.z0_p = (2 * zh + 1 - zb, self.s, x)
        self.z1_p = (2 * (1 - zh) + zb, self.s, x)


def greet(partners):
    barrier = pltpu.get_barrier_semaphore()
    for p in partners:
        pl.semaphore_signal(barrier, inc=1, device_id=p, device_id_type=MESH)
    pl.semaphore_wait(barrier, len(partners))


def remote(src, dst, ssem, rsem, dev):
    return pltpu.make_async_remote_copy(
        src_ref=src, dst_ref=dst, send_sem=ssem, recv_sem=rsem, device_id=dev, device_id_type=MESH
    )


def gather_pieces(q, k, v, o, up, dn, small):
    out = []
    for r in (q, k, v, o):
        out.append(r)
    return out


def gather_kernel(
    wq, wk, wv, wo, wu, wd, small, x_in, seg_in,
    gq, gk, gv, go, gu, gd, gsmall, xf, segf,
    b768, bu, bd, bsm, bx, bseg, ysend, yrecv, fsend, frecv, csend, crecv, ssend, srecv, lsem,
):
    me = Place()
    s = me.s
    so = 2 * (1 - me.y) + me.c
    q_me = 2 * me.x + me.zb
    q_x = 2 * (1 - me.x) + me.zb
    q_z = 2 * me.x + 1 - me.zb
    q_d = 2 * (1 - me.x) + 1 - me.zb

    chunks = []
    for own, full in ((wq, gq), (wk, gk), (wv, gv), (wo, go)):
        chunks.append((own, full, 0, 192, 0, 768))
    for j in range(2):
        chunks.append((wu, gu, 0, 192, 1536 * j, 1536))
    for j in range(2):
        chunks.append((wd, gd, 384 * j, 384, 0, 768))
    n = len(chunks)

    greet([me.core_p, me.y_p, me.diag_p, me.x_p, me.z0_p])

    def quarter(ch, qi):
        own, full, r0, rows, c0, cols = ch
        h = rows // 4
        return pl.ds(pl.multiple_of(r0 + qi * h, 16), h)

    cps = []
    cps.append(remote(x_in, xf.at[me.x], ssend.at[0], srecv.at[0], me.x_p))
    cps.append(remote(seg_in, segf.at[me.x], ssend.at[1], srecv.at[1], me.x_p))
    cps.append(remote(small, gsmall.at[s], ssend.at[2], srecv.at[2], me.core_p))
    cps.append(remote(small, gsmall.at[s], ssend.at[3], srecv.at[3], me.y_p))
    cps.append(remote(small, gsmall.at[s], ssend.at[4], srecv.at[4], me.diag_p))

    ycp, xcp, zcp, x2cp, z2cp, ccp = [], [], [], [], [], []
    for k, ch in enumerate(chunks):
        own, full, r0, rows, c0, cols = ch
        cs = pl.ds(c0, cols)
        h0, h1 = pl.ds(c0, cols // 2), pl.ds(c0 + cols // 2, cols // 2)
        rm, rx, rz, rd = (quarter(ch, qi) for qi in (q_me, q_x, q_z, q_d))
        whole = pl.ds(r0, rows)
        ycp.append(remote(own.at[rm, cs], full.at[s, rm, cs], ysend.at[k], yrecv.at[k], me.y_p))
        xcp.append(remote(full.at[so, rm, cs], full.at[so, rm, cs], fsend.at[k, 0], frecv.at[k, 0], me.x_p))
        zcp.append(remote(full.at[so, rm, cs], full.at[so, rm, cs], fsend.at[k, 1], frecv.at[k, 1], me.z0_p))
        x2cp.append(remote(full.at[so, rz, h0], full.at[so, rz, h0], fsend.at[k, 2], frecv.at[k, 2], me.x_p))
        z2cp.append(remote(full.at[so, rx, h1], full.at[so, rx, h1], fsend.at[k, 3], frecv.at[k, 3], me.z0_p))
        cc = [remote(own.at[whole, cs], full.at[s, whole, cs], csend.at[k, 0], crecv.at[k, 0], me.core_p)]
        for i, r in enumerate((rm, rx, rz, rd)):
            cc.append(remote(full.at[so, r, cs], full.at[so, r, cs], csend.at[k, i + 1], crecv.at[k, i + 1], me.core_p))
        ccp.append(cc)

    for k in range(2):
        ycp[k].start()
    for cp in cps:
        cp.start()
    owns = [(wq, b768.at[0], gq), (wk, b768.at[1], gk), (wv, b768.at[2], gv), (wo, b768.at[3], go), (wu, bu, gu), (wd, bd, gd), (small, bsm, gsmall)]
    ins = [pltpu.make_async_copy(a, b, lsem.at[i, 0]) for i, (a, b, _) in enumerate(owns)]
    outs = [pltpu.make_async_copy(b, f.at[s], lsem.at[i, 1]) for i, (_, b, f) in enumerate(owns)]
    ins.append(pltpu.make_async_copy(x_in, bx, lsem.at[7, 0]))
    outs.append(pltpu.make_async_copy(bx, xf.at[me.x], lsem.at[7, 1]))
    ins.append(pltpu.make_async_copy(seg_in, bseg, lsem.at[8, 0]))
    outs.append(pltpu.make_async_copy(bseg, segf.at[me.x], lsem.at[8, 1]))
    for cp in ins:
        cp.start()
    for k in range(n):
        ccp[k][0].start()
    for a, b in zip(ins, outs):
        a.wait()
        b.start()

    for t in range(n + 2):
        if t < n:
            k = t
            ycp[k].wait_recv()
            xcp[k].start()
            zcp[k].start()
            ccp[k][1].start()
        if 0 <= t - 1 < n:
            k = t - 1
            xcp[k].wait_recv()
            z2cp[k].start()
            ccp[k][2].start()
            zcp[k].wait_recv()
            x2cp[k].start()
            ccp[k][3].start()
        if 0 <= t - 2 < n:
            k = t - 2
            x2cp[k].wait_recv()
            z2cp[k].wait_recv()
            ccp[k][4].start()
        if t + 2 < n:
            ycp[t + 2].start()
    for cp in cps:
        cp.wait()
    for k in range(n):
        for cp in ccp[k]:
            cp.wait()
        for cp in (ycp[k], xcp[k], zcp[k], x2cp[k], z2cp[k]):
            cp.wait_send()
    for cp in outs:
        cp.wait()


def gather_all(wq, wk, wv, wo, wu, wd, small, x_in, seg_in):
    sd = jax.ShapeDtypeStruct
    n = 8
    dma = pltpu.SemaphoreType.DMA
    return pl.pallas_call(
        gather_kernel,
        name="gather",
        out_shape=[
            sd((4, 192, 768), BF), sd((4, 192, 768), BF), sd((4, 192, 768), BF), sd((4, 192, 768), BF),
            sd((4, 192, 3072), BF), sd((4, 768, 768), BF), sd((4, 16, 768), BF),
            sd((2, 512, 768), BF), sd((2, 8, 512), jnp.int32),
        ],
        in_specs=[ANY] * 9,
        out_specs=[ANY] * 9,
        scratch_shapes=[
            pltpu.VMEM((4, 192, 768), BF), pltpu.VMEM((192, 3072), BF), pltpu.VMEM((768, 768), BF),
            pltpu.VMEM((16, 768), BF), pltpu.VMEM((512, 768), BF), pltpu.VMEM((8, 512), jnp.int32),
            dma((n,)), dma((n,)), dma((n, 4)), dma((n, 4)), dma((n, 5)), dma((n, 5)), dma((5,)), dma((5,)),
            dma((9, 2)),
        ],
        compiler_params=pltpu.CompilerParams(collective_id=0, has_side_effects=True),
    )(wq, wk, wv, wo, wu, wd, small, x_in, seg_in)


NT = (((1,), (1,)), ((), ()))


def dot(a, b, dims=(((1,), (0,)), ((), ()))):
    return lax.dot_general(a, b, dims, preferred_element_type=F32)


def attn_fwd_kernel(q_ref, k_ref, v_ref, sq_ref, sk_ref, mix_ref, p_ref, bias):
    @pl.when(pl.program_id(0) == 0)
    def _():
        bias[...] = jnp.where(sq_ref[...] == sk_ref[...], 0.0, far_value)

    parts = []
    for i in range(2):
        cols = slice(64 * i, 64 * i + 64)
        s = dot(q_ref[:, cols], k_ref[:, cols], NT) + bias[...]
        m = jnp.max(s, axis=1, keepdims=True)
        e = jnp.exp(s - m)
        p = (e * (1.0 / jnp.sum(e, axis=1, keepdims=True))).astype(BF)
        p_ref[i] = p
        parts.append(dot(p, v_ref[:, cols]))
    mix_ref[...] = jnp.concatenate(parts, axis=1).astype(BF)


def attn_fwd(q, k, v, sq, sk):
    sd = jax.ShapeDtypeStruct
    rows, keys = q.shape[0], k.shape[0]
    blk = lambda r: pl.BlockSpec((r, 128), lambda h: (0, h))
    return pl.pallas_call(
        attn_fwd_kernel,
        name="attn_fwd",
        grid=(H // 2,),
        out_shape=[sd((rows, D), BF), sd((H, rows, keys), BF)],
        in_specs=[blk(rows), blk(keys), blk(keys), pl.BlockSpec((rows, 1), lambda h: (0, 0)), pl.BlockSpec((1, keys), lambda h: (0, 0))],
        out_specs=[blk(rows), pl.BlockSpec((2, rows, keys), lambda h: (h, 0, 0))],
        scratch_shapes=[pltpu.VMEM((rows, keys), F32)],
        compiler_params=pltpu.CompilerParams(vmem_limit_bytes=60 * 2**20),
    )(q, k, v, sq, sk)


NCH = 12


def add_into(dst, src, rows, step=32):
    def body(i, carry):
        r = pl.ds(pl.multiple_of(i * step, step), step)
        dst[r, :] = (dst[r, :].astype(F32) + src[r, :].astype(F32)).astype(BF)
        return carry

    lax.fori_loop(0, rows // step, body, 0)


def backward_kernel(
    gd, gffn_in, gmid_in, slope_in, hid_in, z_in, q_in, k_in, v_in, mix_in, p_in, x_in,
    wd, wu, wo, wq, wk, wv, vecs, vec0,
    o_wd, o_wu, o_wo, o_wv, o_wk, o_wq, vec_out, own_out, gx_out,
    kbuf, gbuf, cbuf, ybuf, xbuf, z0buf, z1buf, fin,
    wt, st, gf, hid, zf, gp, gh, tr, qb, kb, vb, mixb, dk, dv, pb, xb, xt, oth, vbuf, vval,
    ksem, csend, crecv, send, recv, vsend, vrecv, gsend, grecv, osem, lsem, wsem, psem,
):
    me = Place()
    x, y, c, zb, z, s = me.x, me.y, me.c, me.zb, me.z, me.s

    def load(i, src, dst):
        return pltpu.make_async_copy(src, dst, lsem.at[i])

    l_gf, l_gh, l_hid = load(0, gffn_in, gf), load(1, gmid_in, gh), load(2, hid_in, hid)
    l_z, l_q, l_k, l_v = load(3, z_in, zf), load(4, q_in, qb), load(5, k_in, kb), load(6, v_in, vb)
    l_mix, l_x = load(7, mix_in, mixb), load(8, x_in, xb)
    own_cp = load(9, gh, own_out)

    def wdcp(j):
        return pltpu.make_async_copy(wd.at[pl.ds(pl.multiple_of(768 * j, 768), 768), :], wt.at[j % 2], wsem.at[0, j])

    def wucp(j):
        return pltpu.make_async_copy(wu.at[:, pl.ds(pl.multiple_of(768 * j, 768), 768)], wt.at[2 + j % 2], wsem.at[1, j])

    def slcp(j):
        return pltpu.make_async_copy(slope_in.at[:, pl.ds(pl.multiple_of(768 * j, 768), 768)], st.at[j % 2], wsem.at[2, j])

    def pcp(h):
        return pltpu.make_async_copy(p_in.at[pl.ds(2 * h, 2)], pb.at[h % 2], psem.at[h])

    w_o = pltpu.make_async_copy(wo, wt.at[0], wsem.at[3, 0])
    w_k = pltpu.make_async_copy(wk, wt.at[2], wsem.at[3, 1])
    w_v = pltpu.make_async_copy(wv, wt.at[1], wsem.at[3, 2])
    w_q = pltpu.make_async_copy(wq, wt.at[3], wsem.at[3, 3])

    def source(k, sh):
        if isinstance(k, int) and k < 4:
            return gd.at[sh, pl.ds(192 * k, 192), :]
        return gbuf.at[k - 4, sh]

    def ccp(k, yy):
        return remote(source(k, 2 * yy + 1 - c), cbuf.at[k, yy], csend.at[k, yy], crecv.at[k, yy], me.core_p)

    def kcp(k, yy):
        return pltpu.make_async_copy(source(k, 2 * yy + c), kbuf.at[k, yy], ksem.at[k, yy])

    def core_start(k):
        for yy in range(2):
            ccp(k, yy).start()

    def bits(k):
        e = k % 2
        return e, x + e * (zb - x), zb + e * (x - zb)

    def rows(a, n):
        return pl.ds(pl.multiple_of(a * n, 16), n)

    def ycp(k):
        return remote(cbuf.at[k, 1 - y], ybuf.at[k], send.at[0, k], recv.at[0, k], me.y_p)

    def p1cp(k):
        e, b1, b2 = bits(k)
        p = (z + e * (1 - 2 * zb), s, x + (1 - e) * (1 - 2 * x))
        return remote(ybuf.at[k, rows(1 - b1, 96), :], xbuf.at[k], send.at[1, k], recv.at[1, k], p)

    def second(k):
        e = k % 2
        return (z + (1 - e) * (1 - 2 * zb), s, x + e * (1 - 2 * x))

    def p2cp(k):
        e, b1, b2 = bits(k)
        return remote(xbuf.at[k, rows(1 - b2, 48), :], z0buf.at[k], send.at[2, k], recv.at[2, k], second(k))

    def z1cp(k):
        return remote(z0buf.at[k], z1buf.at[k], send.at[3, k], recv.at[3, k], me.z1_p)

    def a2cp(k):
        e, b1, b2 = bits(k)
        r = fin.at[k, rows(2 * b1 + b2, 48), :]
        return remote(r, r, send.at[4, k], recv.at[4, k], second(k))

    def a1cp(k):
        e, b1, b2 = bits(k)
        r = fin.at[k, rows(b1, 96), :]
        p = (z + e * (1 - 2 * zb), s, x + (1 - e) * (1 - 2 * x))
        return remote(r, r, send.at[5, k], recv.at[5, k], p)

    def branch(cond, fn):
        if isinstance(cond, bool):
            if cond:
                fn()
        else:
            pl.when(cond)(fn)

    def out_copy(k, act):
        def wd_out():
            kk = jnp.minimum(k, 3)
            act(pltpu.make_async_copy(fin.at[k], o_wd.at[pl.ds(pl.multiple_of(192 * kk, 192), 192), :], osem.at[k]))

        def wu_out():
            kk = jnp.clip(k - 4, 0, 3)
            act(pltpu.make_async_copy(fin.at[k], o_wu.at[:, pl.ds(pl.multiple_of(768 * kk, 768), 768)], osem.at[k]))

        branch(k < 4, wd_out)
        both = (4 <= k < 8) if isinstance(k, int) else jnp.logical_and(k >= 4, k < 8)
        branch(both, wu_out)
        for i, o in enumerate((o_wo, o_wv, o_wk, o_wq)):
            branch(k == 8 + i, lambda o=o: act(pltpu.make_async_copy(fin.at[k], o, osem.at[k])))

    def pump(t):
        def at(d, fn):
            k = t - d
            if isinstance(k, int):
                if 0 <= k < NCH:
                    fn(k)
            else:
                pl.when(jnp.logical_and(k >= 0, k < NCH))(lambda: fn(jnp.clip(k, 0, NCH - 1)))

        def core(k):
            for yy in range(2):
                remote(cbuf.at[k, yy], cbuf.at[k, yy], csend.at[k, yy], crecv.at[k, yy], me.core_p).wait_recv()

            def first():
                kk = jnp.minimum(k, 3)
                for yy in range(2):
                    pltpu.make_async_copy(kbuf.at[kk, yy], kbuf.at[kk, yy], ksem.at[kk, yy]).wait()
                    add_into(cbuf.at[k, yy], kbuf.at[kk, yy], 192)

            def later():
                kk = jnp.maximum(k - 4, 0)
                for yy in range(2):
                    add_into(cbuf.at[k, yy], gbuf.at[kk, 2 * yy + c], 192)

            branch(k < 4, first)
            branch(k >= 4, later)

        def s_p1(k):
            e, b1, b2 = bits(k)
            p1cp(k).wait_recv()
            add_into(xbuf.at[k], ybuf.at[k, rows(b1, 96), :], 96)
            p2cp(k).start()

        def s_p2(k):
            e, b1, b2 = bits(k)
            p2cp(k).wait_recv()
            add_into(z0buf.at[k], xbuf.at[k, rows(b2, 48), :], 48, 16)
            z1cp(k).start()

        def s_z1(k):
            e, b1, b2 = bits(k)
            z1cp(k).wait_recv()
            fin[k, rows(2 * b1 + b2, 48), :] = (z0buf[k].astype(F32) + z1buf[k].astype(F32)).astype(BF)
            a2cp(k).start()

        def s_a2(k):
            a2cp(k).wait_recv()
            a1cp(k).start()

        def s_a1(k):
            a1cp(k).wait_recv()
            out_copy(k, lambda cp: cp.start())

        def s_y(k):
            ycp(k).wait_recv()
            add_into(ybuf.at[k], cbuf.at[k, y], 192)
            p1cp(k).start()

        at(0, core)
        at(2, s_y)
        at(3, s_p1)
        at(4, s_p2)
        at(5, s_z1)
        at(6, s_a2)
        at(7, s_a1)
        at(0, lambda k: ycp(k).start())

    l_gf.start()
    wdcp(0).start()
    slcp(0).start()
    for k in range(4):
        for yy in range(2):
            kcp(k, yy).start()
        if k == 0:
            l_hid.start()
            wucp(0).start()
            l_gh.start()
    wdcp(1).start()
    slcp(1).start()
    wucp(1).start()
    for cp in (l_z, l_mix, l_q, l_k, l_v, l_x):
        cp.start()
    pcp(0).start()
    pcp(1).start()
    greet([me.core_p, me.y_p, me.x_p, me.z0_p, me.z1_p])
    for k in range(4):
        core_start(k)
    vval[0] = vec0[...]
    pump(0)
    pump(1)

    def transposed(dst, src, n):
        for i in range(n // 256):
            dst[:, 256 * i : 256 * i + 256] = src[256 * i : 256 * i + 256, :].T

    def weight_grad(lhs, rhs, k):
        def body(n, carry):
            cs = pl.ds(pl.multiple_of(n * 256, 256), 256)
            r = dot(lhs[...], rhs[:, cs]).astype(BF)
            for sh in range(4):
                gbuf[k - 4, sh, :, cs] = r[192 * sh : 192 * sh + 192]
            return carry

        lax.fori_loop(0, 3, body, 0)
        core_start(k)

    def blocks(n, step, fn, init):
        return lax.fori_loop(0, n // step, lambda i, a: fn(pl.ds(pl.multiple_of(i * step, step), step), a), init)

    zero = jnp.zeros((1, D), F32)
    l_gf.wait()
    l_hid.wait()
    transposed(tr, hid, 512)
    l_gh.wait()

    def ffn(j, carry):
        wdcp(j).wait()
        slcp(j).wait()
        sl = j % 2

        def up(r, a):
            t = (dot(gf[r, :], wt[sl], NT) * st[sl, r, :].astype(F32)).astype(BF)
            gp[r, :] = t
            return a + jnp.sum(t.astype(F32), 0, keepdims=True)

        vval[0, pl.ds(8 + j, 1), :] = blocks(512, 256, up, zero)
        weight_grad(tr, gp, 4 + j)
        wucp(j).wait()

        def down(r, a):
            gh[r, :] = gh[r, :] + dot(gp[r, :], wt[2 + sl], NT)
            return a

        blocks(512, 256, down, 0)

        @pl.when(j < 2)
        def _():
            jj = jnp.minimum(j + 2, 3)
            wdcp(jj).start()
            slcp(jj).start()
            wucp(jj).start()

        @pl.when(j == 2)
        def _():
            w_o.start()
            w_k.start()

        @pl.when(j == 3)
        def _():
            w_v.start()
            w_q.start()

        pump(2 + j)
        return carry

    lax.fori_loop(0, 4, ffn, 0)

    l_z.wait()
    l_mix.wait()
    gain = vecs[3:4, :]

    def norm(r, a):
        zz = zf[r, :]
        m = jnp.mean(zz, -1, keepdims=True)
        zz = zz - m
        inv = lax.rsqrt(jnp.mean(zz * zz, -1, keepdims=True) + norm_eps)
        n = zz * inv
        e = gh[r, :]
        ge = e * gain
        g = (ge - jnp.mean(ge, -1, keepdims=True) - n * jnp.mean(ge * n, -1, keepdims=True)) * inv
        gh[r, :] = g
        low = g.astype(BF)
        gf[r, :] = low
        total = lambda v: jnp.sum(v, 0, keepdims=True)
        return a[0] + total(low.astype(F32)), a[1] + total(e * n), a[2] + total(e)

    sums = blocks(512, 64, norm, (zero, zero, zero))
    for i in range(3):
        vval[0, 2 + i : 3 + i, :] = sums[i]
    transposed(tr, mixb, 512)
    weight_grad(tr, gf, 8)
    w_o.wait()

    def mixg(r, a):
        hid[r, :] = dot(gf[r, :], wt[0], NT).astype(BF)
        return a

    blocks(512, 256, mixg, 0)
    l_q.wait()
    l_k.wait()
    l_v.wait()
    pump(6)

    def attn(h, carry):
        cs = pl.ds(pl.multiple_of(h * 128, 128), 128)
        pcp(h).wait()
        g = hid[:, cs]
        prod = g.astype(F32) * mixb[:, cs].astype(F32)
        gt = g.T
        qt = qb[:, cs].T
        kk = kb[:, cs]
        vv = vb[:, cs]
        dqs, dks, dvs = [], [], []
        for i in range(2):
            cols = slice(64 * i, 64 * i + 64)
            p = pb[h % 2, i]
            delta = jnp.sum(prod[:, cols], axis=1, keepdims=True)
            dp = dot(g[:, cols], vv[:, cols], NT)
            gs = (p.astype(F32) * (dp - delta)).astype(BF)
            dqs.append(dot(gs, kk[:, cols]) * 0.125)
            dks.append(dot(qt[cols, :], gs))
            dvs.append(dot(gt[cols, :], p))
        gp[:, cs] = jnp.concatenate(dqs, axis=1).astype(BF)
        dk[:, cs] = jnp.concatenate(dks, axis=0).T.astype(BF)
        dv[:, cs] = jnp.concatenate(dvs, axis=0).T.astype(BF)

        @pl.when(h < 4)
        def _():
            pcp(jnp.minimum(h + 2, 5)).start()

        return carry

    def attn_pair(i, carry):
        lax.fori_loop(2 * i, 2 * i + 2, attn, 0)
        pump(7 + i)
        return carry

    lax.fori_loop(0, 2, attn_pair, 0)
    lax.fori_loop(4, 6, attn, 0)
    l_x.wait()
    transposed(xt, xb, 1024)
    weight_grad(xt, dv, 9)
    weight_grad(xt, dk, 10)
    pump(9)
    weight_grad(xt.at[:, pl.ds(pl.multiple_of(x * 512, 512), 512)], gp, 11)
    w_k.wait()
    w_v.wait()
    w_q.wait()

    def gxcp(i):
        r = pl.ds(256 * i, 256)
        return remote(oth.at[r, :], gx_out.at[r, :], gsend.at[i], grecv.at[i], me.x_p)

    for i in range(2):
        r = pl.ds(pl.multiple_of((1 - x) * 512 + 256 * i, 256), 256)
        oth[256 * i : 256 * i + 256, :] = (dot(dk[r, :], wt[2], NT) + dot(dv[r, :], wt[1], NT)).astype(BF)
    gxcp(0).start()

    def colsum(r, a):
        return a + jnp.sum(dv[r, :].astype(F32), 0, keepdims=True)

    def colsum_q(r, a):
        return a + jnp.sum(gp[r, :].astype(F32), 0, keepdims=True)

    vval[0, 0:1, :] = blocks(512, 128, colsum_q, zero)
    vval[0, 1:2, :] = blocks(1024, 128, colsum, zero)
    vps = (me.core_p, me.y_p, me.x_p, me.z0_p, me.z1_p)
    vcps = [remote(vval.at[b], vbuf.at[b], vsend.at[b], vrecv.at[b], vps[b]) for b in range(5)]
    vcps[0].start()
    pump(10)
    gxcp(1).start()

    def own(i, carry):
        r = pl.ds(pl.multiple_of(256 * i, 256), 256)
        ro = pl.ds(pl.multiple_of(x * 512 + 256 * i, 256), 256)
        gh[r, :] = gh[r, :] + dot(gp[r, :], wt[3], NT) + dot(dk[ro, :], wt[2], NT) + dot(dv[ro, :], wt[1], NT)
        return carry

    lax.fori_loop(0, 2, own, 0)
    own_cp.start()
    for t in range(11, NCH + 7):
        pump(t)
        b = t - 11
        if b < 5:
            vcps[b].wait_recv()
            if b < 4:
                vval[b + 1] = vval[b] + vbuf[b]
                vcps[b + 1].start()
            else:
                vec_out[...] = vval[b] + vbuf[b]

    def finish(k, carry):
        for f in (ycp, p1cp, p2cp, z1cp, a2cp, a1cp):
            f(k).wait_send()
        for yy in range(2):
            remote(cbuf.at[k, yy], cbuf.at[k, yy], csend.at[k, yy], crecv.at[k, yy], me.core_p).wait_send()
        out_copy(k, lambda cp: cp.wait())
        return carry

    lax.fori_loop(0, NCH, finish, 0)
    for cp in vcps:
        cp.wait_send()
    own_cp.wait()
    for i in range(2):
        gxcp(i).wait()


def backward_all(*args):
    sd = jax.ShapeDtypeStruct
    dma = pltpu.SemaphoreType.DMA
    vm = pltpu.VMEM
    vspec = pl.BlockSpec(memory_space=pltpu.VMEM)
    one = lambda: sd((192, 768), BF)
    half = lambda: vm((512, 768), BF)
    full = lambda: vm((1024, 768), BF)
    return pl.pallas_call(
        backward_kernel,
        name="backward",
        out_shape=[
            sd((768, 768), BF), sd((192, 3072), BF), one(), one(), one(), one(),
            sd((16, 768), F32), sd((512, 768), F32), sd((512, 768), BF),
        ],
        in_specs=[ANY] * 18 + [vspec] * 2,
        out_specs=[ANY] * 6 + [vspec, ANY, ANY],
        scratch_shapes=[
            vm((4, 2, 192, 768), BF), vm((8, 4, 192, 768), BF), vm((NCH, 2, 192, 768), BF), vm((NCH, 192, 768), BF),
            vm((NCH, 96, 768), BF), vm((NCH, 48, 768), BF), vm((NCH, 48, 768), BF), vm((NCH, 192, 768), BF),
            vm((4, 768, 768), BF), vm((2, 512, 768), BF), half(), half(), vm((512, 768), F32), half(), vm((512, 768), F32),
            vm((768, 512), BF), half(), full(), full(), half(), full(), full(), vm((2, 2, 512, 1024), BF),
            full(), vm((768, 1024), BF), half(), vm((5, 16, 768), F32), vm((5, 16, 768), F32),
            dma((4, 2)), dma((NCH, 2)), dma((NCH, 2)), dma((6, NCH)), dma((6, NCH)), dma((5,)), dma((5,)), dma((2,)), dma((2,)),
            dma((NCH,)), dma((10,)), dma((4, 4)), dma((6,)),
        ],
        compiler_params=pltpu.CompilerParams(collective_id=1, has_side_effects=True, vmem_limit_bytes=63 * 2**20),
    )(*args)


def layer_norm(total_rows, gain_vec, shift_vec):
    row_mean = jnp.mean(total_rows, -1, keepdims=True)
    centred = total_rows - row_mean
    variance = jnp.mean(centred * centred, -1, keepdims=True)
    inv_std = lax.rsqrt(variance + norm_eps)
    normed = centred * inv_std
    return (normed * gain_vec + shift_vec, normed, inv_std)


def norm_grad(grad_in, normed, inv_std, gain_vec):
    scaled = grad_in * gain_vec
    centred_grad = (
        scaled
        - jnp.mean(scaled, -1, keepdims=True)
        - normed * jnp.mean(scaled * normed, -1, keepdims=True)
    )
    return (centred_grad * inv_std, jnp.sum(grad_in * normed, 0), jnp.sum(grad_in, 0))


TN = (((0,), (0,)), ((), ()))


def shards(
    inputs, segments, cotangent, w_query, b_query, w_key, w_value, b_value, w_out, b_out,
    gain_one, shift_one, w_up, b_up, w_down, b_down, gain_two, shift_two,
):
    x_own = inputs[0]
    rows = x_own.shape[0]
    singles = (b_query, b_value, b_out, gain_one, shift_one, b_down, gain_two, shift_two, b_up)
    small = sum(jnp.pad(a, (D * i, 16 * D - D * i - a.shape[0])) for i, a in enumerate(singles)).reshape(16, D)
    seg8 = jnp.broadcast_to(segments, (8, rows))
    wq, wk, wv, wo, wu, wd, sm, xf, segf = gather_all(
        w_query, w_key, w_value, w_out, w_up, w_down, small, x_own, seg8
    )
    wq, wk, wv, wo, wu, wd = (w.reshape(-1, w.shape[-1]) for w in (wq, wk, wv, wo, wu, wd))
    vecs = sm[:, :8, :192].transpose(1, 0, 2).reshape(8, 768).astype(F32)
    bq, bv, bo, g1, s1, bd, g2, s2 = (vecs[i] for i in range(8))
    bu = sm[:, 8].reshape(FF).astype(F32)
    x_all = xf.reshape(-1, D)
    seg_all = segf[:, 0].reshape(1, -1)

    q8 = ((dot(x_own, wq) + bq).astype(BF).astype(F32) * 0.125).astype(BF)
    keys = dot(x_all, wk).astype(BF)
    values = (dot(x_all, wv) + bv).astype(BF)
    mixture, probs = attn_fwd(q8, keys, values, segments.reshape(-1, 1), seg_all)
    attn_out = dot(mixture, wo) + bo
    z_one = x_own.astype(F32) + attn_out
    norm_one, _, _ = layer_norm(z_one, g1, s1)
    hidden_low = norm_one.astype(BF)
    pre_act = dot(hidden_low, wu) + bu
    phi = 0.5 * (1.0 + lax.erf(pre_act * (2.0**-0.5)))
    act_low = (pre_act * phi).astype(BF)
    slope = (phi + pre_act * jnp.exp(-0.5 * pre_act * pre_act) * (2 * math.pi) ** -0.5).astype(BF)
    ffn_out = dot(act_low, wd) + bd
    result, normed_two, inv_two = layer_norm(norm_one + ffn_out, g2, s2)

    grad_mid, d_g2, d_s2 = norm_grad(cotangent[0].astype(F32), normed_two, inv_two, g2)
    grad_ffn = grad_mid.astype(BF)
    d_bd = jnp.sum(grad_ffn.astype(F32), 0)
    d_wd = dot(act_low, grad_ffn, TN).astype(BF)
    vec0 = jnp.zeros((16, D), F32)
    for i, a in ((5, d_bd), (6, d_g2), (7, d_s2)):
        vec0 = vec0 + jnp.pad(a.reshape(1, D), ((i, 15 - i), (0, 0)))
    o_wd, o_wu, o_wo, o_wv, o_wk, o_wq, vec, own_part, gx = backward_all(
        d_wd.reshape(4, -1, D), grad_ffn, grad_mid, slope, hidden_low, z_one, q8, keys, values, mixture, probs, x_all,
        wd, wu, wo, wq, wk, wv, vecs, vec0,
    )
    o_wd, o_wu, o_wo, o_wv, o_wk, o_wq = (a.astype(F32) for a in (o_wd, o_wu, o_wo, o_wv, o_wk, o_wq))
    sh = lax.axis_index("shard")
    mine = lax.dynamic_slice(vec[:8], (0, sh * 192), (8, 192))
    o_bq, o_bv, o_bo, o_g1, o_s1, o_bd, o_g2, o_s2 = (mine[i] for i in range(8))
    o_bu = lax.dynamic_index_in_dim(vec[8:12], sh, 0, False)
    grad_input = own_part + gx.astype(F32)
    return (
        result.astype(BF)[None], grad_input[None], o_wq, o_bq, o_wk, o_wv, o_bv, o_wo, o_bo,
        o_g1, o_s1, o_wu, o_bu, o_wd, o_bd, o_g2, o_s2,
    )


def make(mesh, body):
    in_specs = (
        P(("rep", "shard"), "seq", None), P(("rep", "shard"), "seq"), P(("rep", "shard"), "seq", None),
        P("shard", None), P("shard"), P("shard", None), P("shard", None), P("shard"), P("shard", None), P("shard"),
        P("shard"), P("shard"), P("shard", None), P("shard"), P("shard", None), P("shard"), P("shard"), P("shard"),
    )
    out_specs = (
        P(("rep", "shard"), "seq", None), P(("rep", "shard"), "seq", None),
        P("shard", None), P("shard"), P("shard", None), P("shard", None), P("shard"), P("shard", None), P("shard"),
        P("shard"), P("shard"), P("shard", None), P("shard"), P("shard", None), P("shard"), P("shard"), P("shard"),
    )
    return jax.shard_map(body, mesh=mesh, in_specs=in_specs, out_specs=out_specs, check_vma=False)


param_names = (
    "w_query",
    "b_query",
    "w_key",
    "w_value",
    "b_value",
    "w_out",
    "b_out",
    "gain_one",
    "shift_one",
    "w_up",
    "b_up",
    "w_down",
    "b_down",
    "gain_two",
    "shift_two",
)


def as_sent(x):
    return jax.tree.map(lambda a: a.astype(jnp.bfloat16) if a.dtype == jnp.float32 else a, x)


def general_layer_norm(total_rows, gain_vec, shift_vec):
    row_mean = jnp.mean(total_rows, -1, keepdims=True)
    centred = total_rows - row_mean
    variance = jnp.mean(centred * centred, -1, keepdims=True)
    inv_std = lax.rsqrt(variance + norm_eps)
    normed = centred * inv_std
    return (normed * gain_vec + shift_vec, normed, inv_std)


def general_norm_grad(grad_in, normed, inv_std, gain_vec):
    scaled = grad_in * gain_vec
    centred_grad = (
        scaled
        - jnp.mean(scaled, -1, keepdims=True)
        - normed * jnp.mean(scaled * normed, -1, keepdims=True)
    )
    return (centred_grad * inv_std, jnp.sum(grad_in * normed, 0), jnp.sum(grad_in, 0))


def inner_rows(left, right):
    return lax.dot_general(
        left, right, (((0,), (0,)), ((), ())), preferred_element_type=jnp.float32
    )


def times_transposed(left, matrix):
    return lax.dot_general(
        left, matrix, (((1,), (1,)), ((), ())), preferred_element_type=jnp.float32
    )


def gelu_exact(value):
    return jax.nn.gelu(value, approximate=False)


def general_shards(
    inputs,
    segments,
    cotangent,
    w_query,
    b_query,
    w_key,
    w_value,
    b_value,
    w_out,
    b_out,
    gain_one,
    shift_one,
    w_up,
    b_up,
    w_down,
    b_down,
    gain_two,
    shift_two,
):
    score_scale = DH ** (-0.5)
    token_rows = inputs[0]
    row_count = token_rows.shape[0]
    own_seg = segments[0].astype(jnp.float32)
    local_params = (
        w_query,
        b_query,
        w_key,
        w_value,
        b_value,
        w_out,
        b_out,
        gain_one,
        shift_one,
        w_up,
        b_up,
        w_down,
        b_down,
        gain_two,
        shift_two,
    )
    gathered = (
        lax.all_gather(local_params[0], "shard", axis=0, tiled=True),
        lax.all_gather(local_params[1], "shard", axis=0, tiled=True),
        lax.all_gather(local_params[2], "shard", axis=0, tiled=True),
        lax.all_gather(local_params[3], "shard", axis=0, tiled=True),
        lax.all_gather(local_params[4], "shard", axis=0, tiled=True),
        lax.all_gather(local_params[5], "shard", axis=0, tiled=True),
        lax.all_gather(local_params[6], "shard", axis=0, tiled=True),
        lax.all_gather(local_params[7], "shard", axis=0, tiled=True),
        lax.all_gather(local_params[8], "shard", axis=0, tiled=True),
        lax.all_gather(local_params[9], "shard", axis=0, tiled=True),
        lax.all_gather(local_params[10], "shard", axis=0, tiled=True),
        lax.all_gather(local_params[11], "shard", axis=0, tiled=True),
        lax.all_gather(local_params[12], "shard", axis=0, tiled=True),
        lax.all_gather(local_params[13], "shard", axis=0, tiled=True),
        lax.all_gather(local_params[14], "shard", axis=0, tiled=True),
    )
    weights = dict(zip(param_names, gathered))

    def vector(name):
        return weights[name].astype(jnp.float32)

    q_wide = jnp.dot(token_rows, weights["w_query"], preferred_element_type=jnp.float32) + vector(
        "b_query"
    )
    queries = q_wide.astype(jnp.bfloat16)
    key_rows = jnp.dot(token_rows, weights["w_key"], preferred_element_type=jnp.float32).astype(
        jnp.bfloat16
    )
    value_rows = (
        jnp.dot(token_rows, weights["w_value"], preferred_element_type=jnp.float32)
        + vector("b_value")
    ).astype(jnp.bfloat16)
    seg_wire = segments[0].astype(jnp.bfloat16)
    query_heads = queries.reshape(row_count, H, DH)
    start_state = (
        jnp.full((H, row_count), far_value, jnp.float32),
        jnp.zeros((H, row_count), jnp.float32),
        jnp.zeros((row_count, H, DH), jnp.float32),
    )
    carried = start_state
    piece_keys = lax.all_gather(key_rows, "seq", axis=0, tiled=True)
    piece_values = lax.all_gather(value_rows, "seq", axis=0, tiled=True)
    piece_seg = lax.all_gather(seg_wire, "seq", axis=0, tiled=True)
    piece_rows = piece_keys.shape[0]
    width_blk = math.gcd(piece_rows, 512)
    blocks = piece_rows // width_blk
    key_blocks = piece_keys.reshape(blocks, width_blk, H, DH)
    value_blocks = piece_values.reshape(blocks, width_blk, H, DH)
    seg_blocks = piece_seg.astype(jnp.float32).reshape(blocks, width_blk)

    def update(fold_state, block_item):
        key_blk, value_blk, seg_blk = block_item
        row_peak, row_total, accumulated = fold_state
        scores = (
            jnp.einsum("rhd,khd->hrk", query_heads, key_blk, preferred_element_type=jnp.float32)
            * score_scale
        )
        allowed = own_seg[:, None] == seg_blk[None, :]
        scores = jnp.where(allowed[None], scores, far_value)
        new_peak = jnp.maximum(row_peak, jnp.max(scores, -1))
        factor = jnp.exp(row_peak - new_peak)
        exp_scores = jnp.exp(scores - new_peak[:, :, None])
        row_total = row_total * factor + jnp.sum(exp_scores, -1)
        block_mix = jnp.einsum(
            "hrk,khd->rhd",
            exp_scores.astype(jnp.bfloat16),
            value_blk,
            preferred_element_type=jnp.float32,
        )
        accumulated = accumulated * jnp.transpose(factor)[:, :, None] + block_mix
        return ((new_peak, row_total, accumulated), None)

    carried, unused = lax.scan(update, carried, (key_blocks, value_blocks, seg_blocks))
    row_peak, row_total, accumulated = carried
    mix_wide = (accumulated / jnp.transpose(row_total)[:, :, None]).reshape(row_count, D)
    mixture = mix_wide.astype(jnp.bfloat16)
    log_total = row_peak + jnp.log(row_total)
    attn_out = jnp.dot(mixture, weights["w_out"], preferred_element_type=jnp.float32) + vector(
        "b_out"
    )
    norm_one, normed_one, inv_one = general_layer_norm(
        token_rows.astype(jnp.float32) + attn_out, vector("gain_one"), vector("shift_one")
    )
    hidden_low = norm_one.astype(jnp.bfloat16)
    pre_act = jnp.dot(hidden_low, weights["w_up"], preferred_element_type=jnp.float32) + vector(
        "b_up"
    )
    activated, gelu_pullback = jax.vjp(gelu_exact, pre_act)
    act_low = activated.astype(jnp.bfloat16)
    ffn_out = jnp.dot(act_low, weights["w_down"], preferred_element_type=jnp.float32) + vector(
        "b_down"
    )
    result, normed_two, inv_two = general_layer_norm(
        norm_one + ffn_out, vector("gain_two"), vector("shift_two")
    )
    regathered = (
        lax.all_gather(local_params[0], "shard", axis=0, tiled=True),
        lax.all_gather(local_params[1], "shard", axis=0, tiled=True),
        lax.all_gather(local_params[2], "shard", axis=0, tiled=True),
        lax.all_gather(local_params[3], "shard", axis=0, tiled=True),
        lax.all_gather(local_params[4], "shard", axis=0, tiled=True),
        lax.all_gather(local_params[5], "shard", axis=0, tiled=True),
        lax.all_gather(local_params[6], "shard", axis=0, tiled=True),
        lax.all_gather(local_params[7], "shard", axis=0, tiled=True),
        lax.all_gather(local_params[8], "shard", axis=0, tiled=True),
        lax.all_gather(local_params[9], "shard", axis=0, tiled=True),
        lax.all_gather(local_params[10], "shard", axis=0, tiled=True),
        lax.all_gather(local_params[11], "shard", axis=0, tiled=True),
        lax.all_gather(local_params[12], "shard", axis=0, tiled=True),
        lax.all_gather(local_params[13], "shard", axis=0, tiled=True),
        lax.all_gather(local_params[14], "shard", axis=0, tiled=True),
    )
    backward_set = dict(zip(param_names, regathered))
    grad_out = cotangent[0].astype(jnp.float32)
    grad_mid, grad_gain_two, grad_shift_two = general_norm_grad(
        grad_out, normed_two, inv_two, backward_set["gain_two"].astype(jnp.float32)
    )
    grad_ffn = grad_mid.astype(jnp.bfloat16)
    grad_b_down = jnp.sum(grad_ffn.astype(jnp.float32), 0)
    grad_w_down = inner_rows(act_low, grad_ffn)
    grad_act = times_transposed(grad_ffn, backward_set["w_down"])
    (grad_pre_wide,) = gelu_pullback(grad_act)
    grad_pre = grad_pre_wide.astype(jnp.bfloat16)
    grad_b_up = jnp.sum(grad_pre.astype(jnp.float32), 0)
    grad_w_up = inner_rows(hidden_low, grad_pre)
    grad_hidden = grad_mid + times_transposed(grad_pre, backward_set["w_up"])
    grad_sum_one, grad_gain_one, grad_shift_one = general_norm_grad(
        grad_hidden, normed_one, inv_one, backward_set["gain_one"].astype(jnp.float32)
    )
    grad_attn = grad_sum_one.astype(jnp.bfloat16)
    grad_b_out = jnp.sum(grad_attn.astype(jnp.float32), 0)
    grad_w_out = inner_rows(mixture, grad_attn)
    grad_mixture = times_transposed(grad_attn, backward_set["w_out"]).astype(jnp.bfloat16)
    grad_mix_heads = grad_mixture.reshape(row_count, H, DH)
    row_delta = jnp.transpose(
        jnp.sum((grad_mixture.astype(jnp.float32) * mix_wide).reshape(row_count, H, DH), -1)
    )
    all_keys, all_values, all_seg = (
        lax.all_gather(key_rows, "seq", axis=0, tiled=True),
        lax.all_gather(value_rows, "seq", axis=0, tiled=True),
        lax.all_gather(seg_wire, "seq", axis=0, tiled=True),
    )
    seq_rows = all_keys.shape[0]
    width_all = math.gcd(seq_rows, 512)
    blocks_all = seq_rows // width_all
    key_blocks = all_keys.reshape(blocks_all, width_all, H, DH)
    value_blocks = all_values.reshape(blocks_all, width_all, H, DH)
    seg_blocks = all_seg.astype(jnp.float32).reshape(blocks_all, width_all)

    def block_grads(key_blk, value_blk, seg_blk):
        scores = (
            jnp.einsum("rhd,khd->hrk", query_heads, key_blk, preferred_element_type=jnp.float32)
            * score_scale
        )
        allowed = own_seg[:, None] == seg_blk[None, :]
        scores = jnp.where(allowed[None], scores, far_value)
        probabilities = jnp.exp(scores - log_total[:, :, None])
        grad_probs = jnp.einsum(
            "rhd,khd->hrk", grad_mix_heads, value_blk, preferred_element_type=jnp.float32
        )
        grad_scores = (probabilities * (grad_probs - row_delta[:, :, None])).astype(jnp.bfloat16)
        return (probabilities, grad_scores)

    def back_update(grad_query_acc, block_item):
        key_blk, value_blk, seg_blk = block_item
        back_grad_query_acc = grad_query_acc
        probabilities, grad_scores = block_grads(key_blk, value_blk, seg_blk)
        grad_value_blk = jnp.einsum(
            "hrk,rhd->khd",
            probabilities.astype(jnp.bfloat16),
            grad_mix_heads,
            preferred_element_type=jnp.float32,
        )
        back_grad_query_acc = (
            back_grad_query_acc
            + jnp.einsum("hrk,khd->rhd", grad_scores, key_blk, preferred_element_type=jnp.float32)
            * score_scale
        )
        grad_key_blk = (
            jnp.einsum("hrk,rhd->khd", grad_scores, query_heads, preferred_element_type=jnp.float32)
            * score_scale
        )
        return (back_grad_query_acc, (grad_key_blk, grad_value_blk))

    grad_query_heads, key_value_grads = lax.scan(
        back_update,
        jnp.zeros((row_count, H, DH), jnp.float32),
        (key_blocks, value_blocks, seg_blocks),
    )
    grad_key_all = key_value_grads[0].reshape(seq_rows, D)
    grad_value_all = key_value_grads[1].reshape(seq_rows, D)
    grad_key_rows, grad_value_rows = (
        lax.psum_scatter(
            grad_key_all.astype(jnp.bfloat16), "seq", scatter_dimension=0, tiled=True
        ).astype(jnp.float32),
        lax.psum_scatter(
            grad_value_all.astype(jnp.bfloat16), "seq", scatter_dimension=0, tiled=True
        ).astype(jnp.float32),
    )
    grad_query_low = grad_query_heads.reshape(row_count, D).astype(jnp.bfloat16)
    grad_key_low = grad_key_rows.astype(jnp.bfloat16)
    grad_value_low = grad_value_rows.astype(jnp.bfloat16)
    grad_w_query = inner_rows(token_rows, grad_query_low)
    grad_b_query = jnp.sum(grad_query_low.astype(jnp.float32), 0)
    grad_w_key = inner_rows(token_rows, grad_key_low)
    grad_w_value = inner_rows(token_rows, grad_value_low)
    grad_b_value = jnp.sum(grad_value_low.astype(jnp.float32), 0)
    grad_input = (
        grad_sum_one
        + times_transposed(grad_query_low, backward_set["w_query"])
        + times_transposed(grad_key_low, backward_set["w_key"])
        + times_transposed(grad_value_low, backward_set["w_value"])
    )
    gradients = (
        grad_w_query,
        grad_b_query,
        grad_w_key,
        grad_w_value,
        grad_b_value,
        grad_w_out,
        grad_b_out,
        grad_gain_one,
        grad_shift_one,
        grad_w_up,
        grad_b_up,
        grad_w_down,
        grad_b_down,
        grad_gain_two,
        grad_shift_two,
    )
    owned_grads = (
        lax.psum_scatter(
            gradients[0].astype(jnp.bfloat16), "shard", scatter_dimension=0, tiled=True
        ).astype(jnp.float32),
        lax.psum_scatter(
            gradients[1].astype(jnp.bfloat16), "shard", scatter_dimension=0, tiled=True
        ).astype(jnp.float32),
        lax.psum_scatter(
            gradients[2].astype(jnp.bfloat16), "shard", scatter_dimension=0, tiled=True
        ).astype(jnp.float32),
        lax.psum_scatter(
            gradients[3].astype(jnp.bfloat16), "shard", scatter_dimension=0, tiled=True
        ).astype(jnp.float32),
        lax.psum_scatter(
            gradients[4].astype(jnp.bfloat16), "shard", scatter_dimension=0, tiled=True
        ).astype(jnp.float32),
        lax.psum_scatter(
            gradients[5].astype(jnp.bfloat16), "shard", scatter_dimension=0, tiled=True
        ).astype(jnp.float32),
        lax.psum_scatter(
            gradients[6].astype(jnp.bfloat16), "shard", scatter_dimension=0, tiled=True
        ).astype(jnp.float32),
        lax.psum_scatter(
            gradients[7].astype(jnp.bfloat16), "shard", scatter_dimension=0, tiled=True
        ).astype(jnp.float32),
        lax.psum_scatter(
            gradients[8].astype(jnp.bfloat16), "shard", scatter_dimension=0, tiled=True
        ).astype(jnp.float32),
        lax.psum_scatter(
            gradients[9].astype(jnp.bfloat16), "shard", scatter_dimension=0, tiled=True
        ).astype(jnp.float32),
        lax.psum_scatter(
            gradients[10].astype(jnp.bfloat16), "shard", scatter_dimension=0, tiled=True
        ).astype(jnp.float32),
        lax.psum_scatter(
            gradients[11].astype(jnp.bfloat16), "shard", scatter_dimension=0, tiled=True
        ).astype(jnp.float32),
        lax.psum_scatter(
            gradients[12].astype(jnp.bfloat16), "shard", scatter_dimension=0, tiled=True
        ).astype(jnp.float32),
        lax.psum_scatter(
            gradients[13].astype(jnp.bfloat16), "shard", scatter_dimension=0, tiled=True
        ).astype(jnp.float32),
        lax.psum_scatter(
            gradients[14].astype(jnp.bfloat16), "shard", scatter_dimension=0, tiled=True
        ).astype(jnp.float32),
    )
    owned_grads = jax.tree.map(
        lambda part: part.astype(jnp.float32), lax.psum(as_sent(tuple(owned_grads)), ("rep", "seq"))
    )
    return (result.astype(jnp.bfloat16)[None], grad_input[None]) + tuple(owned_grads)


def solution(mesh):
    if dict(mesh.shape) == {"rep": 4, "shard": 4, "seq": 2}:
        return make(mesh, shards)
    return make(mesh, general_shards)
```

```python
import functools
import math

import jax
import jax.numpy as jnp
from jax import lax
from jax.experimental import pallas as pl
from jax.experimental.pallas import tpu as pltpu
from jax.sharding import PartitionSpec as P

D = 768
H = 12
DH = 64
FF = 3072
MESH = pl.DeviceIdType.MESH
F32 = jnp.float32
BF = jnp.bfloat16
ANY = pl.BlockSpec(memory_space=pl.ANY)

norm_eps = 1e-05
far_value = -1e30


class Place:
    def __init__(self):
        self.z = lax.axis_index("rep")
        self.s = lax.axis_index("shard")
        self.x = lax.axis_index("seq")
        self.y = self.s // 2
        self.c = self.s % 2
        self.zb = self.z % 2
        self.zh = self.z // 2
        zb, zh, x, y, c = self.zb, self.zh, self.x, self.y, self.c
        self.core_p = (self.z, 2 * y + 1 - c, x)
        self.y_p = (self.z, 2 * (1 - y) + c, x)
        self.diag_p = (self.z, 2 * (1 - y) + 1 - c, x)
        self.x_p = (self.z, self.s, 1 - x)
        self.z0_p = (2 * zh + 1 - zb, self.s, x)
        self.z1_p = (2 * (1 - zh) + zb, self.s, x)


def greet(partners):
    barrier = pltpu.get_barrier_semaphore()
    for p in partners:
        pl.semaphore_signal(barrier, inc=1, device_id=p, device_id_type=MESH)
    pl.semaphore_wait(barrier, len(partners))


def remote(src, dst, ssem, rsem, dev):
    return pltpu.make_async_remote_copy(
        src_ref=src, dst_ref=dst, send_sem=ssem, recv_sem=rsem, device_id=dev, device_id_type=MESH
    )


NT = (((1,), (1,)), ((), ()))
TN = (((0,), (0,)), ((), ()))


def dot(a, b, dims=(((1,), (0,)), ((), ()))):
    return lax.dot_general(a, b, dims, preferred_element_type=F32)


def forward_kernel(
    wq, wk, wv, wo, wu, wd, small, x_in, seg_in,
    gq, gk, gv, go, gu, gd, vecs, x_out, q_out, k_out, v_out, mix_out, p_out,
    b768, bu, bd, sb, xb, segb, wb, qb, kb, vb, mixb, pb, bias,
    ysend, yrecv, fsend, frecv, csend, crecv, ssend, srecv, lsem, wsem, osem, psem,
):
    me = Place()
    s, x, zb = me.s, me.x, me.zb
    so = 2 * (1 - me.y) + me.c

    chunks = [(own, full, 0, 192, 0, 768, False) for own, full in ((wq, gq), (wk, gk), (wv, gv))]
    chunks.append((wo, go, 0, 192, 0, 768, True))
    for j in range(2):
        chunks.append((wu, gu, 0, 192, 1536 * j, 1536, True))
    for j in range(4):
        chunks.append((wd, gd, 192 * j, 192, 0, 768, False))
    n = len(chunks)

    greet([me.core_p, me.y_p, me.diag_p, me.x_p, me.z0_p])

    ycp, relays, seconds, lasts, ccp = [], [], [], [], []
    for k, (own, full, r0, rows, c0, cols, quad) in enumerate(chunks):
        cs = pl.ds(c0, cols)
        whole = pl.ds(r0, rows)

        def part(i, h):
            return pl.ds(pl.multiple_of(r0 + i * h, 16), h)

        def relay(i, r, c, dev):
            return remote(full.at[so, r, c], full.at[so, r, c], fsend.at[k, i], frecv.at[k, i], dev)

        def across(i, r):
            return remote(full.at[so, r, cs], full.at[so, r, cs], csend.at[k, i], crecv.at[k, i], me.core_p)

        cc = [remote(own.at[whole, cs], full.at[s, whole, cs], csend.at[k, 0], crecv.at[k, 0], me.core_p)]
        if quad:
            h = rows // 4
            rm, rx = part(2 * x + zb, h), part(2 * (1 - x) + zb, h)
            rz, rd = part(2 * x + 1 - zb, h), part(2 * (1 - x) + 1 - zb, h)
            h0, h1 = pl.ds(c0, cols // 2), pl.ds(c0 + cols // 2, cols // 2)
            relays.append([relay(0, rm, cs, me.x_p), relay(1, rm, cs, me.z0_p)])
            seconds.append([relay(3, rx, h1, me.z0_p), relay(2, rz, h0, me.x_p)])
            cc += [across(1 + i, r) for i, r in enumerate((rm, rx, rz, rd))]
        else:
            h = rows // 2
            rm, rz = part(zb, h), part(1 - zb, h)
            relays.append([relay(1, rm, cs, me.z0_p)])
            seconds.append([])
            cc += [across(1 + i, r) for i, r in enumerate((rm, rz))]
        ycp.append(remote(own.at[rm, cs], full.at[s, rm, cs], ysend.at[k], yrecv.at[k], me.y_p))
        ccp.append(cc)

    def pump(t):
        if t < n:
            ycp[t].wait_recv()
            for cp in relays[t]:
                cp.start()
            ccp[t][1].start()
        k = t - 1
        if 0 <= k < n:
            for i, cp in enumerate(relays[k]):
                cp.wait_recv()
                ccp[k][2 + i].start()
                if seconds[k]:
                    seconds[k][i].start()
        k = t - 2
        if 0 <= k < n and seconds[k]:
            for cp in seconds[k]:
                cp.wait_recv()
            ccp[k][4].start()
        if t + 2 < n:
            ycp[t + 2].start()

    cps = [
        remote(x_in, xb.at[x], ssend.at[0], srecv.at[0], me.x_p),
        remote(seg_in, segb.at[x], ssend.at[1], srecv.at[1], me.x_p),
        remote(small, sb.at[s], ssend.at[2], srecv.at[2], me.core_p),
        remote(small, sb.at[s], ssend.at[3], srecv.at[3], me.y_p),
        remote(small, sb.at[s], ssend.at[4], srecv.at[4], me.diag_p),
    ]
    ycp[0].start()
    cps[0].start()
    ycp[1].start()
    for cp in cps[1:]:
        cp.start()
    for k in range(3):
        ccp[k][0].start()
    owns = [(wq, b768.at[0], gq), (wk, b768.at[1], gk), (wv, b768.at[2], gv), (wo, b768.at[3], go), (wu, bu, gu), (wd, bd, gd)]
    ins = [pltpu.make_async_copy(a, b, lsem.at[i, 0]) for i, (a, b, _) in enumerate(owns)]
    outs = [pltpu.make_async_copy(b, f.at[s], lsem.at[i, 1]) for i, (_, b, f) in enumerate(owns)]
    more = [(x_in, xb.at[x]), (seg_in, segb.at[x]), (small, sb.at[s])]
    more = [pltpu.make_async_copy(a, b, lsem.at[6 + i, 0]) for i, (a, b) in enumerate(more)]
    for cp in more + ins:
        cp.start()
    for a, b in zip(ins, outs):
        a.wait()
        b.start()
    for k in range(3, n):
        ccp[k][0].start()
    for cp in more:
        cp.wait()

    def weight(i):
        for cp in ccp[i]:
            cp.wait_recv()
        outs[i].wait()
        cp = pltpu.make_async_copy((gq, gk, gv)[i], wb.at[i], wsem.at[i])
        cp.start()
        cp.wait()

    def whole_weight(i):
        return wb[i].reshape(768, 768)

    pump(0)
    pump(1)
    pump(2)
    for cp in cps[2:]:
        cp.wait_recv()
    row = lax.broadcasted_iota(jnp.int32, (192, 768), 0)
    col = lax.broadcasted_iota(jnp.int32, (192, 768), 1)
    total = jnp.zeros((16, 768), F32)
    for i in range(4):
        pick = jnp.where(col == row + 192 * i, 1.0, 0.0).astype(BF)
        total = total + dot(sb[i, :, 0:192], pick)
    vecs[...] = total
    for i in range(4):
        vecs[8 + i : 9 + i, :] = sb[i].astype(F32)[8:9, :]

    def project(i, half, fn):
        w = whole_weight(i)
        for r in range(2):
            fn(256 * r, dot(xb[half, 256 * r : 256 * r + 256, :], w))

    weight(0)

    def put_q(r, v):
        qb[r : r + 256, :] = ((v + vecs[0:1, :]).astype(BF).astype(F32) * 0.125).astype(BF)

    project(0, x, put_q)
    pump(3)
    weight(1)

    def put(dst, half, bias_row):
        def fn(r, v):
            if bias_row is not None:
                v = v + vecs[bias_row : bias_row + 1, :]
            dst[pl.ds(pl.multiple_of(half * 512 + r, 256), 256), :] = v.astype(BF)

        return fn

    project(1, x, put(kb, x, None))
    pump(4)
    weight(2)
    project(2, x, put(vb, x, 1))
    cps[0].wait_recv()
    cps[1].wait_recv()
    project(1, 1 - x, put(kb, 1 - x, None))
    pump(5)
    project(2, 1 - x, put(vb, 1 - x, 1))

    def pair(i):
        v = segb[i].astype(F32)
        r = lax.broadcasted_iota(jnp.int32, (16, 512), 0)
        return jnp.where(r == 0, v, jnp.where(r == 1, 1.0 - v, 0.0)).astype(BF)

    mine = pair(x)
    for i in range(2):
        same = dot(mine, pair(i), TN)
        bias[:, 512 * i : 512 * i + 512] = (same - 1.0) * -far_value
    saves = [
        pltpu.make_async_copy(a, b, osem.at[i])
        for i, (a, b) in enumerate(((xb, x_out), (qb, q_out), (kb, k_out), (vb, v_out)))
    ]
    for cp in saves:
        cp.start()

    def pcp(h):
        return pltpu.make_async_copy(pb.at[h % 2], p_out.at[pl.ds(2 * h, 2)], psem.at[h])

    def attn(h, carry):
        cs = pl.ds(pl.multiple_of(h * 128, 128), 128)

        @pl.when(h >= 2)
        def _():
            pcp(jnp.maximum(h - 2, 0)).wait()

        qq, kk, vv = qb[:, cs], kb[:, cs], vb[:, cs]
        parts = []
        for i in range(2):
            cols = slice(64 * i, 64 * i + 64)
            sc = dot(qq[:, cols], kk[:, cols], NT) + bias[...]
            m = jnp.max(sc, axis=1, keepdims=True)
            e = jnp.exp(sc - m)
            p = (e * (1.0 / jnp.sum(e, axis=1, keepdims=True))).astype(BF)
            pb[h % 2, i] = p
            parts.append(dot(p, vv[:, cols]))
        mixb[:, cs] = jnp.concatenate(parts, axis=1).astype(BF)
        pcp(h).start()
        for i in range(6):

            @pl.when(h == i)
            def _(i=i):
                pump(6 + i)

        return carry

    lax.fori_loop(0, 6, attn, 0)
    mix_cp = pltpu.make_async_copy(mixb, mix_out, osem.at[4])
    mix_cp.start()
    for t in range(12, n + 2):
        pump(t)
    for cp in cps:
        cp.wait_send()
    for k in range(n):
        for cp in ccp[k]:
            cp.wait_send()
            if k >= 3:
                cp.wait_recv()
        for cp in [ycp[k]] + relays[k] + seconds[k]:
            cp.wait_send()
    for cp in outs[3:] + saves + [mix_cp, pcp(4), pcp(5)]:
        cp.wait()


def forward_all(*args):
    sd = jax.ShapeDtypeStruct
    n = 10
    dma = pltpu.SemaphoreType.DMA
    vm = pltpu.VMEM
    square = lambda: sd((4, 192, 768), BF)
    return pl.pallas_call(
        forward_kernel,
        name="forward",
        out_shape=[
            square(), square(), square(), square(), sd((4, 192, 3072), BF), sd((4, 768, 768), BF), sd((16, 768), F32),
            sd((2, 512, 768), BF), sd((512, 768), BF), sd((1024, 768), BF), sd((1024, 768), BF), sd((512, 768), BF),
            sd((H, 512, 1024), BF),
        ],
        in_specs=[ANY] * 9,
        out_specs=[ANY] * 6 + [pl.BlockSpec(memory_space=pltpu.VMEM)] + [ANY] * 6,
        scratch_shapes=[
            vm((4, 192, 768), BF), vm((192, 3072), BF), vm((768, 768), BF), vm((4, 16, 768), BF), vm((2, 512, 768), BF),
            vm((2, 1, 512), jnp.int32), vm((3, 4, 192, 768), BF), vm((512, 768), BF), vm((1024, 768), BF),
            vm((1024, 768), BF), vm((512, 768), BF), vm((2, 2, 512, 1024), BF), vm((512, 1024), F32),
            dma((n,)), dma((n,)), dma((n, 4)), dma((n, 4)), dma((n, 5)), dma((n, 5)), dma((5,)), dma((5,)),
            dma((9, 2)), dma((3,)), dma((5,)), dma((6,)),
        ],
        compiler_params=pltpu.CompilerParams(collective_id=0, has_side_effects=True, vmem_limit_bytes=60 * 2**20),
    )(*args)


NCH = 24
CW = 384
LAGS = (2, 4, 6, 8, 10, 12)


def add_into(dst, src, rows, step=32):
    def body(i, carry):
        r = pl.ds(pl.multiple_of(i * step, step), step)
        dst[r, :] = (dst[r, :].astype(F32) + src[r, :].astype(F32)).astype(BF)
        return carry

    lax.fori_loop(0, rows // step, body, 0)


def backward_kernel(
    gd, gffn_in, gmid_in, slope_in, hid_in, z_in, q_in, k_in, v_in, mix_in, p_in, x_in,
    wd, wu, wo, wq, wk, wv, vecs, vec0,
    o_wd, o_wu, o_wo, o_wv, o_wk, o_wq, vec_out, own_out, gx_out,
    kbuf, gbuf, cbuf, ybuf, xbuf, z0buf, z1buf, fin,
    wt, st, gf, hid, zf, gp, gh, tr, qb, kb, vb, mixb, dk, dv, pb, xb, xt, oth, vbuf, vval,
    ksem, csend, crecv, send, recv, vsend, vrecv, gsend, grecv, osem, lsem, wsem, psem,
):
    me = Place()
    x, y, c, zb, z, s = me.x, me.y, me.c, me.zb, me.z, me.s

    def load(i, src, dst):
        return pltpu.make_async_copy(src, dst, lsem.at[i])

    l_gf, l_gh, l_hid = load(0, gffn_in, gf), load(1, gmid_in, gh), load(2, hid_in, hid)
    l_z, l_q, l_k, l_v = load(3, z_in, zf), load(4, q_in, qb), load(5, k_in, kb), load(6, v_in, vb)
    l_mix, l_x = load(7, mix_in, mixb), load(8, x_in, xb)
    own_cp = load(9, gh, own_out)

    def wdcp(j):
        return pltpu.make_async_copy(wd.at[pl.ds(pl.multiple_of(768 * j, 768), 768), :], wt.at[j % 2], wsem.at[0, j])

    def wucp(j):
        return pltpu.make_async_copy(wu.at[:, pl.ds(pl.multiple_of(768 * j, 768), 768)], wt.at[2 + j % 2], wsem.at[1, j])

    def slcp(j):
        return pltpu.make_async_copy(slope_in.at[:, pl.ds(pl.multiple_of(768 * j, 768), 768)], st.at[j % 2], wsem.at[2, j])

    def pcp(h):
        return pltpu.make_async_copy(p_in.at[pl.ds(2 * h, 2)], pb.at[h % 2], psem.at[h])

    w_o = pltpu.make_async_copy(wo, wt.at[0], wsem.at[3, 0])
    w_k = pltpu.make_async_copy(wk, wt.at[2], wsem.at[3, 1])
    w_v = pltpu.make_async_copy(wv, wt.at[1], wsem.at[3, 2])
    w_q = pltpu.make_async_copy(wq, wt.at[3], wsem.at[3, 3])

    def columns(k):
        return pl.ds(pl.multiple_of(k % 2 * CW, CW), CW)

    def source(k, sh):
        cs = columns(k)
        if isinstance(k, int) and k < 8:
            return gd.at[sh, pl.ds(192 * (k // 2), 192), cs]
        return gbuf.at[k // 2 - 4, sh, :, cs]

    def ccp(k, yy):
        return remote(source(k, 2 * yy + 1 - c), cbuf.at[k, yy], csend.at[k, yy], crecv.at[k, yy], me.core_p)

    def kcp(k, yy):
        return pltpu.make_async_copy(source(k, 2 * yy + c), kbuf.at[k, yy], ksem.at[k, yy])

    def core_start(k):
        for yy in range(2):
            ccp(k, yy).start()

    def bits(k):
        e = (k + 16) // 24
        return e, x + e * (zb - x), zb + e * (x - zb)

    def rows(a, n):
        return pl.ds(pl.multiple_of(a * n, 16), n)

    def ycp(k):
        return remote(cbuf.at[k, 1 - y], ybuf.at[k], send.at[0, k], recv.at[0, k], me.y_p)

    def p1cp(k):
        e, b1, b2 = bits(k)
        p = (z + e * (1 - 2 * zb), s, x + (1 - e) * (1 - 2 * x))
        return remote(ybuf.at[k, rows(1 - b1, 96), :], xbuf.at[k], send.at[1, k], recv.at[1, k], p)

    def second(k):
        e = (k + 16) // 24
        return (z + (1 - e) * (1 - 2 * zb), s, x + e * (1 - 2 * x))

    def p2cp(k):
        e, b1, b2 = bits(k)
        return remote(xbuf.at[k, rows(1 - b2, 48), :], z0buf.at[k], send.at[2, k], recv.at[2, k], second(k))

    def z1cp(k):
        return remote(z0buf.at[k], z1buf.at[k], send.at[3, k], recv.at[3, k], me.z1_p)

    def a2cp(k):
        e, b1, b2 = bits(k)
        r = fin.at[k, rows(2 * b1 + b2, 48), :]
        return remote(r, r, send.at[4, k], recv.at[4, k], second(k))

    def a1cp(k):
        e, b1, b2 = bits(k)
        r = fin.at[k, rows(b1, 96), :]
        p = (z + e * (1 - 2 * zb), s, x + (1 - e) * (1 - 2 * x))
        return remote(r, r, send.at[5, k], recv.at[5, k], p)

    def branch(cond, fn):
        if isinstance(cond, bool):
            if cond:
                fn()
        else:
            pl.when(cond)(fn)

    def out_copy(k, act):
        def wd_out():
            kk = jnp.minimum(k, 7) // 2
            o = o_wd.at[pl.ds(pl.multiple_of(192 * kk, 192), 192), columns(k)]
            act(pltpu.make_async_copy(fin.at[k], o, osem.at[k]))

        def wu_out():
            kk = jnp.clip(k - 8, 0, 7)
            o = o_wu.at[:, pl.ds(pl.multiple_of(CW * kk, CW), CW)]
            act(pltpu.make_async_copy(fin.at[k], o, osem.at[k]))

        branch(k < 8, wd_out)
        both = (8 <= k < 16) if isinstance(k, int) else jnp.logical_and(k >= 8, k < 16)
        branch(both, wu_out)
        for i, o in enumerate((o_wo, o_wv, o_wk, o_wq)):
            branch(k // 2 == 8 + i, lambda o=o: act(pltpu.make_async_copy(fin.at[k], o.at[:, columns(k)], osem.at[k])))

    def pump(t):
        def at(d, fn):
            k = t - d
            if isinstance(k, int):
                if 0 <= k < NCH:
                    fn(k)
            else:
                pl.when(jnp.logical_and(k >= 0, k < NCH))(lambda: fn(jnp.clip(k, 0, NCH - 1)))

        def core(k):
            for yy in range(2):
                remote(cbuf.at[k, yy], cbuf.at[k, yy], csend.at[k, yy], crecv.at[k, yy], me.core_p).wait_recv()

            def first():
                kk = jnp.minimum(k, 7)
                for yy in range(2):
                    pltpu.make_async_copy(kbuf.at[kk, yy], kbuf.at[kk, yy], ksem.at[kk, yy]).wait()
                    add_into(cbuf.at[k, yy], kbuf.at[kk, yy], 192)

            def later():
                kk = jnp.maximum(k - 8, 0) // 2
                for yy in range(2):
                    add_into(cbuf.at[k, yy], gbuf.at[kk, 2 * yy + c, :, columns(k)], 192)

            branch(k < 8, first)
            branch(k >= 8, later)

        def s_p1(k):
            e, b1, b2 = bits(k)
            p1cp(k).wait_recv()
            add_into(xbuf.at[k], ybuf.at[k, rows(b1, 96), :], 96)
            p2cp(k).start()

        def s_p2(k):
            e, b1, b2 = bits(k)
            p2cp(k).wait_recv()
            add_into(z0buf.at[k], xbuf.at[k, rows(b2, 48), :], 48, 16)
            z1cp(k).start()

        def s_z1(k):
            e, b1, b2 = bits(k)
            z1cp(k).wait_recv()
            fin[k, rows(2 * b1 + b2, 48), :] = (z0buf[k].astype(F32) + z1buf[k].astype(F32)).astype(BF)
            a2cp(k).start()

        def s_a2(k):
            a2cp(k).wait_recv()
            a1cp(k).start()

        def s_a1(k):
            a1cp(k).wait_recv()
            out_copy(k, lambda cp: cp.start())

        def s_y(k):
            ycp(k).wait_recv()
            add_into(ybuf.at[k], cbuf.at[k, y], 192)
            p1cp(k).start()

        at(0, core)
        for lag, stage in zip(LAGS, (s_y, s_p1, s_p2, s_z1, s_a2, s_a1)):
            at(lag, stage)
        at(0, lambda k: ycp(k).start())

    greet([me.core_p, me.y_p, me.x_p, me.z0_p, me.z1_p])

    def first_chunks(ks):
        for k in ks:
            core_start(k)
            for yy in range(2):
                kcp(k, yy).start()

    first_chunks((0, 1))
    l_gf.start()
    wdcp(0).start()
    slcp(0).start()
    l_hid.start()
    pump(0)
    first_chunks((2, 3))
    wucp(0).start()
    l_gh.start()
    pump(1)
    first_chunks((4, 5, 6, 7))
    wdcp(1).start()
    slcp(1).start()
    wucp(1).start()
    vval[0] = vec0[...]

    def transposed(dst, src, n):
        for i in range(n // 256):
            dst[:, 256 * i : 256 * i + 256] = src[256 * i : 256 * i + 256, :].T

    def weight_grad(lhs, rhs, k):
        def body(n, carry):
            cs = pl.ds(pl.multiple_of(n * 256, 256), 256)
            r = dot(lhs[...], rhs[:, cs]).astype(BF)
            for sh in range(4):
                gbuf[k - 4, sh, :, cs] = r[192 * sh : 192 * sh + 192]
            return carry

        lax.fori_loop(0, 3, body, 0)
        core_start(2 * k)
        core_start(2 * k + 1)

    def blocks(n, step, fn, init):
        return lax.fori_loop(0, n // step, lambda i, a: fn(pl.ds(pl.multiple_of(i * step, step), step), a), init)

    zero = jnp.zeros((1, D), F32)
    l_gf.wait()
    l_hid.wait()
    transposed(tr, hid, 512)
    l_gh.wait()

    def ffn(j, carry):
        wdcp(j).wait()
        slcp(j).wait()
        sl = j % 2

        def up(r, a):
            t = (dot(gf[r, :], wt[sl], NT) * st[sl, r, :].astype(F32)).astype(BF)
            gp[r, :] = t
            return a + jnp.sum(t.astype(F32), 0, keepdims=True)

        vval[0, pl.ds(8 + j, 1), :] = blocks(512, 256, up, zero)
        weight_grad(tr, gp, 4 + j)
        pump(2 + 2 * j)
        wucp(j).wait()

        def down(r, a):
            gh[r, :] = gh[r, :] + dot(gp[r, :], wt[2 + sl], NT)
            return a

        blocks(512, 256, down, 0)

        @pl.when(j < 2)
        def _():
            jj = jnp.minimum(j + 2, 3)
            wdcp(jj).start()
            slcp(jj).start()
            wucp(jj).start()

        @pl.when(j == 2)
        def _():
            w_o.start()
            w_k.start()

        @pl.when(j == 3)
        def _():
            w_v.start()
            w_q.start()

        for i, cps in enumerate(((l_z, l_mix, l_q), (l_k, pcp(0)), (l_v, pcp(1)), (l_x,))):

            @pl.when(j == i)
            def _(cps=cps):
                for cp in cps:
                    cp.start()

        pump(3 + 2 * j)
        return carry

    lax.fori_loop(0, 4, ffn, 0)

    pump(10)
    l_z.wait()
    l_mix.wait()
    gain = vecs[3:4, :]

    def norm(r, a):
        zz = zf[r, :]
        m = jnp.mean(zz, -1, keepdims=True)
        zz = zz - m
        inv = lax.rsqrt(jnp.mean(zz * zz, -1, keepdims=True) + norm_eps)
        n = zz * inv
        e = gh[r, :]
        ge = e * gain
        g = (ge - jnp.mean(ge, -1, keepdims=True) - n * jnp.mean(ge * n, -1, keepdims=True)) * inv
        gh[r, :] = g
        low = g.astype(BF)
        gf[r, :] = low
        total = lambda v: jnp.sum(v, 0, keepdims=True)
        return a[0] + total(low.astype(F32)), a[1] + total(e * n), a[2] + total(e)

    sums = blocks(512, 64, norm, (zero, zero, zero))
    for i in range(3):
        vval[0, 2 + i : 3 + i, :] = sums[i]
    transposed(tr, mixb, 512)
    weight_grad(tr, gf, 8)
    w_o.wait()

    def mixg(r, a):
        hid[r, :] = dot(gf[r, :], wt[0], NT).astype(BF)
        return a

    blocks(512, 256, mixg, 0)
    l_q.wait()
    l_k.wait()
    l_v.wait()
    pump(11)

    def attn(h, carry):
        cs = pl.ds(pl.multiple_of(h * 128, 128), 128)
        pcp(h).wait()
        g = hid[:, cs]
        prod = g.astype(F32) * mixb[:, cs].astype(F32)
        gt = g.T
        qt = qb[:, cs].T
        kk = kb[:, cs]
        vv = vb[:, cs]
        dqs, dks, dvs = [], [], []
        for i in range(2):
            cols = slice(64 * i, 64 * i + 64)
            p = pb[h % 2, i]
            delta = jnp.sum(prod[:, cols], axis=1, keepdims=True)
            dp = dot(g[:, cols], vv[:, cols], NT)
            gs = (p.astype(F32) * (dp - delta)).astype(BF)
            dqs.append(dot(gs, kk[:, cols]) * 0.125)
            dks.append(dot(qt[cols, :], gs))
            dvs.append(dot(gt[cols, :], p))
        gp[:, cs] = jnp.concatenate(dqs, axis=1).astype(BF)
        dk[:, cs] = jnp.concatenate(dks, axis=0).T.astype(BF)
        dv[:, cs] = jnp.concatenate(dvs, axis=0).T.astype(BF)

        @pl.when(h < 4)
        def _():
            pcp(jnp.minimum(h + 2, 5)).start()

        pump(12 + h)
        return carry

    lax.fori_loop(0, 6, attn, 0)
    l_x.wait()
    transposed(xt, xb, 1024)
    weight_grad(xt, dv, 9)
    pump(18)
    weight_grad(xt, dk, 10)
    pump(19)
    weight_grad(xt.at[:, pl.ds(pl.multiple_of(x * 512, 512), 512)], gp, 11)
    w_k.wait()
    w_v.wait()
    w_q.wait()

    def gxcp(i):
        r = pl.ds(128 * i, 128)
        return remote(oth.at[r, :], gx_out.at[r, :], gsend.at[i], grecv.at[i], me.x_p)

    for i in range(2):
        r = pl.ds(pl.multiple_of((1 - x) * 512 + 256 * i, 256), 256)
        oth[256 * i : 256 * i + 256, :] = (dot(dk[r, :], wt[2], NT) + dot(dv[r, :], wt[1], NT)).astype(BF)
    pump(20)
    gxcp(0).start()

    def colsum(r, a):
        return a + jnp.sum(dv[r, :].astype(F32), 0, keepdims=True)

    def colsum_q(r, a):
        return a + jnp.sum(gp[r, :].astype(F32), 0, keepdims=True)

    vval[0, 0:1, :] = blocks(512, 128, colsum_q, zero)
    vval[0, 1:2, :] = blocks(1024, 128, colsum, zero)
    vps = (me.core_p, me.y_p, me.x_p, me.z0_p, me.z1_p)
    vcps = [remote(vval.at[b], vbuf.at[b], vsend.at[b], vrecv.at[b], vps[b]) for b in range(5)]
    vcps[0].start()
    pump(21)
    gxcp(1).start()

    def own(i, carry):
        r = pl.ds(pl.multiple_of(256 * i, 256), 256)
        ro = pl.ds(pl.multiple_of(x * 512 + 256 * i, 256), 256)
        gh[r, :] = gh[r, :] + dot(gp[r, :], wt[3], NT) + dot(dk[ro, :], wt[2], NT) + dot(dv[ro, :], wt[1], NT)
        return carry

    lax.fori_loop(0, 2, own, 0)
    own_cp.start()
    for t in range(22, NCH + LAGS[-1]):
        pump(t)
        b = t - 22
        if b < 2:
            gxcp(2 + b).start()
        if b < 5:
            vcps[b].wait_recv()
            if b < 4:
                vval[b + 1] = vval[b] + vbuf[b]
                vcps[b + 1].start()
            else:
                vec_out[...] = vval[b] + vbuf[b]

    def finish(k, carry):
        for f in (ycp, p1cp, p2cp, z1cp, a2cp, a1cp):
            f(k).wait_send()
        for yy in range(2):
            remote(cbuf.at[k, yy], cbuf.at[k, yy], csend.at[k, yy], crecv.at[k, yy], me.core_p).wait_send()
        out_copy(k, lambda cp: cp.wait())
        return carry

    lax.fori_loop(0, NCH, finish, 0)
    for cp in vcps:
        cp.wait_send()
    own_cp.wait()
    for i in range(4):
        gxcp(i).wait()


def backward_all(*args):
    sd = jax.ShapeDtypeStruct
    dma = pltpu.SemaphoreType.DMA
    vm = pltpu.VMEM
    vspec = pl.BlockSpec(memory_space=pltpu.VMEM)
    one = lambda: sd((192, 768), BF)
    half = lambda: vm((512, 768), BF)
    full = lambda: vm((1024, 768), BF)
    return pl.pallas_call(
        backward_kernel,
        name="backward",
        out_shape=[
            sd((768, 768), BF), sd((192, 3072), BF), one(), one(), one(), one(),
            sd((16, 768), F32), sd((512, 768), F32), sd((512, 768), BF),
        ],
        in_specs=[ANY] * 18 + [vspec] * 2,
        out_specs=[ANY] * 6 + [vspec, ANY, ANY],
        scratch_shapes=[
            vm((8, 2, 192, CW), BF), vm((8, 4, 192, 768), BF), vm((NCH, 2, 192, CW), BF), vm((NCH, 192, CW), BF),
            vm((NCH, 96, CW), BF), vm((NCH, 48, CW), BF), vm((NCH, 48, CW), BF), vm((NCH, 192, CW), BF),
            vm((4, 768, 768), BF), vm((2, 512, 768), BF), half(), half(), vm((512, 768), F32), half(), vm((512, 768), F32),
            vm((768, 512), BF), half(), full(), full(), half(), full(), full(), vm((2, 2, 512, 1024), BF),
            full(), vm((768, 1024), BF), half(), vm((5, 16, 768), F32), vm((5, 16, 768), F32),
            dma((8, 2)), dma((NCH, 2)), dma((NCH, 2)), dma((6, NCH)), dma((6, NCH)), dma((5,)), dma((5,)), dma((4,)), dma((4,)),
            dma((NCH,)), dma((10,)), dma((4, 4)), dma((6,)),
        ],
        compiler_params=pltpu.CompilerParams(collective_id=1, has_side_effects=True, vmem_limit_bytes=63 * 2**20),
    )(*args)


def layer_norm(total_rows, gain_vec, shift_vec):
    row_mean = jnp.mean(total_rows, -1, keepdims=True)
    centred = total_rows - row_mean
    variance = jnp.mean(centred * centred, -1, keepdims=True)
    inv_std = lax.rsqrt(variance + norm_eps)
    normed = centred * inv_std
    return (normed * gain_vec + shift_vec, normed, inv_std)


def norm_grad(grad_in, normed, inv_std, gain_vec):
    scaled = grad_in * gain_vec
    centred_grad = (
        scaled
        - jnp.mean(scaled, -1, keepdims=True)
        - normed * jnp.mean(scaled * normed, -1, keepdims=True)
    )
    return (centred_grad * inv_std, jnp.sum(grad_in * normed, 0), jnp.sum(grad_in, 0))


def shards(
    inputs, segments, cotangent, w_query, b_query, w_key, w_value, b_value, w_out, b_out,
    gain_one, shift_one, w_up, b_up, w_down, b_down, gain_two, shift_two,
):
    x_own = inputs[0]
    singles = (b_query, b_value, b_out, gain_one, shift_one, b_down, gain_two, shift_two, b_up)
    small = sum(jnp.pad(a, (D * i, 16 * D - D * i - a.shape[0])) for i, a in enumerate(singles)).reshape(16, D)
    wq, wk, wv, wo, wu, wd, vecs, xf, q8, keys, values, mixture, probs = forward_all(
        w_query, w_key, w_value, w_out, w_up, w_down, small, x_own, segments
    )
    wq, wk, wv, wo, wu, wd = (w.reshape(-1, w.shape[-1]) for w in (wq, wk, wv, wo, wu, wd))
    bo, g1, s1, bd, g2, s2 = (vecs[i : i + 1] for i in range(2, 8))
    bu = vecs[8:12].reshape(1, FF)
    x_all = xf.reshape(-1, D)

    attn_out = dot(mixture, wo) + bo
    z_one = x_own.astype(F32) + attn_out
    norm_one, _, _ = layer_norm(z_one, g1, s1)
    hidden_low = norm_one.astype(BF)
    pre_act = dot(hidden_low, wu) + bu
    phi = 0.5 * (1.0 + lax.erf(pre_act * (2.0**-0.5)))
    act_low = (pre_act * phi).astype(BF)
    slope = (phi + pre_act * jnp.exp(-0.5 * pre_act * pre_act) * (2 * math.pi) ** -0.5).astype(BF)
    ffn_out = dot(act_low, wd) + bd
    result, normed_two, inv_two = layer_norm(norm_one + ffn_out, g2, s2)

    grad_mid, d_g2, d_s2 = norm_grad(cotangent[0].astype(F32), normed_two, inv_two, g2)
    grad_ffn = grad_mid.astype(BF)
    d_bd = jnp.sum(grad_ffn.astype(F32), 0)
    d_wd = dot(act_low, grad_ffn, TN).astype(BF)
    vec0 = jnp.zeros((16, D), F32)
    for i, a in ((5, d_bd), (6, d_g2), (7, d_s2)):
        vec0 = vec0 + jnp.pad(a.reshape(1, D), ((i, 15 - i), (0, 0)))
    o_wd, o_wu, o_wo, o_wv, o_wk, o_wq, vec, own_part, gx = backward_all(
        d_wd.reshape(4, -1, D), grad_ffn, grad_mid, slope, hidden_low, z_one, q8, keys, values, mixture, probs, x_all,
        wd, wu, wo, wq, wk, wv, vecs, vec0,
    )
    o_wd, o_wu, o_wo, o_wv, o_wk, o_wq = (a.astype(F32) for a in (o_wd, o_wu, o_wo, o_wv, o_wk, o_wq))
    sh = lax.axis_index("shard")
    mine = lax.dynamic_slice(vec[:8], (0, sh * 192), (8, 192))
    o_bq, o_bv, o_bo, o_g1, o_s1, o_bd, o_g2, o_s2 = (mine[i] for i in range(8))
    o_bu = lax.dynamic_index_in_dim(vec[8:12], sh, 0, False)
    grad_input = own_part + gx.astype(F32)
    return (
        result.astype(BF)[None], grad_input[None], o_wq, o_bq, o_wk, o_wv, o_bv, o_wo, o_bo,
        o_g1, o_s1, o_wu, o_bu, o_wd, o_bd, o_g2, o_s2,
    )


def make(mesh, body):
    in_specs = (
        P(("rep", "shard"), "seq", None), P(("rep", "shard"), "seq"), P(("rep", "shard"), "seq", None),
        P("shard", None), P("shard"), P("shard", None), P("shard", None), P("shard"), P("shard", None), P("shard"),
        P("shard"), P("shard"), P("shard", None), P("shard"), P("shard", None), P("shard"), P("shard"), P("shard"),
    )
    out_specs = (
        P(("rep", "shard"), "seq", None), P(("rep", "shard"), "seq", None),
        P("shard", None), P("shard"), P("shard", None), P("shard", None), P("shard"), P("shard", None), P("shard"),
        P("shard"), P("shard"), P("shard", None), P("shard"), P("shard", None), P("shard"), P("shard"), P("shard"),
    )
    return jax.shard_map(body, mesh=mesh, in_specs=in_specs, out_specs=out_specs, check_vma=False)


param_names = (
    "w_query",
    "b_query",
    "w_key",
    "w_value",
    "b_value",
    "w_out",
    "b_out",
    "gain_one",
    "shift_one",
    "w_up",
    "b_up",
    "w_down",
    "b_down",
    "gain_two",
    "shift_two",
)


def as_sent(x):
    return jax.tree.map(lambda a: a.astype(jnp.bfloat16) if a.dtype == jnp.float32 else a, x)


def general_layer_norm(total_rows, gain_vec, shift_vec):
    row_mean = jnp.mean(total_rows, -1, keepdims=True)
    centred = total_rows - row_mean
    variance = jnp.mean(centred * centred, -1, keepdims=True)
    inv_std = lax.rsqrt(variance + norm_eps)
    normed = centred * inv_std
    return (normed * gain_vec + shift_vec, normed, inv_std)


def general_norm_grad(grad_in, normed, inv_std, gain_vec):
    scaled = grad_in * gain_vec
    centred_grad = (
        scaled
        - jnp.mean(scaled, -1, keepdims=True)
        - normed * jnp.mean(scaled * normed, -1, keepdims=True)
    )
    return (centred_grad * inv_std, jnp.sum(grad_in * normed, 0), jnp.sum(grad_in, 0))


def inner_rows(left, right):
    return lax.dot_general(
        left, right, (((0,), (0,)), ((), ())), preferred_element_type=jnp.float32
    )


def times_transposed(left, matrix):
    return lax.dot_general(
        left, matrix, (((1,), (1,)), ((), ())), preferred_element_type=jnp.float32
    )


def gelu_exact(value):
    return jax.nn.gelu(value, approximate=False)


def general_shards(
    inputs,
    segments,
    cotangent,
    w_query,
    b_query,
    w_key,
    w_value,
    b_value,
    w_out,
    b_out,
    gain_one,
    shift_one,
    w_up,
    b_up,
    w_down,
    b_down,
    gain_two,
    shift_two,
):
    score_scale = DH ** (-0.5)
    token_rows = inputs[0]
    row_count = token_rows.shape[0]
    own_seg = segments[0].astype(jnp.float32)
    local_params = (
        w_query,
        b_query,
        w_key,
        w_value,
        b_value,
        w_out,
        b_out,
        gain_one,
        shift_one,
        w_up,
        b_up,
        w_down,
        b_down,
        gain_two,
        shift_two,
    )
    gathered = (
        lax.all_gather(local_params[0], "shard", axis=0, tiled=True),
        lax.all_gather(local_params[1], "shard", axis=0, tiled=True),
        lax.all_gather(local_params[2], "shard", axis=0, tiled=True),
        lax.all_gather(local_params[3], "shard", axis=0, tiled=True),
        lax.all_gather(local_params[4], "shard", axis=0, tiled=True),
        lax.all_gather(local_params[5], "shard", axis=0, tiled=True),
        lax.all_gather(local_params[6], "shard", axis=0, tiled=True),
        lax.all_gather(local_params[7], "shard", axis=0, tiled=True),
        lax.all_gather(local_params[8], "shard", axis=0, tiled=True),
        lax.all_gather(local_params[9], "shard", axis=0, tiled=True),
        lax.all_gather(local_params[10], "shard", axis=0, tiled=True),
        lax.all_gather(local_params[11], "shard", axis=0, tiled=True),
        lax.all_gather(local_params[12], "shard", axis=0, tiled=True),
        lax.all_gather(local_params[13], "shard", axis=0, tiled=True),
        lax.all_gather(local_params[14], "shard", axis=0, tiled=True),
    )
    weights = dict(zip(param_names, gathered))

    def vector(name):
        return weights[name].astype(jnp.float32)

    q_wide = jnp.dot(token_rows, weights["w_query"], preferred_element_type=jnp.float32) + vector(
        "b_query"
    )
    queries = q_wide.astype(jnp.bfloat16)
    key_rows = jnp.dot(token_rows, weights["w_key"], preferred_element_type=jnp.float32).astype(
        jnp.bfloat16
    )
    value_rows = (
        jnp.dot(token_rows, weights["w_value"], preferred_element_type=jnp.float32)
        + vector("b_value")
    ).astype(jnp.bfloat16)
    seg_wire = segments[0].astype(jnp.bfloat16)
    query_heads = queries.reshape(row_count, H, DH)
    start_state = (
        jnp.full((H, row_count), far_value, jnp.float32),
        jnp.zeros((H, row_count), jnp.float32),
        jnp.zeros((row_count, H, DH), jnp.float32),
    )
    carried = start_state
    piece_keys = lax.all_gather(key_rows, "seq", axis=0, tiled=True)
    piece_values = lax.all_gather(value_rows, "seq", axis=0, tiled=True)
    piece_seg = lax.all_gather(seg_wire, "seq", axis=0, tiled=True)
    piece_rows = piece_keys.shape[0]
    width_blk = math.gcd(piece_rows, 512)
    blocks = piece_rows // width_blk
    key_blocks = piece_keys.reshape(blocks, width_blk, H, DH)
    value_blocks = piece_values.reshape(blocks, width_blk, H, DH)
    seg_blocks = piece_seg.astype(jnp.float32).reshape(blocks, width_blk)

    def update(fold_state, block_item):
        key_blk, value_blk, seg_blk = block_item
        row_peak, row_total, accumulated = fold_state
        scores = (
            jnp.einsum("rhd,khd->hrk", query_heads, key_blk, preferred_element_type=jnp.float32)
            * score_scale
        )
        allowed = own_seg[:, None] == seg_blk[None, :]
        scores = jnp.where(allowed[None], scores, far_value)
        new_peak = jnp.maximum(row_peak, jnp.max(scores, -1))
        factor = jnp.exp(row_peak - new_peak)
        exp_scores = jnp.exp(scores - new_peak[:, :, None])
        row_total = row_total * factor + jnp.sum(exp_scores, -1)
        block_mix = jnp.einsum(
            "hrk,khd->rhd",
            exp_scores.astype(jnp.bfloat16),
            value_blk,
            preferred_element_type=jnp.float32,
        )
        accumulated = accumulated * jnp.transpose(factor)[:, :, None] + block_mix
        return ((new_peak, row_total, accumulated), None)

    carried, unused = lax.scan(update, carried, (key_blocks, value_blocks, seg_blocks))
    row_peak, row_total, accumulated = carried
    mix_wide = (accumulated / jnp.transpose(row_total)[:, :, None]).reshape(row_count, D)
    mixture = mix_wide.astype(jnp.bfloat16)
    log_total = row_peak + jnp.log(row_total)
    attn_out = jnp.dot(mixture, weights["w_out"], preferred_element_type=jnp.float32) + vector(
        "b_out"
    )
    norm_one, normed_one, inv_one = general_layer_norm(
        token_rows.astype(jnp.float32) + attn_out, vector("gain_one"), vector("shift_one")
    )
    hidden_low = norm_one.astype(jnp.bfloat16)
    pre_act = jnp.dot(hidden_low, weights["w_up"], preferred_element_type=jnp.float32) + vector(
        "b_up"
    )
    activated, gelu_pullback = jax.vjp(gelu_exact, pre_act)
    act_low = activated.astype(jnp.bfloat16)
    ffn_out = jnp.dot(act_low, weights["w_down"], preferred_element_type=jnp.float32) + vector(
        "b_down"
    )
    result, normed_two, inv_two = general_layer_norm(
        norm_one + ffn_out, vector("gain_two"), vector("shift_two")
    )
    regathered = (
        lax.all_gather(local_params[0], "shard", axis=0, tiled=True),
        lax.all_gather(local_params[1], "shard", axis=0, tiled=True),
        lax.all_gather(local_params[2], "shard", axis=0, tiled=True),
        lax.all_gather(local_params[3], "shard", axis=0, tiled=True),
        lax.all_gather(local_params[4], "shard", axis=0, tiled=True),
        lax.all_gather(local_params[5], "shard", axis=0, tiled=True),
        lax.all_gather(local_params[6], "shard", axis=0, tiled=True),
        lax.all_gather(local_params[7], "shard", axis=0, tiled=True),
        lax.all_gather(local_params[8], "shard", axis=0, tiled=True),
        lax.all_gather(local_params[9], "shard", axis=0, tiled=True),
        lax.all_gather(local_params[10], "shard", axis=0, tiled=True),
        lax.all_gather(local_params[11], "shard", axis=0, tiled=True),
        lax.all_gather(local_params[12], "shard", axis=0, tiled=True),
        lax.all_gather(local_params[13], "shard", axis=0, tiled=True),
        lax.all_gather(local_params[14], "shard", axis=0, tiled=True),
    )
    backward_set = dict(zip(param_names, regathered))
    grad_out = cotangent[0].astype(jnp.float32)
    grad_mid, grad_gain_two, grad_shift_two = general_norm_grad(
        grad_out, normed_two, inv_two, backward_set["gain_two"].astype(jnp.float32)
    )
    grad_ffn = grad_mid.astype(jnp.bfloat16)
    grad_b_down = jnp.sum(grad_ffn.astype(jnp.float32), 0)
    grad_w_down = inner_rows(act_low, grad_ffn)
    grad_act = times_transposed(grad_ffn, backward_set["w_down"])
    (grad_pre_wide,) = gelu_pullback(grad_act)
    grad_pre = grad_pre_wide.astype(jnp.bfloat16)
    grad_b_up = jnp.sum(grad_pre.astype(jnp.float32), 0)
    grad_w_up = inner_rows(hidden_low, grad_pre)
    grad_hidden = grad_mid + times_transposed(grad_pre, backward_set["w_up"])
    grad_sum_one, grad_gain_one, grad_shift_one = general_norm_grad(
        grad_hidden, normed_one, inv_one, backward_set["gain_one"].astype(jnp.float32)
    )
    grad_attn = grad_sum_one.astype(jnp.bfloat16)
    grad_b_out = jnp.sum(grad_attn.astype(jnp.float32), 0)
    grad_w_out = inner_rows(mixture, grad_attn)
    grad_mixture = times_transposed(grad_attn, backward_set["w_out"]).astype(jnp.bfloat16)
    grad_mix_heads = grad_mixture.reshape(row_count, H, DH)
    row_delta = jnp.transpose(
        jnp.sum((grad_mixture.astype(jnp.float32) * mix_wide).reshape(row_count, H, DH), -1)
    )
    all_keys, all_values, all_seg = (
        lax.all_gather(key_rows, "seq", axis=0, tiled=True),
        lax.all_gather(value_rows, "seq", axis=0, tiled=True),
        lax.all_gather(seg_wire, "seq", axis=0, tiled=True),
    )
    seq_rows = all_keys.shape[0]
    width_all = math.gcd(seq_rows, 512)
    blocks_all = seq_rows // width_all
    key_blocks = all_keys.reshape(blocks_all, width_all, H, DH)
    value_blocks = all_values.reshape(blocks_all, width_all, H, DH)
    seg_blocks = all_seg.astype(jnp.float32).reshape(blocks_all, width_all)

    def block_grads(key_blk, value_blk, seg_blk):
        scores = (
            jnp.einsum("rhd,khd->hrk", query_heads, key_blk, preferred_element_type=jnp.float32)
            * score_scale
        )
        allowed = own_seg[:, None] == seg_blk[None, :]
        scores = jnp.where(allowed[None], scores, far_value)
        probabilities = jnp.exp(scores - log_total[:, :, None])
        grad_probs = jnp.einsum(
            "rhd,khd->hrk", grad_mix_heads, value_blk, preferred_element_type=jnp.float32
        )
        grad_scores = (probabilities * (grad_probs - row_delta[:, :, None])).astype(jnp.bfloat16)
        return (probabilities, grad_scores)

    def back_update(grad_query_acc, block_item):
        key_blk, value_blk, seg_blk = block_item
        back_grad_query_acc = grad_query_acc
        probabilities, grad_scores = block_grads(key_blk, value_blk, seg_blk)
        grad_value_blk = jnp.einsum(
            "hrk,rhd->khd",
            probabilities.astype(jnp.bfloat16),
            grad_mix_heads,
            preferred_element_type=jnp.float32,
        )
        back_grad_query_acc = (
            back_grad_query_acc
            + jnp.einsum("hrk,khd->rhd", grad_scores, key_blk, preferred_element_type=jnp.float32)
            * score_scale
        )
        grad_key_blk = (
            jnp.einsum("hrk,rhd->khd", grad_scores, query_heads, preferred_element_type=jnp.float32)
            * score_scale
        )
        return (back_grad_query_acc, (grad_key_blk, grad_value_blk))

    grad_query_heads, key_value_grads = lax.scan(
        back_update,
        jnp.zeros((row_count, H, DH), jnp.float32),
        (key_blocks, value_blocks, seg_blocks),
    )
    grad_key_all = key_value_grads[0].reshape(seq_rows, D)
    grad_value_all = key_value_grads[1].reshape(seq_rows, D)
    grad_key_rows, grad_value_rows = (
        lax.psum_scatter(
            grad_key_all.astype(jnp.bfloat16), "seq", scatter_dimension=0, tiled=True
        ).astype(jnp.float32),
        lax.psum_scatter(
            grad_value_all.astype(jnp.bfloat16), "seq", scatter_dimension=0, tiled=True
        ).astype(jnp.float32),
    )
    grad_query_low = grad_query_heads.reshape(row_count, D).astype(jnp.bfloat16)
    grad_key_low = grad_key_rows.astype(jnp.bfloat16)
    grad_value_low = grad_value_rows.astype(jnp.bfloat16)
    grad_w_query = inner_rows(token_rows, grad_query_low)
    grad_b_query = jnp.sum(grad_query_low.astype(jnp.float32), 0)
    grad_w_key = inner_rows(token_rows, grad_key_low)
    grad_w_value = inner_rows(token_rows, grad_value_low)
    grad_b_value = jnp.sum(grad_value_low.astype(jnp.float32), 0)
    grad_input = (
        grad_sum_one
        + times_transposed(grad_query_low, backward_set["w_query"])
        + times_transposed(grad_key_low, backward_set["w_key"])
        + times_transposed(grad_value_low, backward_set["w_value"])
    )
    gradients = (
        grad_w_query,
        grad_b_query,
        grad_w_key,
        grad_w_value,
        grad_b_value,
        grad_w_out,
        grad_b_out,
        grad_gain_one,
        grad_shift_one,
        grad_w_up,
        grad_b_up,
        grad_w_down,
        grad_b_down,
        grad_gain_two,
        grad_shift_two,
    )
    owned_grads = (
        lax.psum_scatter(
            gradients[0].astype(jnp.bfloat16), "shard", scatter_dimension=0, tiled=True
        ).astype(jnp.float32),
        lax.psum_scatter(
            gradients[1].astype(jnp.bfloat16), "shard", scatter_dimension=0, tiled=True
        ).astype(jnp.float32),
        lax.psum_scatter(
            gradients[2].astype(jnp.bfloat16), "shard", scatter_dimension=0, tiled=True
        ).astype(jnp.float32),
        lax.psum_scatter(
            gradients[3].astype(jnp.bfloat16), "shard", scatter_dimension=0, tiled=True
        ).astype(jnp.float32),
        lax.psum_scatter(
            gradients[4].astype(jnp.bfloat16), "shard", scatter_dimension=0, tiled=True
        ).astype(jnp.float32),
        lax.psum_scatter(
            gradients[5].astype(jnp.bfloat16), "shard", scatter_dimension=0, tiled=True
        ).astype(jnp.float32),
        lax.psum_scatter(
            gradients[6].astype(jnp.bfloat16), "shard", scatter_dimension=0, tiled=True
        ).astype(jnp.float32),
        lax.psum_scatter(
            gradients[7].astype(jnp.bfloat16), "shard", scatter_dimension=0, tiled=True
        ).astype(jnp.float32),
        lax.psum_scatter(
            gradients[8].astype(jnp.bfloat16), "shard", scatter_dimension=0, tiled=True
        ).astype(jnp.float32),
        lax.psum_scatter(
            gradients[9].astype(jnp.bfloat16), "shard", scatter_dimension=0, tiled=True
        ).astype(jnp.float32),
        lax.psum_scatter(
            gradients[10].astype(jnp.bfloat16), "shard", scatter_dimension=0, tiled=True
        ).astype(jnp.float32),
        lax.psum_scatter(
            gradients[11].astype(jnp.bfloat16), "shard", scatter_dimension=0, tiled=True
        ).astype(jnp.float32),
        lax.psum_scatter(
            gradients[12].astype(jnp.bfloat16), "shard", scatter_dimension=0, tiled=True
        ).astype(jnp.float32),
        lax.psum_scatter(
            gradients[13].astype(jnp.bfloat16), "shard", scatter_dimension=0, tiled=True
        ).astype(jnp.float32),
        lax.psum_scatter(
            gradients[14].astype(jnp.bfloat16), "shard", scatter_dimension=0, tiled=True
        ).astype(jnp.float32),
    )
    owned_grads = jax.tree.map(
        lambda part: part.astype(jnp.float32), lax.psum(as_sent(tuple(owned_grads)), ("rep", "seq"))
    )
    return (result.astype(jnp.bfloat16)[None], grad_input[None]) + tuple(owned_grads)


def solution(mesh):
    if dict(mesh.shape) == {"rep": 4, "shard": 4, "seq": 2}:
        return make(mesh, shards)
    return make(mesh, general_shards)
```

```python
import functools
import math

import jax
import jax.numpy as jnp
from jax import lax
from jax.experimental import pallas as pl
from jax.experimental.pallas import tpu as pltpu
from jax.sharding import PartitionSpec as P

D = 768
H = 12
DH = 64
FF = 3072
MESH = pl.DeviceIdType.MESH
F32 = jnp.float32
BF = jnp.bfloat16
ANY = pl.BlockSpec(memory_space=pl.ANY)

norm_eps = 1e-05
far_value = -1e30


class Place:
    def __init__(self):
        self.z = lax.axis_index("rep")
        self.s = lax.axis_index("shard")
        self.x = lax.axis_index("seq")
        self.y = self.s // 2
        self.c = self.s % 2
        self.zb = self.z % 2
        self.zh = self.z // 2
        zb, zh, x, y, c = self.zb, self.zh, self.x, self.y, self.c
        self.core_p = (self.z, 2 * y + 1 - c, x)
        self.y_p = (self.z, 2 * (1 - y) + c, x)
        self.diag_p = (self.z, 2 * (1 - y) + 1 - c, x)
        self.x_p = (self.z, self.s, 1 - x)
        self.z0_p = (2 * zh + 1 - zb, self.s, x)
        self.z1_p = (2 * (1 - zh) + zb, self.s, x)


def greet(partners):
    barrier = pltpu.get_barrier_semaphore()
    for p in partners:
        pl.semaphore_signal(barrier, inc=1, device_id=p, device_id_type=MESH)
    pl.semaphore_wait(barrier, len(partners))


def remote(src, dst, ssem, rsem, dev):
    return pltpu.make_async_remote_copy(
        src_ref=src, dst_ref=dst, send_sem=ssem, recv_sem=rsem, device_id=dev, device_id_type=MESH
    )


NT = (((1,), (1,)), ((), ()))
TN = (((0,), (0,)), ((), ()))


def dot(a, b, dims=(((1,), (0,)), ((), ()))):
    return lax.dot_general(a, b, dims, preferred_element_type=F32)


L1, L2, YD = 1, 3, 2
KINDS = (1, 2, 2, 2, 2, 1, 1, 0)


def forward_kernel(
    wq, wk, wv, wo, wu, wd, small, x_in, seg_in,
    gq, gk, gv, go, gu, gd, vecs, x_out, q_out, k_out, v_out, mix_out, p_out,
    b768, bu, bd, sb, xb, segb, wb, qb, kb, vb, mixb, pb, bias,
    ysend, yrecv, fsend, frecv, csend, crecv, ssend, srecv, lsem, wsem, osem, psem,
):
    me = Place()
    s, x, zb = me.s, me.x, me.zb
    so = 2 * (1 - me.y) + me.c

    chunks = [(own, full, 0, 192, 0, 768, KINDS[0]) for own, full in ((wq, gq), (wk, gk), (wv, gv))]
    chunks.append((wo, go, 0, 192, 0, 768, KINDS[1]))
    for j in range(2):
        chunks.append((wu, gu, 0, 192, 1536 * j, 1536, KINDS[2 + j]))
    for j in range(4):
        chunks.append((wd, gd, 192 * j, 192, 0, 768, KINDS[4 + j]))
    n = len(chunks)

    greet([me.core_p, me.y_p, me.diag_p, me.x_p, me.z0_p])

    ycp, relays, seconds, lasts, ccp = [], [], [], [], []
    for k, (own, full, r0, rows, c0, cols, kind) in enumerate(chunks):
        cs = pl.ds(c0, cols)
        whole = pl.ds(r0, rows)

        def part(i, h):
            return pl.ds(pl.multiple_of(r0 + i * h, 16), h)

        def relay(i, r, c, dev):
            return remote(full.at[so, r, c], full.at[so, r, c], fsend.at[k, i], frecv.at[k, i], dev)

        def across(i, r):
            return remote(full.at[so, r, cs], full.at[so, r, cs], csend.at[k, i], crecv.at[k, i], me.core_p)

        cc = [remote(own.at[whole, cs], full.at[s, whole, cs], csend.at[k, 0], crecv.at[k, 0], me.core_p)]
        if kind == 2:
            h = rows // 4
            rm, rx = part(2 * x + zb, h), part(2 * (1 - x) + zb, h)
            rz, rd = part(2 * x + 1 - zb, h), part(2 * (1 - x) + 1 - zb, h)
            h0, h1 = pl.ds(c0, cols // 2), pl.ds(c0 + cols // 2, cols // 2)
            relays.append([relay(0, rm, cs, me.x_p), relay(1, rm, cs, me.z0_p)])
            seconds.append([relay(3, rx, h1, me.z0_p), relay(2, rz, h0, me.x_p)])
            cc += [across(1 + i, r) for i, r in enumerate((rm, rx, rz, rd))]
        elif kind == 1:
            h = rows // 2
            rm, rz = part(zb, h), part(1 - zb, h)
            relays.append([relay(1, rm, cs, me.z0_p)])
            seconds.append([])
            cc += [across(1 + i, r) for i, r in enumerate((rm, rz))]
        else:
            rm = whole
            relays.append([])
            seconds.append([])
            cc.append(across(1, rm))
        ycp.append(remote(own.at[rm, cs], full.at[s, rm, cs], ysend.at[k], yrecv.at[k], me.y_p))
        ccp.append(cc)

    def pump(t):
        if t < n:
            ycp[t].wait_recv()
            for cp in relays[t]:
                cp.start()
            ccp[t][1].start()
        k = t - L1
        if 0 <= k < n:
            for i, cp in enumerate(relays[k]):
                cp.wait_recv()
                ccp[k][2 + i].start()
                if seconds[k]:
                    seconds[k][i].start()
        k = t - L2
        if 0 <= k < n and seconds[k]:
            for cp in seconds[k]:
                cp.wait_recv()
            ccp[k][4].start()
        if t + YD < n:
            ycp[t + YD].start()

    cps = [
        remote(x_in, xb.at[x], ssend.at[0], srecv.at[0], me.x_p),
        remote(seg_in, segb.at[x], ssend.at[1], srecv.at[1], me.x_p),
        remote(small, sb.at[s], ssend.at[2], srecv.at[2], me.core_p),
        remote(small, sb.at[s], ssend.at[3], srecv.at[3], me.y_p),
        remote(small, sb.at[s], ssend.at[4], srecv.at[4], me.diag_p),
    ]
    ycp[0].start()
    cps[0].start()
    for k in range(1, YD):
        ycp[k].start()
    for cp in cps[1:]:
        cp.start()
    for k in range(3):
        ccp[k][0].start()
    owns = [(wq, b768.at[0], gq), (wk, b768.at[1], gk), (wv, b768.at[2], gv), (wo, b768.at[3], go), (wu, bu, gu), (wd, bd, gd)]
    ins = [pltpu.make_async_copy(a, b, lsem.at[i, 0]) for i, (a, b, _) in enumerate(owns)]
    outs = [pltpu.make_async_copy(b, f.at[s], lsem.at[i, 1]) for i, (_, b, f) in enumerate(owns)]
    more = [(x_in, xb.at[x]), (seg_in, segb.at[x]), (small, sb.at[s])]
    more = [pltpu.make_async_copy(a, b, lsem.at[6 + i, 0]) for i, (a, b) in enumerate(more)]
    for cp in more + ins:
        cp.start()
    for a, b in zip(ins, outs):
        a.wait()
        b.start()
    for k in range(3, n):
        ccp[k][0].start()
    for cp in more:
        cp.wait()

    def weight(i):
        for cp in ccp[i]:
            cp.wait_recv()
        outs[i].wait()
        cp = pltpu.make_async_copy((gq, gk, gv)[i], wb.at[i], wsem.at[i])
        cp.start()
        cp.wait()

    def whole_weight(i):
        return wb[i].reshape(768, 768)

    pump(0)
    pump(1)
    pump(2)
    for cp in cps[2:]:
        cp.wait_recv()
    row = lax.broadcasted_iota(jnp.int32, (192, 768), 0)
    col = lax.broadcasted_iota(jnp.int32, (192, 768), 1)
    total = jnp.zeros((16, 768), F32)
    for i in range(4):
        pick = jnp.where(col == row + 192 * i, 1.0, 0.0).astype(BF)
        total = total + dot(sb[i, :, 0:192], pick)
    vecs[...] = total
    for i in range(4):
        vecs[8 + i : 9 + i, :] = sb[i].astype(F32)[8:9, :]

    def project(i, half, fn):
        w = whole_weight(i)
        for r in range(2):
            fn(256 * r, dot(xb[half, 256 * r : 256 * r + 256, :], w))

    weight(0)

    def put_q(r, v):
        qb[r : r + 256, :] = ((v + vecs[0:1, :]).astype(BF).astype(F32) * 0.125).astype(BF)

    project(0, x, put_q)
    pump(3)
    weight(1)

    def put(dst, half, bias_row):
        def fn(r, v):
            if bias_row is not None:
                v = v + vecs[bias_row : bias_row + 1, :]
            dst[pl.ds(pl.multiple_of(half * 512 + r, 256), 256), :] = v.astype(BF)

        return fn

    project(1, x, put(kb, x, None))
    pump(4)
    weight(2)
    project(2, x, put(vb, x, 1))
    cps[0].wait_recv()
    cps[1].wait_recv()
    project(1, 1 - x, put(kb, 1 - x, None))
    pump(5)
    project(2, 1 - x, put(vb, 1 - x, 1))

    def pair(i):
        v = segb[i].astype(F32)
        r = lax.broadcasted_iota(jnp.int32, (16, 512), 0)
        return jnp.where(r == 0, v, jnp.where(r == 1, 1.0 - v, 0.0)).astype(BF)

    mine = pair(x)
    for i in range(2):
        same = dot(mine, pair(i), TN)
        bias[:, 512 * i : 512 * i + 512] = (same - 1.0) * -far_value
    saves = [
        pltpu.make_async_copy(a, b, osem.at[i])
        for i, (a, b) in enumerate(((xb, x_out), (qb, q_out), (kb, k_out), (vb, v_out)))
    ]
    for cp in saves:
        cp.start()

    def pcp(h):
        return pltpu.make_async_copy(pb.at[h % 2], p_out.at[pl.ds(2 * h, 2)], psem.at[h])

    def attn(h, carry):
        cs = pl.ds(pl.multiple_of(h * 128, 128), 128)

        @pl.when(h >= 2)
        def _():
            pcp(jnp.maximum(h - 2, 0)).wait()

        qq, kk, vv = qb[:, cs], kb[:, cs], vb[:, cs]
        parts = []
        for i in range(2):
            cols = slice(64 * i, 64 * i + 64)
            sc = dot(qq[:, cols], kk[:, cols], NT) + bias[...]
            m = jnp.max(sc, axis=1, keepdims=True)
            e = jnp.exp(sc - m)
            p = (e * (1.0 / jnp.sum(e, axis=1, keepdims=True))).astype(BF)
            pb[h % 2, i] = p
            parts.append(dot(p, vv[:, cols]))
        mixb[:, cs] = jnp.concatenate(parts, axis=1).astype(BF)
        pcp(h).start()
        for i in range(6):

            @pl.when(h == i)
            def _(i=i):
                pump(6 + i)

        return carry

    lax.fori_loop(0, 6, attn, 0)
    mix_cp = pltpu.make_async_copy(mixb, mix_out, osem.at[4])
    mix_cp.start()
    for t in range(12, n + L2):
        pump(t)
    for cp in cps:
        cp.wait_send()
    for k in range(n):
        for cp in ccp[k]:
            cp.wait_send()
            if k >= 3:
                cp.wait_recv()
        for cp in [ycp[k]] + relays[k] + seconds[k]:
            cp.wait_send()
    for cp in outs[3:] + saves + [mix_cp, pcp(4), pcp(5)]:
        cp.wait()


def forward_all(*args):
    sd = jax.ShapeDtypeStruct
    n = 10
    dma = pltpu.SemaphoreType.DMA
    vm = pltpu.VMEM
    square = lambda: sd((4, 192, 768), BF)
    return pl.pallas_call(
        forward_kernel,
        name="forward",
        out_shape=[
            square(), square(), square(), square(), sd((4, 192, 3072), BF), sd((4, 768, 768), BF), sd((16, 768), F32),
            sd((2, 512, 768), BF), sd((512, 768), BF), sd((1024, 768), BF), sd((1024, 768), BF), sd((512, 768), BF),
            sd((H, 512, 1024), BF),
        ],
        in_specs=[ANY] * 9,
        out_specs=[ANY] * 6 + [pl.BlockSpec(memory_space=pltpu.VMEM)] + [ANY] * 6,
        scratch_shapes=[
            vm((4, 192, 768), BF), vm((192, 3072), BF), vm((768, 768), BF), vm((4, 16, 768), BF), vm((2, 512, 768), BF),
            vm((2, 1, 512), jnp.int32), vm((3, 4, 192, 768), BF), vm((512, 768), BF), vm((1024, 768), BF),
            vm((1024, 768), BF), vm((512, 768), BF), vm((2, 2, 512, 1024), BF), vm((512, 1024), F32),
            dma((n,)), dma((n,)), dma((n, 4)), dma((n, 4)), dma((n, 5)), dma((n, 5)), dma((5,)), dma((5,)),
            dma((9, 2)), dma((3,)), dma((5,)), dma((6,)),
        ],
        compiler_params=pltpu.CompilerParams(collective_id=0, has_side_effects=True, vmem_limit_bytes=60 * 2**20),
    )(*args)


NCH = 24
CW = 384
LAGS = (2, 4, 6, 8, 10, 12)


def add_into(dst, src, rows, step=32):
    def body(i, carry):
        r = pl.ds(pl.multiple_of(i * step, step), step)
        dst[r, :] = (dst[r, :].astype(F32) + src[r, :].astype(F32)).astype(BF)
        return carry

    lax.fori_loop(0, rows // step, body, 0)


def backward_kernel(
    gd, gffn_in, gmid_in, slope_in, hid_in, z_in, q_in, k_in, v_in, mix_in, p_in, x_in,
    wd, wu, wo, wq, wk, wv, vecs, vec0,
    o_wd, o_wu, o_wo, o_wv, o_wk, o_wq, vec_out, own_out, gx_out,
    kbuf, gbuf, cbuf, ybuf, xbuf, z0buf, z1buf, fin,
    wt, st, gf, hid, zf, gp, gh, tr, qb, kb, vb, mixb, dk, dv, pb, xb, xt, oth, vbuf, vval,
    ksem, csend, crecv, send, recv, vsend, vrecv, gsend, grecv, osem, lsem, wsem, psem,
):
    me = Place()
    x, y, c, zb, z, s = me.x, me.y, me.c, me.zb, me.z, me.s

    def load(i, src, dst):
        return pltpu.make_async_copy(src, dst, lsem.at[i])

    l_gf, l_gh, l_hid = load(0, gffn_in, gf), load(1, gmid_in, gh), load(2, hid_in, hid)
    l_z, l_q, l_k, l_v = load(3, z_in, zf), load(4, q_in, qb), load(5, k_in, kb), load(6, v_in, vb)
    l_mix, l_x = load(7, mix_in, mixb), load(8, x_in, xb)
    own_cp = load(9, gh, own_out)

    def wdcp(j):
        return pltpu.make_async_copy(wd.at[pl.ds(pl.multiple_of(768 * j, 768), 768), :], wt.at[j % 2], wsem.at[0, j])

    def wucp(j):
        return pltpu.make_async_copy(wu.at[:, pl.ds(pl.multiple_of(768 * j, 768), 768)], wt.at[2 + j % 2], wsem.at[1, j])

    def slcp(j):
        return pltpu.make_async_copy(slope_in.at[:, pl.ds(pl.multiple_of(768 * j, 768), 768)], st.at[j % 2], wsem.at[2, j])

    def pcp(h):
        return pltpu.make_async_copy(p_in.at[pl.ds(2 * h, 2)], pb.at[h % 2], psem.at[h])

    w_o = pltpu.make_async_copy(wo, wt.at[0], wsem.at[3, 0])
    w_k = pltpu.make_async_copy(wk, wt.at[2], wsem.at[3, 1])
    w_v = pltpu.make_async_copy(wv, wt.at[1], wsem.at[3, 2])
    w_q = pltpu.make_async_copy(wq, wt.at[3], wsem.at[3, 3])

    def columns(k):
        return pl.ds(pl.multiple_of(k % 2 * CW, CW), CW)

    def source(k, sh):
        cs = columns(k)
        if isinstance(k, int) and k < 8:
            return gd.at[sh, pl.ds(192 * (k // 2), 192), cs]
        return gbuf.at[k // 2 - 4, sh, :, cs]

    def ccp(k, yy):
        return remote(source(k, 2 * yy + 1 - c), cbuf.at[k, yy], csend.at[k, yy], crecv.at[k, yy], me.core_p)

    def kcp(k, yy):
        return pltpu.make_async_copy(source(k, 2 * yy + c), kbuf.at[k, yy], ksem.at[k, yy])

    def core_start(k):
        for yy in range(2):
            ccp(k, yy).start()

    def bits(k):
        e = (k + 16) // 24
        return e, x + e * (zb - x), zb + e * (x - zb)

    def rows(a, n):
        return pl.ds(pl.multiple_of(a * n, 16), n)

    def ycp(k):
        return remote(cbuf.at[k, 1 - y], ybuf.at[k], send.at[0, k], recv.at[0, k], me.y_p)

    def p1cp(k):
        e, b1, b2 = bits(k)
        p = (z + e * (1 - 2 * zb), s, x + (1 - e) * (1 - 2 * x))
        return remote(ybuf.at[k, rows(1 - b1, 96), :], xbuf.at[k], send.at[1, k], recv.at[1, k], p)

    def second(k):
        e = (k + 16) // 24
        return (z + (1 - e) * (1 - 2 * zb), s, x + e * (1 - 2 * x))

    def p2cp(k):
        e, b1, b2 = bits(k)
        return remote(xbuf.at[k, rows(1 - b2, 48), :], z0buf.at[k], send.at[2, k], recv.at[2, k], second(k))

    def z1cp(k):
        return remote(z0buf.at[k], z1buf.at[k], send.at[3, k], recv.at[3, k], me.z1_p)

    def a2cp(k):
        e, b1, b2 = bits(k)
        r = fin.at[k, rows(2 * b1 + b2, 48), :]
        return remote(r, r, send.at[4, k], recv.at[4, k], second(k))

    def a1cp(k):
        e, b1, b2 = bits(k)
        r = fin.at[k, rows(b1, 96), :]
        p = (z + e * (1 - 2 * zb), s, x + (1 - e) * (1 - 2 * x))
        return remote(r, r, send.at[5, k], recv.at[5, k], p)

    def branch(cond, fn):
        if isinstance(cond, bool):
            if cond:
                fn()
        else:
            pl.when(cond)(fn)

    def out_copy(k, act):
        def wd_out():
            kk = jnp.minimum(k, 7) // 2
            o = o_wd.at[pl.ds(pl.multiple_of(192 * kk, 192), 192), columns(k)]
            act(pltpu.make_async_copy(fin.at[k], o, osem.at[k]))

        def wu_out():
            kk = jnp.clip(k - 8, 0, 7)
            o = o_wu.at[:, pl.ds(pl.multiple_of(CW * kk, CW), CW)]
            act(pltpu.make_async_copy(fin.at[k], o, osem.at[k]))

        branch(k < 8, wd_out)
        both = (8 <= k < 16) if isinstance(k, int) else jnp.logical_and(k >= 8, k < 16)
        branch(both, wu_out)
        for i, o in enumerate((o_wo, o_wv, o_wk, o_wq)):
            branch(k // 2 == 8 + i, lambda o=o: act(pltpu.make_async_copy(fin.at[k], o.at[:, columns(k)], osem.at[k])))

    def pump(t):
        def at(d, fn):
            k = t - d
            if isinstance(k, int):
                if 0 <= k < NCH:
                    fn(k)
            else:
                pl.when(jnp.logical_and(k >= 0, k < NCH))(lambda: fn(jnp.clip(k, 0, NCH - 1)))

        def core(k):
            for yy in range(2):
                remote(cbuf.at[k, yy], cbuf.at[k, yy], csend.at[k, yy], crecv.at[k, yy], me.core_p).wait_recv()

            def first():
                kk = jnp.minimum(k, 7)
                for yy in range(2):
                    pltpu.make_async_copy(kbuf.at[kk, yy], kbuf.at[kk, yy], ksem.at[kk, yy]).wait()
                    add_into(cbuf.at[k, yy], kbuf.at[kk, yy], 192)

            def later():
                kk = jnp.maximum(k - 8, 0) // 2
                for yy in range(2):
                    add_into(cbuf.at[k, yy], gbuf.at[kk, 2 * yy + c, :, columns(k)], 192)

            branch(k < 8, first)
            branch(k >= 8, later)

        def s_p1(k):
            e, b1, b2 = bits(k)
            p1cp(k).wait_recv()
            add_into(xbuf.at[k], ybuf.at[k, rows(b1, 96), :], 96)
            p2cp(k).start()

        def s_p2(k):
            e, b1, b2 = bits(k)
            p2cp(k).wait_recv()
            add_into(z0buf.at[k], xbuf.at[k, rows(b2, 48), :], 48, 16)
            z1cp(k).start()

        def s_z1(k):
            e, b1, b2 = bits(k)
            z1cp(k).wait_recv()
            fin[k, rows(2 * b1 + b2, 48), :] = (z0buf[k].astype(F32) + z1buf[k].astype(F32)).astype(BF)
            a2cp(k).start()

        def s_a2(k):
            a2cp(k).wait_recv()
            a1cp(k).start()

        def s_a1(k):
            a1cp(k).wait_recv()
            out_copy(k, lambda cp: cp.start())

        def s_y(k):
            ycp(k).wait_recv()
            add_into(ybuf.at[k], cbuf.at[k, y], 192)
            p1cp(k).start()

        at(0, core)
        for lag, stage in zip(LAGS, (s_y, s_p1, s_p2, s_z1, s_a2, s_a1)):
            at(lag, stage)
        at(0, lambda k: ycp(k).start())

    greet([me.core_p, me.y_p, me.x_p, me.z0_p, me.z1_p])

    def first_chunks(ks):
        for k in ks:
            core_start(k)
            for yy in range(2):
                kcp(k, yy).start()

    first_chunks((0, 1))
    l_gf.start()
    wdcp(0).start()
    slcp(0).start()
    l_hid.start()
    pump(0)
    first_chunks((2, 3))
    wucp(0).start()
    l_gh.start()
    pump(1)
    first_chunks((4, 5, 6, 7))
    wdcp(1).start()
    slcp(1).start()
    wucp(1).start()
    vval[0] = vec0[...]

    def transposed(dst, src, n):
        for i in range(n // 256):
            dst[:, 256 * i : 256 * i + 256] = src[256 * i : 256 * i + 256, :].T

    def weight_grad(lhs, rhs, k):
        def body(n, carry):
            cs = pl.ds(pl.multiple_of(n * 256, 256), 256)
            r = dot(lhs[...], rhs[:, cs]).astype(BF)
            for sh in range(4):
                gbuf[k - 4, sh, :, cs] = r[192 * sh : 192 * sh + 192]
            return carry

        lax.fori_loop(0, 3, body, 0)
        core_start(2 * k)
        core_start(2 * k + 1)

    def blocks(n, step, fn, init):
        return lax.fori_loop(0, n // step, lambda i, a: fn(pl.ds(pl.multiple_of(i * step, step), step), a), init)

    zero = jnp.zeros((1, D), F32)
    l_gf.wait()
    l_hid.wait()
    transposed(tr, hid, 512)
    l_gh.wait()

    def ffn(j, carry):
        wdcp(j).wait()
        slcp(j).wait()
        sl = j % 2

        def up(r, a):
            t = (dot(gf[r, :], wt[sl], NT) * st[sl, r, :].astype(F32)).astype(BF)
            gp[r, :] = t
            return a + jnp.sum(t.astype(F32), 0, keepdims=True)

        vval[0, pl.ds(8 + j, 1), :] = blocks(512, 256, up, zero)
        weight_grad(tr, gp, 4 + j)
        pump(2 + 2 * j)
        wucp(j).wait()

        def down(r, a):
            gh[r, :] = gh[r, :] + dot(gp[r, :], wt[2 + sl], NT)
            return a

        blocks(512, 256, down, 0)

        @pl.when(j < 2)
        def _():
            jj = jnp.minimum(j + 2, 3)
            wdcp(jj).start()
            slcp(jj).start()
            wucp(jj).start()

        @pl.when(j == 2)
        def _():
            w_o.start()
            w_k.start()

        @pl.when(j == 3)
        def _():
            w_v.start()
            w_q.start()

        for i, cps in enumerate(((l_z, l_mix, l_q), (l_k, pcp(0)), (l_v, pcp(1)), (l_x,))):

            @pl.when(j == i)
            def _(cps=cps):
                for cp in cps:
                    cp.start()

        pump(3 + 2 * j)
        return carry

    lax.fori_loop(0, 4, ffn, 0)

    pump(10)
    l_z.wait()
    l_mix.wait()
    gain = vecs[3:4, :]

    def norm(r, a):
        zz = zf[r, :]
        m = jnp.mean(zz, -1, keepdims=True)
        zz = zz - m
        inv = lax.rsqrt(jnp.mean(zz * zz, -1, keepdims=True) + norm_eps)
        n = zz * inv
        e = gh[r, :]
        ge = e * gain
        g = (ge - jnp.mean(ge, -1, keepdims=True) - n * jnp.mean(ge * n, -1, keepdims=True)) * inv
        gh[r, :] = g
        low = g.astype(BF)
        gf[r, :] = low
        total = lambda v: jnp.sum(v, 0, keepdims=True)
        return a[0] + total(low.astype(F32)), a[1] + total(e * n), a[2] + total(e)

    sums = blocks(512, 64, norm, (zero, zero, zero))
    for i in range(3):
        vval[0, 2 + i : 3 + i, :] = sums[i]
    transposed(tr, mixb, 512)
    weight_grad(tr, gf, 8)
    w_o.wait()

    def mixg(r, a):
        hid[r, :] = dot(gf[r, :], wt[0], NT).astype(BF)
        return a

    blocks(512, 256, mixg, 0)
    l_q.wait()
    l_k.wait()
    l_v.wait()
    pump(11)

    def attn(h, carry):
        cs = pl.ds(pl.multiple_of(h * 128, 128), 128)
        pcp(h).wait()
        g = hid[:, cs]
        prod = g.astype(F32) * mixb[:, cs].astype(F32)
        gt = g.T
        qt = qb[:, cs].T
        kk = kb[:, cs]
        vv = vb[:, cs]
        dqs, dks, dvs = [], [], []
        for i in range(2):
            cols = slice(64 * i, 64 * i + 64)
            p = pb[h % 2, i]
            delta = jnp.sum(prod[:, cols], axis=1, keepdims=True)
            dp = dot(g[:, cols], vv[:, cols], NT)
            gs = (p.astype(F32) * (dp - delta)).astype(BF)
            dqs.append(dot(gs, kk[:, cols]) * 0.125)
            dks.append(dot(qt[cols, :], gs))
            dvs.append(dot(gt[cols, :], p))
        gp[:, cs] = jnp.concatenate(dqs, axis=1).astype(BF)
        dk[:, cs] = jnp.concatenate(dks, axis=0).T.astype(BF)
        dv[:, cs] = jnp.concatenate(dvs, axis=0).T.astype(BF)

        @pl.when(h < 4)
        def _():
            pcp(jnp.minimum(h + 2, 5)).start()

        pump(12 + h)
        return carry

    lax.fori_loop(0, 6, attn, 0)
    l_x.wait()
    transposed(xt, xb, 1024)
    weight_grad(xt, dv, 9)
    pump(18)
    weight_grad(xt, dk, 10)
    pump(19)
    weight_grad(xt.at[:, pl.ds(pl.multiple_of(x * 512, 512), 512)], gp, 11)
    w_k.wait()
    w_v.wait()
    w_q.wait()

    def gxcp(i):
        r = pl.ds(32 * i, 32)
        return remote(oth.at[r, :], gx_out.at[r, :], gsend.at[i], grecv.at[i], me.x_p)

    for i in range(2):
        r = pl.ds(pl.multiple_of((1 - x) * 512 + 256 * i, 256), 256)
        oth[256 * i : 256 * i + 256, :] = (dot(dk[r, :], wt[2], NT) + dot(dv[r, :], wt[1], NT)).astype(BF)
    pump(20)
    gxcp(0).start()

    def colsum(r, a):
        return a + jnp.sum(dv[r, :].astype(F32), 0, keepdims=True)

    def colsum_q(r, a):
        return a + jnp.sum(gp[r, :].astype(F32), 0, keepdims=True)

    vval[0, 0:1, :] = blocks(512, 128, colsum_q, zero)
    vval[0, 1:2, :] = blocks(1024, 128, colsum, zero)
    vps = (me.core_p, me.y_p, me.x_p, me.z0_p, me.z1_p)
    vcps = [remote(vval.at[b], vbuf.at[b], vsend.at[b], vrecv.at[b], vps[b]) for b in range(5)]
    vcps[0].start()
    pump(21)
    gxcp(1).start()

    def own(i, carry):
        r = pl.ds(pl.multiple_of(256 * i, 256), 256)
        ro = pl.ds(pl.multiple_of(x * 512 + 256 * i, 256), 256)
        gh[r, :] = gh[r, :] + dot(gp[r, :], wt[3], NT) + dot(dk[ro, :], wt[2], NT) + dot(dv[ro, :], wt[1], NT)
        return carry

    lax.fori_loop(0, 2, own, 0)
    own_cp.start()
    for t in range(22, NCH + LAGS[-1]):
        pump(t)
        b = t - 22
        for i in range(16):
            if t == (22 + i - 2 if i < 4 else 22 + i // 2):
                gxcp(i).start()
        if b < 5:
            vcps[b].wait_recv()
            if b < 4:
                vval[b + 1] = vval[b] + vbuf[b]
                vcps[b + 1].start()
            else:
                vec_out[...] = vval[b] + vbuf[b]

    def finish(k, carry):
        for f in (ycp, p1cp, p2cp, z1cp, a2cp, a1cp):
            f(k).wait_send()
        for yy in range(2):
            remote(cbuf.at[k, yy], cbuf.at[k, yy], csend.at[k, yy], crecv.at[k, yy], me.core_p).wait_send()
        out_copy(k, lambda cp: cp.wait())
        return carry

    lax.fori_loop(0, NCH, finish, 0)
    for cp in vcps:
        cp.wait_send()
    own_cp.wait()
    for i in range(16):
        gxcp(i).wait()


def backward_all(*args):
    sd = jax.ShapeDtypeStruct
    dma = pltpu.SemaphoreType.DMA
    vm = pltpu.VMEM
    vspec = pl.BlockSpec(memory_space=pltpu.VMEM)
    one = lambda: sd((192, 768), BF)
    half = lambda: vm((512, 768), BF)
    full = lambda: vm((1024, 768), BF)
    return pl.pallas_call(
        backward_kernel,
        name="backward",
        out_shape=[
            sd((768, 768), BF), sd((192, 3072), BF), one(), one(), one(), one(),
            sd((16, 768), F32), sd((512, 768), F32), sd((512, 768), BF),
        ],
        in_specs=[ANY] * 18 + [vspec] * 2,
        out_specs=[ANY] * 6 + [vspec, ANY, ANY],
        scratch_shapes=[
            vm((8, 2, 192, CW), BF), vm((8, 4, 192, 768), BF), vm((NCH, 2, 192, CW), BF), vm((NCH, 192, CW), BF),
            vm((NCH, 96, CW), BF), vm((NCH, 48, CW), BF), vm((NCH, 48, CW), BF), vm((NCH, 192, CW), BF),
            vm((4, 768, 768), BF), vm((2, 512, 768), BF), half(), half(), vm((512, 768), F32), half(), vm((512, 768), F32),
            vm((768, 512), BF), half(), full(), full(), half(), full(), full(), vm((2, 2, 512, 1024), BF),
            full(), vm((768, 1024), BF), half(), vm((5, 16, 768), F32), vm((5, 16, 768), F32),
            dma((8, 2)), dma((NCH, 2)), dma((NCH, 2)), dma((6, NCH)), dma((6, NCH)), dma((5,)), dma((5,)), dma((16,)), dma((16,)),
            dma((NCH,)), dma((10,)), dma((4, 4)), dma((6,)),
        ],
        compiler_params=pltpu.CompilerParams(collective_id=1, has_side_effects=True, vmem_limit_bytes=63 * 2**20),
    )(*args)


def finish_kernel(wd, wu, wo, wv, wk, wq, own, gx, o_wd, o_wu, o_wo, o_wv, o_wk, o_wq, o_x):
    for a, b in ((wd, o_wd), (wu, o_wu), (wo, o_wo), (wv, o_wv), (wk, o_wk), (wq, o_wq)):
        b[...] = a[...].astype(F32)
    o_x[...] = own[...] + gx[...].astype(F32)


def finish_all(*args):
    steps = 4
    block = lambda a: pl.BlockSpec((a.shape[0] // steps, a.shape[1]), lambda i: (i, 0))
    return pl.pallas_call(
        finish_kernel,
        name="finish",
        grid=(steps,),
        out_shape=[jax.ShapeDtypeStruct(a.shape, F32) for a in args[:7]],
        in_specs=[block(a) for a in args],
        out_specs=[block(a) for a in args[:7]],
    )(*args)


def layer_norm(total_rows, gain_vec, shift_vec):
    row_mean = jnp.mean(total_rows, -1, keepdims=True)
    centred = total_rows - row_mean
    variance = jnp.mean(centred * centred, -1, keepdims=True)
    inv_std = lax.rsqrt(variance + norm_eps)
    normed = centred * inv_std
    return (normed * gain_vec + shift_vec, normed, inv_std)


def norm_grad(grad_in, normed, inv_std, gain_vec):
    scaled = grad_in * gain_vec
    centred_grad = (
        scaled
        - jnp.mean(scaled, -1, keepdims=True)
        - normed * jnp.mean(scaled * normed, -1, keepdims=True)
    )
    return (centred_grad * inv_std, jnp.sum(grad_in * normed, 0), jnp.sum(grad_in, 0))


def shards(
    inputs, segments, cotangent, w_query, b_query, w_key, w_value, b_value, w_out, b_out,
    gain_one, shift_one, w_up, b_up, w_down, b_down, gain_two, shift_two,
):
    x_own = inputs[0]
    singles = (b_query, b_value, b_out, gain_one, shift_one, b_down, gain_two, shift_two, b_up)
    small = sum(jnp.pad(a, (D * i, 16 * D - D * i - a.shape[0])) for i, a in enumerate(singles)).reshape(16, D)
    wq, wk, wv, wo, wu, wd, vecs, xf, q8, keys, values, mixture, probs = forward_all(
        w_query, w_key, w_value, w_out, w_up, w_down, small, x_own, segments
    )
    wq, wk, wv, wo, wu, wd = (w.reshape(-1, w.shape[-1]) for w in (wq, wk, wv, wo, wu, wd))
    bo, g1, s1, bd, g2, s2 = (vecs[i : i + 1] for i in range(2, 8))
    bu = vecs[8:12].reshape(1, FF)
    x_all = xf.reshape(-1, D)

    attn_out = dot(mixture, wo) + bo
    z_one = x_own.astype(F32) + attn_out
    norm_one, _, _ = layer_norm(z_one, g1, s1)
    hidden_low = norm_one.astype(BF)
    pre_act = dot(hidden_low, wu) + bu
    phi = 0.5 * (1.0 + lax.erf(pre_act * (2.0**-0.5)))
    act_low = (pre_act * phi).astype(BF)
    slope = (phi + pre_act * jnp.exp(-0.5 * pre_act * pre_act) * (2 * math.pi) ** -0.5).astype(BF)
    ffn_out = dot(act_low, wd) + bd
    result, normed_two, inv_two = layer_norm(norm_one + ffn_out, g2, s2)

    grad_mid, d_g2, d_s2 = norm_grad(cotangent[0].astype(F32), normed_two, inv_two, g2)
    grad_ffn = grad_mid.astype(BF)
    d_bd = jnp.sum(grad_ffn.astype(F32), 0)
    d_wd = dot(act_low, grad_ffn, TN).astype(BF)
    vec0 = jnp.zeros((16, D), F32)
    for i, a in ((5, d_bd), (6, d_g2), (7, d_s2)):
        vec0 = vec0 + jnp.pad(a.reshape(1, D), ((i, 15 - i), (0, 0)))
    o_wd, o_wu, o_wo, o_wv, o_wk, o_wq, vec, own_part, gx = backward_all(
        d_wd.reshape(4, -1, D), grad_ffn, grad_mid, slope, hidden_low, z_one, q8, keys, values, mixture, probs, x_all,
        wd, wu, wo, wq, wk, wv, vecs, vec0,
    )
    o_wd, o_wu, o_wo, o_wv, o_wk, o_wq, grad_input = finish_all(o_wd, o_wu, o_wo, o_wv, o_wk, o_wq, own_part, gx)
    sh = lax.axis_index("shard")
    mine = lax.dynamic_slice(vec[:8], (0, sh * 192), (8, 192))
    o_bq, o_bv, o_bo, o_g1, o_s1, o_bd, o_g2, o_s2 = (mine[i] for i in range(8))
    o_bu = lax.dynamic_index_in_dim(vec[8:12], sh, 0, False)
    return (
        result.astype(BF)[None], grad_input[None], o_wq, o_bq, o_wk, o_wv, o_bv, o_wo, o_bo,
        o_g1, o_s1, o_wu, o_bu, o_wd, o_bd, o_g2, o_s2,
    )


def make(mesh, body):
    in_specs = (
        P(("rep", "shard"), "seq", None), P(("rep", "shard"), "seq"), P(("rep", "shard"), "seq", None),
        P("shard", None), P("shard"), P("shard", None), P("shard", None), P("shard"), P("shard", None), P("shard"),
        P("shard"), P("shard"), P("shard", None), P("shard"), P("shard", None), P("shard"), P("shard"), P("shard"),
    )
    out_specs = (
        P(("rep", "shard"), "seq", None), P(("rep", "shard"), "seq", None),
        P("shard", None), P("shard"), P("shard", None), P("shard", None), P("shard"), P("shard", None), P("shard"),
        P("shard"), P("shard"), P("shard", None), P("shard"), P("shard", None), P("shard"), P("shard"), P("shard"),
    )
    return jax.shard_map(body, mesh=mesh, in_specs=in_specs, out_specs=out_specs, check_vma=False)


param_names = (
    "w_query",
    "b_query",
    "w_key",
    "w_value",
    "b_value",
    "w_out",
    "b_out",
    "gain_one",
    "shift_one",
    "w_up",
    "b_up",
    "w_down",
    "b_down",
    "gain_two",
    "shift_two",
)


def as_sent(x):
    return jax.tree.map(lambda a: a.astype(jnp.bfloat16) if a.dtype == jnp.float32 else a, x)


def general_layer_norm(total_rows, gain_vec, shift_vec):
    row_mean = jnp.mean(total_rows, -1, keepdims=True)
    centred = total_rows - row_mean
    variance = jnp.mean(centred * centred, -1, keepdims=True)
    inv_std = lax.rsqrt(variance + norm_eps)
    normed = centred * inv_std
    return (normed * gain_vec + shift_vec, normed, inv_std)


def general_norm_grad(grad_in, normed, inv_std, gain_vec):
    scaled = grad_in * gain_vec
    centred_grad = (
        scaled
        - jnp.mean(scaled, -1, keepdims=True)
        - normed * jnp.mean(scaled * normed, -1, keepdims=True)
    )
    return (centred_grad * inv_std, jnp.sum(grad_in * normed, 0), jnp.sum(grad_in, 0))


def inner_rows(left, right):
    return lax.dot_general(
        left, right, (((0,), (0,)), ((), ())), preferred_element_type=jnp.float32
    )


def times_transposed(left, matrix):
    return lax.dot_general(
        left, matrix, (((1,), (1,)), ((), ())), preferred_element_type=jnp.float32
    )


def gelu_exact(value):
    return jax.nn.gelu(value, approximate=False)


def general_shards(
    inputs,
    segments,
    cotangent,
    w_query,
    b_query,
    w_key,
    w_value,
    b_value,
    w_out,
    b_out,
    gain_one,
    shift_one,
    w_up,
    b_up,
    w_down,
    b_down,
    gain_two,
    shift_two,
):
    score_scale = DH ** (-0.5)
    token_rows = inputs[0]
    row_count = token_rows.shape[0]
    own_seg = segments[0].astype(jnp.float32)
    local_params = (
        w_query,
        b_query,
        w_key,
        w_value,
        b_value,
        w_out,
        b_out,
        gain_one,
        shift_one,
        w_up,
        b_up,
        w_down,
        b_down,
        gain_two,
        shift_two,
    )
    gathered = (
        lax.all_gather(local_params[0], "shard", axis=0, tiled=True),
        lax.all_gather(local_params[1], "shard", axis=0, tiled=True),
        lax.all_gather(local_params[2], "shard", axis=0, tiled=True),
        lax.all_gather(local_params[3], "shard", axis=0, tiled=True),
        lax.all_gather(local_params[4], "shard", axis=0, tiled=True),
        lax.all_gather(local_params[5], "shard", axis=0, tiled=True),
        lax.all_gather(local_params[6], "shard", axis=0, tiled=True),
        lax.all_gather(local_params[7], "shard", axis=0, tiled=True),
        lax.all_gather(local_params[8], "shard", axis=0, tiled=True),
        lax.all_gather(local_params[9], "shard", axis=0, tiled=True),
        lax.all_gather(local_params[10], "shard", axis=0, tiled=True),
        lax.all_gather(local_params[11], "shard", axis=0, tiled=True),
        lax.all_gather(local_params[12], "shard", axis=0, tiled=True),
        lax.all_gather(local_params[13], "shard", axis=0, tiled=True),
        lax.all_gather(local_params[14], "shard", axis=0, tiled=True),
    )
    weights = dict(zip(param_names, gathered))

    def vector(name):
        return weights[name].astype(jnp.float32)

    q_wide = jnp.dot(token_rows, weights["w_query"], preferred_element_type=jnp.float32) + vector(
        "b_query"
    )
    queries = q_wide.astype(jnp.bfloat16)
    key_rows = jnp.dot(token_rows, weights["w_key"], preferred_element_type=jnp.float32).astype(
        jnp.bfloat16
    )
    value_rows = (
        jnp.dot(token_rows, weights["w_value"], preferred_element_type=jnp.float32)
        + vector("b_value")
    ).astype(jnp.bfloat16)
    seg_wire = segments[0].astype(jnp.bfloat16)
    query_heads = queries.reshape(row_count, H, DH)
    start_state = (
        jnp.full((H, row_count), far_value, jnp.float32),
        jnp.zeros((H, row_count), jnp.float32),
        jnp.zeros((row_count, H, DH), jnp.float32),
    )
    carried = start_state
    piece_keys = lax.all_gather(key_rows, "seq", axis=0, tiled=True)
    piece_values = lax.all_gather(value_rows, "seq", axis=0, tiled=True)
    piece_seg = lax.all_gather(seg_wire, "seq", axis=0, tiled=True)
    piece_rows = piece_keys.shape[0]
    width_blk = math.gcd(piece_rows, 512)
    blocks = piece_rows // width_blk
    key_blocks = piece_keys.reshape(blocks, width_blk, H, DH)
    value_blocks = piece_values.reshape(blocks, width_blk, H, DH)
    seg_blocks = piece_seg.astype(jnp.float32).reshape(blocks, width_blk)

    def update(fold_state, block_item):
        key_blk, value_blk, seg_blk = block_item
        row_peak, row_total, accumulated = fold_state
        scores = (
            jnp.einsum("rhd,khd->hrk", query_heads, key_blk, preferred_element_type=jnp.float32)
            * score_scale
        )
        allowed = own_seg[:, None] == seg_blk[None, :]
        scores = jnp.where(allowed[None], scores, far_value)
        new_peak = jnp.maximum(row_peak, jnp.max(scores, -1))
        factor = jnp.exp(row_peak - new_peak)
        exp_scores = jnp.exp(scores - new_peak[:, :, None])
        row_total = row_total * factor + jnp.sum(exp_scores, -1)
        block_mix = jnp.einsum(
            "hrk,khd->rhd",
            exp_scores.astype(jnp.bfloat16),
            value_blk,
            preferred_element_type=jnp.float32,
        )
        accumulated = accumulated * jnp.transpose(factor)[:, :, None] + block_mix
        return ((new_peak, row_total, accumulated), None)

    carried, unused = lax.scan(update, carried, (key_blocks, value_blocks, seg_blocks))
    row_peak, row_total, accumulated = carried
    mix_wide = (accumulated / jnp.transpose(row_total)[:, :, None]).reshape(row_count, D)
    mixture = mix_wide.astype(jnp.bfloat16)
    log_total = row_peak + jnp.log(row_total)
    attn_out = jnp.dot(mixture, weights["w_out"], preferred_element_type=jnp.float32) + vector(
        "b_out"
    )
    norm_one, normed_one, inv_one = general_layer_norm(
        token_rows.astype(jnp.float32) + attn_out, vector("gain_one"), vector("shift_one")
    )
    hidden_low = norm_one.astype(jnp.bfloat16)
    pre_act = jnp.dot(hidden_low, weights["w_up"], preferred_element_type=jnp.float32) + vector(
        "b_up"
    )
    activated, gelu_pullback = jax.vjp(gelu_exact, pre_act)
    act_low = activated.astype(jnp.bfloat16)
    ffn_out = jnp.dot(act_low, weights["w_down"], preferred_element_type=jnp.float32) + vector(
        "b_down"
    )
    result, normed_two, inv_two = general_layer_norm(
        norm_one + ffn_out, vector("gain_two"), vector("shift_two")
    )
    regathered = (
        lax.all_gather(local_params[0], "shard", axis=0, tiled=True),
        lax.all_gather(local_params[1], "shard", axis=0, tiled=True),
        lax.all_gather(local_params[2], "shard", axis=0, tiled=True),
        lax.all_gather(local_params[3], "shard", axis=0, tiled=True),
        lax.all_gather(local_params[4], "shard", axis=0, tiled=True),
        lax.all_gather(local_params[5], "shard", axis=0, tiled=True),
        lax.all_gather(local_params[6], "shard", axis=0, tiled=True),
        lax.all_gather(local_params[7], "shard", axis=0, tiled=True),
        lax.all_gather(local_params[8], "shard", axis=0, tiled=True),
        lax.all_gather(local_params[9], "shard", axis=0, tiled=True),
        lax.all_gather(local_params[10], "shard", axis=0, tiled=True),
        lax.all_gather(local_params[11], "shard", axis=0, tiled=True),
        lax.all_gather(local_params[12], "shard", axis=0, tiled=True),
        lax.all_gather(local_params[13], "shard", axis=0, tiled=True),
        lax.all_gather(local_params[14], "shard", axis=0, tiled=True),
    )
    backward_set = dict(zip(param_names, regathered))
    grad_out = cotangent[0].astype(jnp.float32)
    grad_mid, grad_gain_two, grad_shift_two = general_norm_grad(
        grad_out, normed_two, inv_two, backward_set["gain_two"].astype(jnp.float32)
    )
    grad_ffn = grad_mid.astype(jnp.bfloat16)
    grad_b_down = jnp.sum(grad_ffn.astype(jnp.float32), 0)
    grad_w_down = inner_rows(act_low, grad_ffn)
    grad_act = times_transposed(grad_ffn, backward_set["w_down"])
    (grad_pre_wide,) = gelu_pullback(grad_act)
    grad_pre = grad_pre_wide.astype(jnp.bfloat16)
    grad_b_up = jnp.sum(grad_pre.astype(jnp.float32), 0)
    grad_w_up = inner_rows(hidden_low, grad_pre)
    grad_hidden = grad_mid + times_transposed(grad_pre, backward_set["w_up"])
    grad_sum_one, grad_gain_one, grad_shift_one = general_norm_grad(
        grad_hidden, normed_one, inv_one, backward_set["gain_one"].astype(jnp.float32)
    )
    grad_attn = grad_sum_one.astype(jnp.bfloat16)
    grad_b_out = jnp.sum(grad_attn.astype(jnp.float32), 0)
    grad_w_out = inner_rows(mixture, grad_attn)
    grad_mixture = times_transposed(grad_attn, backward_set["w_out"]).astype(jnp.bfloat16)
    grad_mix_heads = grad_mixture.reshape(row_count, H, DH)
    row_delta = jnp.transpose(
        jnp.sum((grad_mixture.astype(jnp.float32) * mix_wide).reshape(row_count, H, DH), -1)
    )
    all_keys, all_values, all_seg = (
        lax.all_gather(key_rows, "seq", axis=0, tiled=True),
        lax.all_gather(value_rows, "seq", axis=0, tiled=True),
        lax.all_gather(seg_wire, "seq", axis=0, tiled=True),
    )
    seq_rows = all_keys.shape[0]
    width_all = math.gcd(seq_rows, 512)
    blocks_all = seq_rows // width_all
    key_blocks = all_keys.reshape(blocks_all, width_all, H, DH)
    value_blocks = all_values.reshape(blocks_all, width_all, H, DH)
    seg_blocks = all_seg.astype(jnp.float32).reshape(blocks_all, width_all)

    def block_grads(key_blk, value_blk, seg_blk):
        scores = (
            jnp.einsum("rhd,khd->hrk", query_heads, key_blk, preferred_element_type=jnp.float32)
            * score_scale
        )
        allowed = own_seg[:, None] == seg_blk[None, :]
        scores = jnp.where(allowed[None], scores, far_value)
        probabilities = jnp.exp(scores - log_total[:, :, None])
        grad_probs = jnp.einsum(
            "rhd,khd->hrk", grad_mix_heads, value_blk, preferred_element_type=jnp.float32
        )
        grad_scores = (probabilities * (grad_probs - row_delta[:, :, None])).astype(jnp.bfloat16)
        return (probabilities, grad_scores)

    def back_update(grad_query_acc, block_item):
        key_blk, value_blk, seg_blk = block_item
        back_grad_query_acc = grad_query_acc
        probabilities, grad_scores = block_grads(key_blk, value_blk, seg_blk)
        grad_value_blk = jnp.einsum(
            "hrk,rhd->khd",
            probabilities.astype(jnp.bfloat16),
            grad_mix_heads,
            preferred_element_type=jnp.float32,
        )
        back_grad_query_acc = (
            back_grad_query_acc
            + jnp.einsum("hrk,khd->rhd", grad_scores, key_blk, preferred_element_type=jnp.float32)
            * score_scale
        )
        grad_key_blk = (
            jnp.einsum("hrk,rhd->khd", grad_scores, query_heads, preferred_element_type=jnp.float32)
            * score_scale
        )
        return (back_grad_query_acc, (grad_key_blk, grad_value_blk))

    grad_query_heads, key_value_grads = lax.scan(
        back_update,
        jnp.zeros((row_count, H, DH), jnp.float32),
        (key_blocks, value_blocks, seg_blocks),
    )
    grad_key_all = key_value_grads[0].reshape(seq_rows, D)
    grad_value_all = key_value_grads[1].reshape(seq_rows, D)
    grad_key_rows, grad_value_rows = (
        lax.psum_scatter(
            grad_key_all.astype(jnp.bfloat16), "seq", scatter_dimension=0, tiled=True
        ).astype(jnp.float32),
        lax.psum_scatter(
            grad_value_all.astype(jnp.bfloat16), "seq", scatter_dimension=0, tiled=True
        ).astype(jnp.float32),
    )
    grad_query_low = grad_query_heads.reshape(row_count, D).astype(jnp.bfloat16)
    grad_key_low = grad_key_rows.astype(jnp.bfloat16)
    grad_value_low = grad_value_rows.astype(jnp.bfloat16)
    grad_w_query = inner_rows(token_rows, grad_query_low)
    grad_b_query = jnp.sum(grad_query_low.astype(jnp.float32), 0)
    grad_w_key = inner_rows(token_rows, grad_key_low)
    grad_w_value = inner_rows(token_rows, grad_value_low)
    grad_b_value = jnp.sum(grad_value_low.astype(jnp.float32), 0)
    grad_input = (
        grad_sum_one
        + times_transposed(grad_query_low, backward_set["w_query"])
        + times_transposed(grad_key_low, backward_set["w_key"])
        + times_transposed(grad_value_low, backward_set["w_value"])
    )
    gradients = (
        grad_w_query,
        grad_b_query,
        grad_w_key,
        grad_w_value,
        grad_b_value,
        grad_w_out,
        grad_b_out,
        grad_gain_one,
        grad_shift_one,
        grad_w_up,
        grad_b_up,
        grad_w_down,
        grad_b_down,
        grad_gain_two,
        grad_shift_two,
    )
    owned_grads = (
        lax.psum_scatter(
            gradients[0].astype(jnp.bfloat16), "shard", scatter_dimension=0, tiled=True
        ).astype(jnp.float32),
        lax.psum_scatter(
            gradients[1].astype(jnp.bfloat16), "shard", scatter_dimension=0, tiled=True
        ).astype(jnp.float32),
        lax.psum_scatter(
            gradients[2].astype(jnp.bfloat16), "shard", scatter_dimension=0, tiled=True
        ).astype(jnp.float32),
        lax.psum_scatter(
            gradients[3].astype(jnp.bfloat16), "shard", scatter_dimension=0, tiled=True
        ).astype(jnp.float32),
        lax.psum_scatter(
            gradients[4].astype(jnp.bfloat16), "shard", scatter_dimension=0, tiled=True
        ).astype(jnp.float32),
        lax.psum_scatter(
            gradients[5].astype(jnp.bfloat16), "shard", scatter_dimension=0, tiled=True
        ).astype(jnp.float32),
        lax.psum_scatter(
            gradients[6].astype(jnp.bfloat16), "shard", scatter_dimension=0, tiled=True
        ).astype(jnp.float32),
        lax.psum_scatter(
            gradients[7].astype(jnp.bfloat16), "shard", scatter_dimension=0, tiled=True
        ).astype(jnp.float32),
        lax.psum_scatter(
            gradients[8].astype(jnp.bfloat16), "shard", scatter_dimension=0, tiled=True
        ).astype(jnp.float32),
        lax.psum_scatter(
            gradients[9].astype(jnp.bfloat16), "shard", scatter_dimension=0, tiled=True
        ).astype(jnp.float32),
        lax.psum_scatter(
            gradients[10].astype(jnp.bfloat16), "shard", scatter_dimension=0, tiled=True
        ).astype(jnp.float32),
        lax.psum_scatter(
            gradients[11].astype(jnp.bfloat16), "shard", scatter_dimension=0, tiled=True
        ).astype(jnp.float32),
        lax.psum_scatter(
            gradients[12].astype(jnp.bfloat16), "shard", scatter_dimension=0, tiled=True
        ).astype(jnp.float32),
        lax.psum_scatter(
            gradients[13].astype(jnp.bfloat16), "shard", scatter_dimension=0, tiled=True
        ).astype(jnp.float32),
        lax.psum_scatter(
            gradients[14].astype(jnp.bfloat16), "shard", scatter_dimension=0, tiled=True
        ).astype(jnp.float32),
    )
    owned_grads = jax.tree.map(
        lambda part: part.astype(jnp.float32), lax.psum(as_sent(tuple(owned_grads)), ("rep", "seq"))
    )
    return (result.astype(jnp.bfloat16)[None], grad_input[None]) + tuple(owned_grads)


def solution(mesh):
    if dict(mesh.shape) == {"rep": 4, "shard": 4, "seq": 2}:
        return make(mesh, shards)
    return make(mesh, general_shards)
```

```python
import functools
import math

import jax
import jax.numpy as jnp
from jax import lax
from jax.experimental import pallas as pl
from jax.experimental.pallas import tpu as pltpu
from jax.sharding import PartitionSpec as P

D = 768
H = 12
DH = 64
FF = 3072
MESH = pl.DeviceIdType.MESH
F32 = jnp.float32
BF = jnp.bfloat16
ANY = pl.BlockSpec(memory_space=pl.ANY)

norm_eps = 1e-05
far_value = -1e30


class Place:
    def __init__(self):
        self.z = lax.axis_index("rep")
        self.s = lax.axis_index("shard")
        self.x = lax.axis_index("seq")
        self.y = self.s // 2
        self.c = self.s % 2
        self.zb = self.z % 2
        self.zh = self.z // 2
        zb, zh, x, y, c = self.zb, self.zh, self.x, self.y, self.c
        self.core_p = (self.z, 2 * y + 1 - c, x)
        self.y_p = (self.z, 2 * (1 - y) + c, x)
        self.diag_p = (self.z, 2 * (1 - y) + 1 - c, x)
        self.x_p = (self.z, self.s, 1 - x)
        self.z0_p = (2 * zh + 1 - zb, self.s, x)
        self.z1_p = (2 * (1 - zh) + zb, self.s, x)


def greet(partners):
    barrier = pltpu.get_barrier_semaphore()
    for p in partners:
        pl.semaphore_signal(barrier, inc=1, device_id=p, device_id_type=MESH)
    pl.semaphore_wait(barrier, len(partners))


def remote(src, dst, ssem, rsem, dev):
    return pltpu.make_async_remote_copy(
        src_ref=src, dst_ref=dst, send_sem=ssem, recv_sem=rsem, device_id=dev, device_id_type=MESH
    )


NT = (((1,), (1,)), ((), ()))
TN = (((0,), (0,)), ((), ()))


def dot(a, b, dims=(((1,), (0,)), ((), ()))):
    return lax.dot_general(a, b, dims, preferred_element_type=F32)


L1, L2, YD = 1, 3, 2
KINDS = (1, 2, 2, 2, 2, 1, 1, 0)


def forward_kernel(
    wq, wk, wv, wo, wu, wd, small, x_in, seg_in,
    gq, gk, gv, go, gu, gd, vecs, x_out, q_out, k_out, v_out, mix_out, p_out,
    b768, bu, bd, sb, xb, segb, wb, qb, kb, vb, mixb, pb, bias,
    ysend, yrecv, fsend, frecv, csend, crecv, ssend, srecv, lsem, wsem, osem, psem,
):
    me = Place()
    s, x, zb = me.s, me.x, me.zb
    so = 2 * (1 - me.y) + me.c

    chunks = [(own, full, 0, 192, 0, 768, KINDS[0]) for own, full in ((wq, gq), (wk, gk), (wv, gv))]
    chunks.append((wo, go, 0, 192, 0, 768, KINDS[1]))
    for j in range(2):
        chunks.append((wu, gu, 0, 192, 1536 * j, 1536, KINDS[2 + j]))
    for j in range(4):
        chunks.append((wd, gd, 192 * j, 192, 0, 768, KINDS[4 + j]))
    n = len(chunks)

    greet([me.core_p, me.y_p, me.diag_p, me.x_p, me.z0_p])

    ycp, relays, seconds, lasts, ccp = [], [], [], [], []
    for k, (own, full, r0, rows, c0, cols, kind) in enumerate(chunks):
        cs = pl.ds(c0, cols)
        whole = pl.ds(r0, rows)

        def part(i, h):
            return pl.ds(pl.multiple_of(r0 + i * h, 16), h)

        def relay(i, r, c, dev):
            return remote(full.at[so, r, c], full.at[so, r, c], fsend.at[k, i], frecv.at[k, i], dev)

        def across(i, r):
            return remote(full.at[so, r, cs], full.at[so, r, cs], csend.at[k, i], crecv.at[k, i], me.core_p)

        cc = [remote(own.at[whole, cs], full.at[s, whole, cs], csend.at[k, 0], crecv.at[k, 0], me.core_p)]
        if kind == 2:
            h = rows // 4
            rm, rx = part(2 * x + zb, h), part(2 * (1 - x) + zb, h)
            rz, rd = part(2 * x + 1 - zb, h), part(2 * (1 - x) + 1 - zb, h)
            h0, h1 = pl.ds(c0, cols // 2), pl.ds(c0 + cols // 2, cols // 2)
            relays.append([relay(0, rm, cs, me.x_p), relay(1, rm, cs, me.z0_p)])
            seconds.append([relay(3, rx, h1, me.z0_p), relay(2, rz, h0, me.x_p)])
            cc += [across(1 + i, r) for i, r in enumerate((rm, rx, rz, rd))]
        elif kind == 1:
            h = rows // 2
            rm, rz = part(zb, h), part(1 - zb, h)
            relays.append([relay(1, rm, cs, me.z0_p)])
            seconds.append([])
            cc += [across(1 + i, r) for i, r in enumerate((rm, rz))]
        else:
            rm = whole
            relays.append([])
            seconds.append([])
            cc.append(across(1, rm))
        ycp.append(remote(own.at[rm, cs], full.at[s, rm, cs], ysend.at[k], yrecv.at[k], me.y_p))
        ccp.append(cc)

    def pump(t):
        if t < n:
            ycp[t].wait_recv()
            for cp in relays[t]:
                cp.start()
            ccp[t][1].start()
        k = t - L1
        if 0 <= k < n:
            for i, cp in enumerate(relays[k]):
                cp.wait_recv()
                ccp[k][2 + i].start()
                if seconds[k]:
                    seconds[k][i].start()
        k = t - L2
        if 0 <= k < n and seconds[k]:
            for cp in seconds[k]:
                cp.wait_recv()
            ccp[k][4].start()
        if t + YD < n:
            ycp[t + YD].start()

    cps = [
        remote(x_in, xb.at[x], ssend.at[0], srecv.at[0], me.x_p),
        remote(seg_in, segb.at[x], ssend.at[1], srecv.at[1], me.x_p),
        remote(small, sb.at[s], ssend.at[2], srecv.at[2], me.core_p),
        remote(small, sb.at[s], ssend.at[3], srecv.at[3], me.y_p),
        remote(small, sb.at[s], ssend.at[4], srecv.at[4], me.diag_p),
    ]
    ycp[0].start()
    cps[0].start()
    for k in range(1, YD):
        ycp[k].start()
    for cp in cps[1:]:
        cp.start()
    for k in range(3):
        ccp[k][0].start()
    owns = [(wq, b768.at[0], gq), (wk, b768.at[1], gk), (wv, b768.at[2], gv), (wo, b768.at[3], go), (wu, bu, gu), (wd, bd, gd)]
    ins = [pltpu.make_async_copy(a, b, lsem.at[i, 0]) for i, (a, b, _) in enumerate(owns)]
    outs = [pltpu.make_async_copy(b, f.at[s], lsem.at[i, 1]) for i, (_, b, f) in enumerate(owns)]
    more = [(x_in, xb.at[x]), (seg_in, segb.at[x]), (small, sb.at[s])]
    more = [pltpu.make_async_copy(a, b, lsem.at[6 + i, 0]) for i, (a, b) in enumerate(more)]
    for cp in more + ins:
        cp.start()
    for a, b in zip(ins, outs):
        a.wait()
        b.start()
    for k in range(3, n):
        ccp[k][0].start()
    for cp in more:
        cp.wait()

    def weight(i):
        for cp in ccp[i]:
            cp.wait_recv()
        outs[i].wait()
        cp = pltpu.make_async_copy((gq, gk, gv)[i], wb.at[i], wsem.at[i])
        cp.start()
        cp.wait()

    def whole_weight(i):
        return wb[i].reshape(768, 768)

    pump(0)
    pump(1)
    pump(2)
    for cp in cps[2:]:
        cp.wait_recv()
    row = lax.broadcasted_iota(jnp.int32, (192, 768), 0)
    col = lax.broadcasted_iota(jnp.int32, (192, 768), 1)
    total = jnp.zeros((16, 768), F32)
    for i in range(4):
        pick = jnp.where(col == row + 192 * i, 1.0, 0.0).astype(BF)
        total = total + dot(sb[i, :, 0:192], pick)
    vecs[...] = total
    for i in range(4):
        vecs[8 + i : 9 + i, :] = sb[i].astype(F32)[8:9, :]

    def project(i, half, fn):
        w = whole_weight(i)
        for r in range(2):
            fn(256 * r, dot(xb[half, 256 * r : 256 * r + 256, :], w))

    weight(0)

    def put_q(r, v):
        qb[r : r + 256, :] = ((v + vecs[0:1, :]).astype(BF).astype(F32) * 0.125).astype(BF)

    project(0, x, put_q)
    pump(3)
    weight(1)

    def put(dst, half, bias_row):
        def fn(r, v):
            if bias_row is not None:
                v = v + vecs[bias_row : bias_row + 1, :]
            dst[pl.ds(pl.multiple_of(half * 512 + r, 256), 256), :] = v.astype(BF)

        return fn

    project(1, x, put(kb, x, None))
    pump(4)
    weight(2)
    project(2, x, put(vb, x, 1))
    cps[0].wait_recv()
    cps[1].wait_recv()
    project(1, 1 - x, put(kb, 1 - x, None))
    pump(5)
    project(2, 1 - x, put(vb, 1 - x, 1))

    def pair(i):
        v = segb[i].astype(F32)
        r = lax.broadcasted_iota(jnp.int32, (16, 512), 0)
        return jnp.where(r == 0, v, jnp.where(r == 1, 1.0 - v, 0.0)).astype(BF)

    mine = pair(x)
    for i in range(2):
        same = dot(mine, pair(i), TN)
        bias[:, 512 * i : 512 * i + 512] = (same - 1.0) * -far_value
    saves = [
        pltpu.make_async_copy(a, b, osem.at[i])
        for i, (a, b) in enumerate(((xb, x_out), (qb, q_out), (kb, k_out), (vb, v_out)))
    ]
    for cp in saves:
        cp.start()

    def pcp(h):
        return pltpu.make_async_copy(pb.at[h % 2], p_out.at[pl.ds(2 * h, 2)], psem.at[h])

    def attn(h, carry):
        cs = pl.ds(pl.multiple_of(h * 128, 128), 128)

        @pl.when(h >= 2)
        def _():
            pcp(jnp.maximum(h - 2, 0)).wait()

        qq, kk, vv = qb[:, cs], kb[:, cs], vb[:, cs]
        parts = []
        for i in range(2):
            cols = slice(64 * i, 64 * i + 64)
            sc = dot(qq[:, cols], kk[:, cols], NT) + bias[...]
            m = jnp.max(sc, axis=1, keepdims=True)
            e = jnp.exp(sc - m)
            p = (e * (1.0 / jnp.sum(e, axis=1, keepdims=True))).astype(BF)
            pb[h % 2, i] = p
            parts.append(dot(p, vv[:, cols]))
        mixb[:, cs] = jnp.concatenate(parts, axis=1).astype(BF)
        pcp(h).start()
        for i in range(6):

            @pl.when(h == i)
            def _(i=i):
                pump(6 + i)

        return carry

    lax.fori_loop(0, 6, attn, 0)
    mix_cp = pltpu.make_async_copy(mixb, mix_out, osem.at[4])
    mix_cp.start()
    for t in range(12, n + L2):
        pump(t)
    for cp in cps:
        cp.wait_send()
    for k in range(n):
        for cp in ccp[k]:
            cp.wait_send()
            if k >= 3:
                cp.wait_recv()
        for cp in [ycp[k]] + relays[k] + seconds[k]:
            cp.wait_send()
    for cp in outs[3:] + saves + [mix_cp, pcp(4), pcp(5)]:
        cp.wait()


def forward_all(*args):
    sd = jax.ShapeDtypeStruct
    n = 10
    dma = pltpu.SemaphoreType.DMA
    vm = pltpu.VMEM
    square = lambda: sd((4, 192, 768), BF)
    return pl.pallas_call(
        forward_kernel,
        name="forward",
        out_shape=[
            square(), square(), square(), square(), sd((4, 192, 3072), BF), sd((4, 768, 768), BF), sd((16, 768), F32),
            sd((2, 512, 768), BF), sd((512, 768), BF), sd((1024, 768), BF), sd((1024, 768), BF), sd((512, 768), BF),
            sd((H, 512, 1024), BF),
        ],
        in_specs=[ANY] * 9,
        out_specs=[ANY] * 6 + [pl.BlockSpec(memory_space=pltpu.VMEM)] + [ANY] * 6,
        scratch_shapes=[
            vm((4, 192, 768), BF), vm((192, 3072), BF), vm((768, 768), BF), vm((4, 16, 768), BF), vm((2, 512, 768), BF),
            vm((2, 1, 512), jnp.int32), vm((3, 4, 192, 768), BF), vm((512, 768), BF), vm((1024, 768), BF),
            vm((1024, 768), BF), vm((512, 768), BF), vm((2, 2, 512, 1024), BF), vm((512, 1024), F32),
            dma((n,)), dma((n,)), dma((n, 4)), dma((n, 4)), dma((n, 5)), dma((n, 5)), dma((5,)), dma((5,)),
            dma((9, 2)), dma((3,)), dma((5,)), dma((6,)),
        ],
        compiler_params=pltpu.CompilerParams(collective_id=0, has_side_effects=True, vmem_limit_bytes=60 * 2**20),
    )(*args)


NCH = 24
CW = 384
LAGS = (2, 4, 6, 8, 10, 12)


def add_into(dst, src, rows, step=32):
    def body(i, carry):
        r = pl.ds(pl.multiple_of(i * step, step), step)
        dst[r, :] = (dst[r, :].astype(F32) + src[r, :].astype(F32)).astype(BF)
        return carry

    lax.fori_loop(0, rows // step, body, 0)


def backward_kernel(
    gd, gffn_in, gmid_in, slope_in, hid_in, z_in, q_in, k_in, v_in, mix_in, p_in, x_in,
    wd, wu, wo, wq, wk, wv, vecs, vec0,
    o_wd, o_wu, o_wo, o_wv, o_wk, o_wq, vec_out, own_out, gx_out,
    kbuf, gbuf, cbuf, ybuf, xbuf, z0buf, z1buf, fin,
    wt, st, gf, hid, zf, gp, gh, tr, qb, kb, vb, mixb, dk, dv, pb, xt, vbuf, vval,
    ksem, csend, crecv, send, recv, vsend, vrecv, gsend, grecv, osem, lsem, wsem, psem,
):
    me = Place()
    x, y, c, zb, z, s = me.x, me.y, me.c, me.zb, me.z, me.s

    def load(i, src, dst):
        return pltpu.make_async_copy(src, dst, lsem.at[i])

    l_gf, l_gh, l_hid = load(0, gffn_in, gf), load(1, gmid_in, gh), load(2, hid_in, hid)
    l_z, l_q, l_k, l_v = load(3, z_in, zf), load(4, q_in, qb), load(5, k_in, kb), load(6, v_in, vb)
    l_mix, l_x = load(7, mix_in, mixb), load(8, x_in, kb)
    own_cp = load(9, gh, own_out)

    def wdcp(j):
        return pltpu.make_async_copy(wd.at[pl.ds(pl.multiple_of(768 * j, 768), 768), :], wt.at[j % 2], wsem.at[0, j])

    def wucp(j):
        return pltpu.make_async_copy(wu.at[:, pl.ds(pl.multiple_of(768 * j, 768), 768)], wt.at[2 + j % 2], wsem.at[1, j])

    def slcp(j):
        return pltpu.make_async_copy(slope_in.at[:, pl.ds(pl.multiple_of(768 * j, 768), 768)], st.at[j % 2], wsem.at[2, j])

    def pcp(h):
        return pltpu.make_async_copy(p_in.at[pl.ds(2 * h, 2)], pb.at[h % 2], psem.at[h])

    w_o = pltpu.make_async_copy(wo, wt.at[0], wsem.at[3, 0])
    w_k = pltpu.make_async_copy(wk, wt.at[2], wsem.at[3, 1])
    w_v = pltpu.make_async_copy(wv, wt.at[1], wsem.at[3, 2])
    w_q = pltpu.make_async_copy(wq, wt.at[3], wsem.at[3, 3])

    def columns(k):
        return pl.ds(pl.multiple_of(k % 2 * CW, CW), CW)

    def source(k, sh):
        cs = columns(k)
        if isinstance(k, int) and k < 8:
            return gd.at[sh, pl.ds(192 * (k // 2), 192), cs]
        return gbuf.at[k // 2 - 4, sh, :, cs]

    def ccp(k, yy):
        return remote(source(k, 2 * yy + 1 - c), cbuf.at[k, yy], csend.at[k, yy], crecv.at[k, yy], me.core_p)

    def kcp(k, yy):
        return pltpu.make_async_copy(source(k, 2 * yy + c), kbuf.at[k, yy], ksem.at[k, yy])

    def core_start(k):
        for yy in range(2):
            ccp(k, yy).start()

    def bits(k):
        e = (k + 1) % 2
        return e, x + e * (zb - x), zb + e * (x - zb)

    def rows(a, n):
        return pl.ds(pl.multiple_of(a * n, 16), n)

    def ycp(k):
        return remote(cbuf.at[k, 1 - y], ybuf.at[k], send.at[0, k], recv.at[0, k], me.y_p)

    def p1cp(k):
        e, b1, b2 = bits(k)
        p = (z + e * (1 - 2 * zb), s, x + (1 - e) * (1 - 2 * x))
        return remote(ybuf.at[k, rows(1 - b1, 96), :], xbuf.at[k], send.at[1, k], recv.at[1, k], p)

    def second(k):
        e = (k + 1) % 2
        return (z + (1 - e) * (1 - 2 * zb), s, x + e * (1 - 2 * x))

    def p2cp(k):
        e, b1, b2 = bits(k)
        return remote(xbuf.at[k, rows(1 - b2, 48), :], z0buf.at[k], send.at[2, k], recv.at[2, k], second(k))

    def z1cp(k):
        return remote(z0buf.at[k], z1buf.at[k], send.at[3, k], recv.at[3, k], me.z1_p)

    def a2cp(k):
        e, b1, b2 = bits(k)
        r = fin.at[k, rows(2 * b1 + b2, 48), :]
        return remote(r, r, send.at[4, k], recv.at[4, k], second(k))

    def a1cp(k):
        e, b1, b2 = bits(k)
        r = fin.at[k, rows(b1, 96), :]
        p = (z + e * (1 - 2 * zb), s, x + (1 - e) * (1 - 2 * x))
        return remote(r, r, send.at[5, k], recv.at[5, k], p)

    def branch(cond, fn):
        if isinstance(cond, bool):
            if cond:
                fn()
        else:
            pl.when(cond)(fn)

    def out_copy(k, act):
        def wd_out():
            kk = jnp.minimum(k, 7) // 2
            o = o_wd.at[pl.ds(pl.multiple_of(192 * kk, 192), 192), columns(k)]
            act(pltpu.make_async_copy(fin.at[k], o, osem.at[k]))

        def wu_out():
            kk = jnp.clip(k - 10, 0, 7)
            o = o_wu.at[:, pl.ds(pl.multiple_of(CW * kk, CW), CW)]
            act(pltpu.make_async_copy(fin.at[k], o, osem.at[k]))

        branch(k < 8, wd_out)
        both = (10 <= k < 18) if isinstance(k, int) else jnp.logical_and(k >= 10, k < 18)
        branch(both, wu_out)
        for i, o in ((4, o_wo), (9, o_wv), (10, o_wk), (11, o_wq)):
            branch(k // 2 == i, lambda o=o: act(pltpu.make_async_copy(fin.at[k], o.at[:, columns(k)], osem.at[k])))

    def pump(t):
        def at(d, fn):
            k = t - d
            if isinstance(k, int):
                if 0 <= k < NCH:
                    fn(k)
            else:
                pl.when(jnp.logical_and(k >= 0, k < NCH))(lambda: fn(jnp.clip(k, 0, NCH - 1)))

        def core(k):
            for yy in range(2):
                remote(cbuf.at[k, yy], cbuf.at[k, yy], csend.at[k, yy], crecv.at[k, yy], me.core_p).wait_recv()

            def first():
                kk = jnp.minimum(k, 7)
                for yy in range(2):
                    pltpu.make_async_copy(kbuf.at[kk, yy], kbuf.at[kk, yy], ksem.at[kk, yy]).wait()
                    add_into(cbuf.at[k, yy], kbuf.at[kk, yy], 192)

            def later():
                kk = jnp.maximum(k - 8, 0) // 2
                for yy in range(2):
                    add_into(cbuf.at[k, yy], gbuf.at[kk, 2 * yy + c, :, columns(k)], 192)

            branch(k < 8, first)
            branch(k >= 8, later)

        def s_p1(k):
            e, b1, b2 = bits(k)
            p1cp(k).wait_recv()
            add_into(xbuf.at[k], ybuf.at[k, rows(b1, 96), :], 96)
            p2cp(k).start()

        def s_p2(k):
            e, b1, b2 = bits(k)
            p2cp(k).wait_recv()
            add_into(z0buf.at[k], xbuf.at[k, rows(b2, 48), :], 48, 16)
            z1cp(k).start()

        def s_z1(k):
            e, b1, b2 = bits(k)
            z1cp(k).wait_recv()
            fin[k, rows(2 * b1 + b2, 48), :] = (z0buf[k].astype(F32) + z1buf[k].astype(F32)).astype(BF)
            a2cp(k).start()

        def s_a2(k):
            a2cp(k).wait_recv()
            a1cp(k).start()

        def s_a1(k):
            a1cp(k).wait_recv()
            out_copy(k, lambda cp: cp.start())

        def s_y(k):
            ycp(k).wait_recv()
            add_into(ybuf.at[k], cbuf.at[k, y], 192)
            p1cp(k).start()

        at(0, core)
        for lag, stage in zip(LAGS, (s_y, s_p1, s_p2, s_z1, s_a2, s_a1)):
            at(lag, stage)
        at(0, lambda k: ycp(k).start())

    greet([me.core_p, me.y_p, me.x_p, me.z0_p, me.z1_p])

    def first_chunks(ks):
        for k in ks:
            core_start(k)
            for yy in range(2):
                kcp(k, yy).start()

    first_chunks((0, 1))
    l_gf.start()
    wdcp(0).start()
    slcp(0).start()
    l_hid.start()
    pump(0)
    first_chunks((2, 3))
    wucp(0).start()
    l_gh.start()
    pump(1)
    first_chunks((4, 5, 6, 7))
    wdcp(1).start()
    slcp(1).start()
    wucp(1).start()
    vval[0] = vec0[...]

    def transposed(dst, src, n):
        for i in range(n // 256):
            dst[:, 256 * i : 256 * i + 256] = src[256 * i : 256 * i + 256, :].T

    def weight_grad(lhs, rhs, k):
        def body(n, carry):
            cs = pl.ds(pl.multiple_of(n * 256, 256), 256)
            r = dot(lhs[...], rhs[:, cs]).astype(BF)
            for sh in range(4):
                gbuf[k - 4, sh, :, cs] = r[192 * sh : 192 * sh + 192]
            return carry

        lax.fori_loop(0, 3, body, 0)
        core_start(2 * k)
        core_start(2 * k + 1)

    def blocks(n, step, fn, init):
        return lax.fori_loop(0, n // step, lambda i, a: fn(pl.ds(pl.multiple_of(i * step, step), step), a), init)

    zero = jnp.zeros((1, D), F32)
    l_gf.wait()
    l_hid.wait()
    transposed(tr, hid, 512)
    l_gh.wait()

    def ff(j):
        return pl.ds(pl.multiple_of(768 * j, 768), 768)

    def ffn(j, carry):
        wdcp(j).wait()
        slcp(j).wait()
        sl = j % 2

        def up(r, a):
            t = (dot(gf[r, :], wt[sl], NT) * st[sl, r, :].astype(F32)).astype(BF)
            gp[r, ff(j)] = t
            return a + jnp.sum(t.astype(F32), 0, keepdims=True)

        vval[0, pl.ds(8 + j, 1), :] = blocks(512, 256, up, zero)
        wucp(j).wait()

        def down(r, a):
            gh[r, :] = gh[r, :] + dot(gp[r, ff(j)], wt[2 + sl], NT)
            return a

        blocks(512, 256, down, 0)

        @pl.when(j < 2)
        def _():
            jj = jnp.minimum(j + 2, 3)
            wdcp(jj).start()
            slcp(jj).start()
            wucp(jj).start()

        @pl.when(j == 2)
        def _():
            w_o.start()
            w_k.start()

        @pl.when(j == 3)
        def _():
            w_v.start()
            w_q.start()

        for i, cps in enumerate(((l_z, l_mix, l_q), (l_k, pcp(0)), (l_v, pcp(1)))):

            @pl.when(j == i)
            def _(cps=cps):
                for cp in cps:
                    cp.start()

        pump(2 + j)
        return carry

    def up_grad(j):
        weight_grad(tr, gp.at[:, ff(j)], 5 + j)

    lax.fori_loop(0, 4, ffn, 0)

    l_z.wait()
    l_mix.wait()
    gain = vecs[3:4, :]

    def norm(r, a):
        zz = zf[r, :]
        m = jnp.mean(zz, -1, keepdims=True)
        zz = zz - m
        inv = lax.rsqrt(jnp.mean(zz * zz, -1, keepdims=True) + norm_eps)
        n = zz * inv
        e = gh[r, :]
        ge = e * gain
        g = (ge - jnp.mean(ge, -1, keepdims=True) - n * jnp.mean(ge * n, -1, keepdims=True)) * inv
        gh[r, :] = g
        low = g.astype(BF)
        gf[r, :] = low
        total = lambda v: jnp.sum(v, 0, keepdims=True)
        return a[0] + total(low.astype(F32)), a[1] + total(e * n), a[2] + total(e)

    sums = blocks(512, 64, norm, (zero, zero, zero))
    for i in range(3):
        vval[0, 2 + i : 3 + i, :] = sums[i]
    transposed(xt, mixb, 512)
    pump(6)
    weight_grad(xt.at[:, 0:512], gf, 4)
    w_o.wait()

    def mixg(r, a):
        hid[r, :] = dot(gf[r, :], wt[0], NT).astype(BF)
        return a

    blocks(512, 256, mixg, 0)
    l_q.wait()
    l_k.wait()
    l_v.wait()
    pump(7)
    up_grad(0)
    pump(8)

    def attn(h, carry):
        cs = pl.ds(pl.multiple_of(h * 128, 128), 128)
        pcp(h).wait()
        g = hid[:, cs]
        prod = g.astype(F32) * mixb[:, cs].astype(F32)
        gt = g.T
        qt = qb[:, cs].T
        kk = kb[:, cs]
        vv = vb[:, cs]
        dqs, dks, dvs = [], [], []
        for i in range(2):
            cols = slice(64 * i, 64 * i + 64)
            p = pb[h % 2, i]
            delta = jnp.sum(prod[:, cols], axis=1, keepdims=True)
            dp = dot(g[:, cols], vv[:, cols], NT)
            gs = (p.astype(F32) * (dp - delta)).astype(BF)
            dqs.append(dot(gs, kk[:, cols]) * 0.125)
            dks.append(dot(qt[cols, :], gs))
            dvs.append(dot(gt[cols, :], p))
        gf[:, cs] = jnp.concatenate(dqs, axis=1).astype(BF)
        dk[:, cs] = jnp.concatenate(dks, axis=0).T.astype(BF)
        dv[:, cs] = jnp.concatenate(dvs, axis=0).T.astype(BF)

        @pl.when(h < 4)
        def _():
            pcp(jnp.minimum(h + 2, 5)).start()

        pl.when(h % 2 == 1)(lambda: up_grad((h + 1) // 2))
        pump(9 + h)
        return carry

    lax.fori_loop(0, 6, attn, 0)
    w_k.wait()
    w_v.wait()

    def gxcp(i):
        r = pl.ds(32 * i, 32)
        return remote(hid.at[r, :], gx_out.at[r, :], gsend.at[i], grecv.at[i], me.x_p)

    for i in range(2):
        r = pl.ds(pl.multiple_of((1 - x) * 512 + 256 * i, 256), 256)
        hid[256 * i : 256 * i + 256, :] = (dot(dk[r, :], wt[2], NT) + dot(dv[r, :], wt[1], NT)).astype(BF)
    l_x.start()

    def colsum(src):
        return lambda r, a: a + jnp.sum(src[r, :].astype(F32), 0, keepdims=True)

    vval[0, 0:1, :] = blocks(512, 128, colsum(gf), zero)
    vval[0, 1:2, :] = blocks(1024, 128, colsum(dv), zero)
    vps = (me.core_p, me.y_p, me.x_p, me.z0_p, me.z1_p)
    vcps = [remote(vval.at[b], vbuf.at[b], vsend.at[b], vrecv.at[b], vps[b]) for b in range(5)]

    def own(i, carry):
        r = pl.ds(pl.multiple_of(256 * i, 256), 256)
        ro = pl.ds(pl.multiple_of(x * 512 + 256 * i, 256), 256)
        gh[r, :] = gh[r, :] + dot(gf[r, :], wt[3], NT) + dot(dk[ro, :], wt[2], NT) + dot(dv[ro, :], wt[1], NT)
        return carry

    last = NCH + LAGS[-1]
    for t in range(15, last):
        if t == 16:
            l_x.wait()
            transposed(xt, kb, 1024)
            weight_grad(xt, dv, 9)
        if t == 17:
            weight_grad(xt, dk, 10)
        if t == 18:
            weight_grad(xt.at[:, pl.ds(pl.multiple_of(x * 512, 512), 512)], gf, 11)
            w_q.wait()
        if t in (19, 20):
            own(t - 19, 0)
        if t == 21:
            own_cp.start()
        pump(t)
        if 0 <= t - 15 < 16:
            gxcp(t - 15).start()
        b = (t - 19) // 2
        if t == 17:
            vcps[0].start()
        if t % 2 == 1 and 0 <= b < 5:
            vcps[b].wait_recv()
            if b < 4:
                vval[b + 1] = vval[b] + vbuf[b]
                vcps[b + 1].start()
            else:
                vec_out[...] = vval[b] + vbuf[b]

    def finish(k, carry):
        for f in (ycp, p1cp, p2cp, z1cp, a2cp, a1cp):
            f(k).wait_send()
        for yy in range(2):
            remote(cbuf.at[k, yy], cbuf.at[k, yy], csend.at[k, yy], crecv.at[k, yy], me.core_p).wait_send()
        out_copy(k, lambda cp: cp.wait())
        return carry

    lax.fori_loop(0, NCH, finish, 0)
    for cp in vcps:
        cp.wait_send()
    own_cp.wait()
    for i in range(16):
        gxcp(i).wait()


def backward_all(*args):
    sd = jax.ShapeDtypeStruct
    dma = pltpu.SemaphoreType.DMA
    vm = pltpu.VMEM
    vspec = pl.BlockSpec(memory_space=pltpu.VMEM)
    one = lambda: sd((192, 768), BF)
    half = lambda: vm((512, 768), BF)
    full = lambda: vm((1024, 768), BF)
    return pl.pallas_call(
        backward_kernel,
        name="backward",
        out_shape=[
            sd((768, 768), BF), sd((192, 3072), BF), one(), one(), one(), one(),
            sd((16, 768), F32), sd((512, 768), F32), sd((512, 768), BF),
        ],
        in_specs=[ANY] * 18 + [vspec] * 2,
        out_specs=[ANY] * 6 + [vspec, ANY, ANY],
        scratch_shapes=[
            vm((8, 2, 192, CW), BF), vm((8, 4, 192, 768), BF), vm((NCH, 2, 192, CW), BF), vm((NCH, 192, CW), BF),
            vm((NCH, 96, CW), BF), vm((NCH, 48, CW), BF), vm((NCH, 48, CW), BF), vm((NCH, 192, CW), BF),
            vm((4, 768, 768), BF), vm((2, 512, 768), BF), half(), half(), vm((512, 768), F32), vm((512, FF), BF), vm((512, 768), F32),
            vm((768, 512), BF), half(), full(), full(), half(), full(), full(), vm((2, 2, 512, 1024), BF),
            vm((768, 1024), BF), vm((5, 16, 768), F32), vm((5, 16, 768), F32),
            dma((8, 2)), dma((NCH, 2)), dma((NCH, 2)), dma((6, NCH)), dma((6, NCH)), dma((5,)), dma((5,)), dma((16,)), dma((16,)),
            dma((NCH,)), dma((10,)), dma((4, 4)), dma((6,)),
        ],
        compiler_params=pltpu.CompilerParams(collective_id=1, has_side_effects=True, vmem_limit_bytes=63 * 2**20),
    )(*args)


def finish_kernel(wd, wu, wo, wv, wk, wq, own, gx, o_wd, o_wu, o_wo, o_wv, o_wk, o_wq, o_x):
    for a, b in ((wd, o_wd), (wu, o_wu), (wo, o_wo), (wv, o_wv), (wk, o_wk), (wq, o_wq)):
        b[...] = a[...].astype(F32)
    o_x[...] = own[...] + gx[...].astype(F32)


def finish_all(*args):
    steps = 4
    block = lambda a: pl.BlockSpec((a.shape[0] // steps, a.shape[1]), lambda i: (i, 0))
    return pl.pallas_call(
        finish_kernel,
        name="finish",
        grid=(steps,),
        out_shape=[jax.ShapeDtypeStruct(a.shape, F32) for a in args[:7]],
        in_specs=[block(a) for a in args],
        out_specs=[block(a) for a in args[:7]],
    )(*args)


def layer_norm(total_rows, gain_vec, shift_vec):
    row_mean = jnp.mean(total_rows, -1, keepdims=True)
    centred = total_rows - row_mean
    variance = jnp.mean(centred * centred, -1, keepdims=True)
    inv_std = lax.rsqrt(variance + norm_eps)
    normed = centred * inv_std
    return (normed * gain_vec + shift_vec, normed, inv_std)


def norm_grad(grad_in, normed, inv_std, gain_vec):
    scaled = grad_in * gain_vec
    centred_grad = (
        scaled
        - jnp.mean(scaled, -1, keepdims=True)
        - normed * jnp.mean(scaled * normed, -1, keepdims=True)
    )
    return (centred_grad * inv_std, jnp.sum(grad_in * normed, 0), jnp.sum(grad_in, 0))


def shards(
    inputs, segments, cotangent, w_query, b_query, w_key, w_value, b_value, w_out, b_out,
    gain_one, shift_one, w_up, b_up, w_down, b_down, gain_two, shift_two,
):
    x_own = inputs[0]
    singles = (b_query, b_value, b_out, gain_one, shift_one, b_down, gain_two, shift_two, b_up)
    small = sum(jnp.pad(a, (D * i, 16 * D - D * i - a.shape[0])) for i, a in enumerate(singles)).reshape(16, D)
    wq, wk, wv, wo, wu, wd, vecs, xf, q8, keys, values, mixture, probs = forward_all(
        w_query, w_key, w_value, w_out, w_up, w_down, small, x_own, segments
    )
    wq, wk, wv, wo, wu, wd = (w.reshape(-1, w.shape[-1]) for w in (wq, wk, wv, wo, wu, wd))
    bo, g1, s1, bd, g2, s2 = (vecs[i : i + 1] for i in range(2, 8))
    bu = vecs[8:12].reshape(1, FF)
    x_all = xf.reshape(-1, D)

    attn_out = dot(mixture, wo) + bo
    z_one = x_own.astype(F32) + attn_out
    norm_one, _, _ = layer_norm(z_one, g1, s1)
    hidden_low = norm_one.astype(BF)
    pre_act = dot(hidden_low, wu) + bu
    phi = 0.5 * (1.0 + lax.erf(pre_act * (2.0**-0.5)))
    act_low = (pre_act * phi).astype(BF)
    slope = (phi + pre_act * jnp.exp(-0.5 * pre_act * pre_act) * (2 * math.pi) ** -0.5).astype(BF)
    ffn_out = dot(act_low, wd) + bd
    result, normed_two, inv_two = layer_norm(norm_one + ffn_out, g2, s2)

    grad_mid, d_g2, d_s2 = norm_grad(cotangent[0].astype(F32), normed_two, inv_two, g2)
    grad_ffn = grad_mid.astype(BF)
    d_bd = jnp.sum(grad_ffn.astype(F32), 0)
    d_wd = dot(act_low, grad_ffn, TN).astype(BF)
    vec0 = jnp.zeros((16, D), F32)
    for i, a in ((5, d_bd), (6, d_g2), (7, d_s2)):
        vec0 = vec0 + jnp.pad(a.reshape(1, D), ((i, 15 - i), (0, 0)))
    o_wd, o_wu, o_wo, o_wv, o_wk, o_wq, vec, own_part, gx = backward_all(
        d_wd.reshape(4, -1, D), grad_ffn, grad_mid, slope, hidden_low, z_one, q8, keys, values, mixture, probs, x_all,
        wd, wu, wo, wq, wk, wv, vecs, vec0,
    )
    o_wd, o_wu, o_wo, o_wv, o_wk, o_wq, grad_input = finish_all(o_wd, o_wu, o_wo, o_wv, o_wk, o_wq, own_part, gx)
    sh = lax.axis_index("shard")
    mine = lax.dynamic_slice(vec[:8], (0, sh * 192), (8, 192))
    o_bq, o_bv, o_bo, o_g1, o_s1, o_bd, o_g2, o_s2 = (mine[i] for i in range(8))
    o_bu = lax.dynamic_index_in_dim(vec[8:12], sh, 0, False)
    return (
        result.astype(BF)[None], grad_input[None], o_wq, o_bq, o_wk, o_wv, o_bv, o_wo, o_bo,
        o_g1, o_s1, o_wu, o_bu, o_wd, o_bd, o_g2, o_s2,
    )


def make(mesh, body):
    in_specs = (
        P(("rep", "shard"), "seq", None), P(("rep", "shard"), "seq"), P(("rep", "shard"), "seq", None),
        P("shard", None), P("shard"), P("shard", None), P("shard", None), P("shard"), P("shard", None), P("shard"),
        P("shard"), P("shard"), P("shard", None), P("shard"), P("shard", None), P("shard"), P("shard"), P("shard"),
    )
    out_specs = (
        P(("rep", "shard"), "seq", None), P(("rep", "shard"), "seq", None),
        P("shard", None), P("shard"), P("shard", None), P("shard", None), P("shard"), P("shard", None), P("shard"),
        P("shard"), P("shard"), P("shard", None), P("shard"), P("shard", None), P("shard"), P("shard"), P("shard"),
    )
    return jax.shard_map(body, mesh=mesh, in_specs=in_specs, out_specs=out_specs, check_vma=False)


param_names = (
    "w_query",
    "b_query",
    "w_key",
    "w_value",
    "b_value",
    "w_out",
    "b_out",
    "gain_one",
    "shift_one",
    "w_up",
    "b_up",
    "w_down",
    "b_down",
    "gain_two",
    "shift_two",
)


def as_sent(x):
    return jax.tree.map(lambda a: a.astype(jnp.bfloat16) if a.dtype == jnp.float32 else a, x)


def general_layer_norm(total_rows, gain_vec, shift_vec):
    row_mean = jnp.mean(total_rows, -1, keepdims=True)
    centred = total_rows - row_mean
    variance = jnp.mean(centred * centred, -1, keepdims=True)
    inv_std = lax.rsqrt(variance + norm_eps)
    normed = centred * inv_std
    return (normed * gain_vec + shift_vec, normed, inv_std)


def general_norm_grad(grad_in, normed, inv_std, gain_vec):
    scaled = grad_in * gain_vec
    centred_grad = (
        scaled
        - jnp.mean(scaled, -1, keepdims=True)
        - normed * jnp.mean(scaled * normed, -1, keepdims=True)
    )
    return (centred_grad * inv_std, jnp.sum(grad_in * normed, 0), jnp.sum(grad_in, 0))


def inner_rows(left, right):
    return lax.dot_general(
        left, right, (((0,), (0,)), ((), ())), preferred_element_type=jnp.float32
    )


def times_transposed(left, matrix):
    return lax.dot_general(
        left, matrix, (((1,), (1,)), ((), ())), preferred_element_type=jnp.float32
    )


def gelu_exact(value):
    return jax.nn.gelu(value, approximate=False)


def general_shards(
    inputs,
    segments,
    cotangent,
    w_query,
    b_query,
    w_key,
    w_value,
    b_value,
    w_out,
    b_out,
    gain_one,
    shift_one,
    w_up,
    b_up,
    w_down,
    b_down,
    gain_two,
    shift_two,
):
    score_scale = DH ** (-0.5)
    token_rows = inputs[0]
    row_count = token_rows.shape[0]
    own_seg = segments[0].astype(jnp.float32)
    local_params = (
        w_query,
        b_query,
        w_key,
        w_value,
        b_value,
        w_out,
        b_out,
        gain_one,
        shift_one,
        w_up,
        b_up,
        w_down,
        b_down,
        gain_two,
        shift_two,
    )
    gathered = (
        lax.all_gather(local_params[0], "shard", axis=0, tiled=True),
        lax.all_gather(local_params[1], "shard", axis=0, tiled=True),
        lax.all_gather(local_params[2], "shard", axis=0, tiled=True),
        lax.all_gather(local_params[3], "shard", axis=0, tiled=True),
        lax.all_gather(local_params[4], "shard", axis=0, tiled=True),
        lax.all_gather(local_params[5], "shard", axis=0, tiled=True),
        lax.all_gather(local_params[6], "shard", axis=0, tiled=True),
        lax.all_gather(local_params[7], "shard", axis=0, tiled=True),
        lax.all_gather(local_params[8], "shard", axis=0, tiled=True),
        lax.all_gather(local_params[9], "shard", axis=0, tiled=True),
        lax.all_gather(local_params[10], "shard", axis=0, tiled=True),
        lax.all_gather(local_params[11], "shard", axis=0, tiled=True),
        lax.all_gather(local_params[12], "shard", axis=0, tiled=True),
        lax.all_gather(local_params[13], "shard", axis=0, tiled=True),
        lax.all_gather(local_params[14], "shard", axis=0, tiled=True),
    )
    weights = dict(zip(param_names, gathered))

    def vector(name):
        return weights[name].astype(jnp.float32)

    q_wide = jnp.dot(token_rows, weights["w_query"], preferred_element_type=jnp.float32) + vector(
        "b_query"
    )
    queries = q_wide.astype(jnp.bfloat16)
    key_rows = jnp.dot(token_rows, weights["w_key"], preferred_element_type=jnp.float32).astype(
        jnp.bfloat16
    )
    value_rows = (
        jnp.dot(token_rows, weights["w_value"], preferred_element_type=jnp.float32)
        + vector("b_value")
    ).astype(jnp.bfloat16)
    seg_wire = segments[0].astype(jnp.bfloat16)
    query_heads = queries.reshape(row_count, H, DH)
    start_state = (
        jnp.full((H, row_count), far_value, jnp.float32),
        jnp.zeros((H, row_count), jnp.float32),
        jnp.zeros((row_count, H, DH), jnp.float32),
    )
    carried = start_state
    piece_keys = lax.all_gather(key_rows, "seq", axis=0, tiled=True)
    piece_values = lax.all_gather(value_rows, "seq", axis=0, tiled=True)
    piece_seg = lax.all_gather(seg_wire, "seq", axis=0, tiled=True)
    piece_rows = piece_keys.shape[0]
    width_blk = math.gcd(piece_rows, 512)
    blocks = piece_rows // width_blk
    key_blocks = piece_keys.reshape(blocks, width_blk, H, DH)
    value_blocks = piece_values.reshape(blocks, width_blk, H, DH)
    seg_blocks = piece_seg.astype(jnp.float32).reshape(blocks, width_blk)

    def update(fold_state, block_item):
        key_blk, value_blk, seg_blk = block_item
        row_peak, row_total, accumulated = fold_state
        scores = (
            jnp.einsum("rhd,khd->hrk", query_heads, key_blk, preferred_element_type=jnp.float32)
            * score_scale
        )
        allowed = own_seg[:, None] == seg_blk[None, :]
        scores = jnp.where(allowed[None], scores, far_value)
        new_peak = jnp.maximum(row_peak, jnp.max(scores, -1))
        factor = jnp.exp(row_peak - new_peak)
        exp_scores = jnp.exp(scores - new_peak[:, :, None])
        row_total = row_total * factor + jnp.sum(exp_scores, -1)
        block_mix = jnp.einsum(
            "hrk,khd->rhd",
            exp_scores.astype(jnp.bfloat16),
            value_blk,
            preferred_element_type=jnp.float32,
        )
        accumulated = accumulated * jnp.transpose(factor)[:, :, None] + block_mix
        return ((new_peak, row_total, accumulated), None)

    carried, unused = lax.scan(update, carried, (key_blocks, value_blocks, seg_blocks))
    row_peak, row_total, accumulated = carried
    mix_wide = (accumulated / jnp.transpose(row_total)[:, :, None]).reshape(row_count, D)
    mixture = mix_wide.astype(jnp.bfloat16)
    log_total = row_peak + jnp.log(row_total)
    attn_out = jnp.dot(mixture, weights["w_out"], preferred_element_type=jnp.float32) + vector(
        "b_out"
    )
    norm_one, normed_one, inv_one = general_layer_norm(
        token_rows.astype(jnp.float32) + attn_out, vector("gain_one"), vector("shift_one")
    )
    hidden_low = norm_one.astype(jnp.bfloat16)
    pre_act = jnp.dot(hidden_low, weights["w_up"], preferred_element_type=jnp.float32) + vector(
        "b_up"
    )
    activated, gelu_pullback = jax.vjp(gelu_exact, pre_act)
    act_low = activated.astype(jnp.bfloat16)
    ffn_out = jnp.dot(act_low, weights["w_down"], preferred_element_type=jnp.float32) + vector(
        "b_down"
    )
    result, normed_two, inv_two = general_layer_norm(
        norm_one + ffn_out, vector("gain_two"), vector("shift_two")
    )
    regathered = (
        lax.all_gather(local_params[0], "shard", axis=0, tiled=True),
        lax.all_gather(local_params[1], "shard", axis=0, tiled=True),
        lax.all_gather(local_params[2], "shard", axis=0, tiled=True),
        lax.all_gather(local_params[3], "shard", axis=0, tiled=True),
        lax.all_gather(local_params[4], "shard", axis=0, tiled=True),
        lax.all_gather(local_params[5], "shard", axis=0, tiled=True),
        lax.all_gather(local_params[6], "shard", axis=0, tiled=True),
        lax.all_gather(local_params[7], "shard", axis=0, tiled=True),
        lax.all_gather(local_params[8], "shard", axis=0, tiled=True),
        lax.all_gather(local_params[9], "shard", axis=0, tiled=True),
        lax.all_gather(local_params[10], "shard", axis=0, tiled=True),
        lax.all_gather(local_params[11], "shard", axis=0, tiled=True),
        lax.all_gather(local_params[12], "shard", axis=0, tiled=True),
        lax.all_gather(local_params[13], "shard", axis=0, tiled=True),
        lax.all_gather(local_params[14], "shard", axis=0, tiled=True),
    )
    backward_set = dict(zip(param_names, regathered))
    grad_out = cotangent[0].astype(jnp.float32)
    grad_mid, grad_gain_two, grad_shift_two = general_norm_grad(
        grad_out, normed_two, inv_two, backward_set["gain_two"].astype(jnp.float32)
    )
    grad_ffn = grad_mid.astype(jnp.bfloat16)
    grad_b_down = jnp.sum(grad_ffn.astype(jnp.float32), 0)
    grad_w_down = inner_rows(act_low, grad_ffn)
    grad_act = times_transposed(grad_ffn, backward_set["w_down"])
    (grad_pre_wide,) = gelu_pullback(grad_act)
    grad_pre = grad_pre_wide.astype(jnp.bfloat16)
    grad_b_up = jnp.sum(grad_pre.astype(jnp.float32), 0)
    grad_w_up = inner_rows(hidden_low, grad_pre)
    grad_hidden = grad_mid + times_transposed(grad_pre, backward_set["w_up"])
    grad_sum_one, grad_gain_one, grad_shift_one = general_norm_grad(
        grad_hidden, normed_one, inv_one, backward_set["gain_one"].astype(jnp.float32)
    )
    grad_attn = grad_sum_one.astype(jnp.bfloat16)
    grad_b_out = jnp.sum(grad_attn.astype(jnp.float32), 0)
    grad_w_out = inner_rows(mixture, grad_attn)
    grad_mixture = times_transposed(grad_attn, backward_set["w_out"]).astype(jnp.bfloat16)
    grad_mix_heads = grad_mixture.reshape(row_count, H, DH)
    row_delta = jnp.transpose(
        jnp.sum((grad_mixture.astype(jnp.float32) * mix_wide).reshape(row_count, H, DH), -1)
    )
    all_keys, all_values, all_seg = (
        lax.all_gather(key_rows, "seq", axis=0, tiled=True),
        lax.all_gather(value_rows, "seq", axis=0, tiled=True),
        lax.all_gather(seg_wire, "seq", axis=0, tiled=True),
    )
    seq_rows = all_keys.shape[0]
    width_all = math.gcd(seq_rows, 512)
    blocks_all = seq_rows // width_all
    key_blocks = all_keys.reshape(blocks_all, width_all, H, DH)
    value_blocks = all_values.reshape(blocks_all, width_all, H, DH)
    seg_blocks = all_seg.astype(jnp.float32).reshape(blocks_all, width_all)

    def block_grads(key_blk, value_blk, seg_blk):
        scores = (
            jnp.einsum("rhd,khd->hrk", query_heads, key_blk, preferred_element_type=jnp.float32)
            * score_scale
        )
        allowed = own_seg[:, None] == seg_blk[None, :]
        scores = jnp.where(allowed[None], scores, far_value)
        probabilities = jnp.exp(scores - log_total[:, :, None])
        grad_probs = jnp.einsum(
            "rhd,khd->hrk", grad_mix_heads, value_blk, preferred_element_type=jnp.float32
        )
        grad_scores = (probabilities * (grad_probs - row_delta[:, :, None])).astype(jnp.bfloat16)
        return (probabilities, grad_scores)

    def back_update(grad_query_acc, block_item):
        key_blk, value_blk, seg_blk = block_item
        back_grad_query_acc = grad_query_acc
        probabilities, grad_scores = block_grads(key_blk, value_blk, seg_blk)
        grad_value_blk = jnp.einsum(
            "hrk,rhd->khd",
            probabilities.astype(jnp.bfloat16),
            grad_mix_heads,
            preferred_element_type=jnp.float32,
        )
        back_grad_query_acc = (
            back_grad_query_acc
            + jnp.einsum("hrk,khd->rhd", grad_scores, key_blk, preferred_element_type=jnp.float32)
            * score_scale
        )
        grad_key_blk = (
            jnp.einsum("hrk,rhd->khd", grad_scores, query_heads, preferred_element_type=jnp.float32)
            * score_scale
        )
        return (back_grad_query_acc, (grad_key_blk, grad_value_blk))

    grad_query_heads, key_value_grads = lax.scan(
        back_update,
        jnp.zeros((row_count, H, DH), jnp.float32),
        (key_blocks, value_blocks, seg_blocks),
    )
    grad_key_all = key_value_grads[0].reshape(seq_rows, D)
    grad_value_all = key_value_grads[1].reshape(seq_rows, D)
    grad_key_rows, grad_value_rows = (
        lax.psum_scatter(
            grad_key_all.astype(jnp.bfloat16), "seq", scatter_dimension=0, tiled=True
        ).astype(jnp.float32),
        lax.psum_scatter(
            grad_value_all.astype(jnp.bfloat16), "seq", scatter_dimension=0, tiled=True
        ).astype(jnp.float32),
    )
    grad_query_low = grad_query_heads.reshape(row_count, D).astype(jnp.bfloat16)
    grad_key_low = grad_key_rows.astype(jnp.bfloat16)
    grad_value_low = grad_value_rows.astype(jnp.bfloat16)
    grad_w_query = inner_rows(token_rows, grad_query_low)
    grad_b_query = jnp.sum(grad_query_low.astype(jnp.float32), 0)
    grad_w_key = inner_rows(token_rows, grad_key_low)
    grad_w_value = inner_rows(token_rows, grad_value_low)
    grad_b_value = jnp.sum(grad_value_low.astype(jnp.float32), 0)
    grad_input = (
        grad_sum_one
        + times_transposed(grad_query_low, backward_set["w_query"])
        + times_transposed(grad_key_low, backward_set["w_key"])
        + times_transposed(grad_value_low, backward_set["w_value"])
    )
    gradients = (
        grad_w_query,
        grad_b_query,
        grad_w_key,
        grad_w_value,
        grad_b_value,
        grad_w_out,
        grad_b_out,
        grad_gain_one,
        grad_shift_one,
        grad_w_up,
        grad_b_up,
        grad_w_down,
        grad_b_down,
        grad_gain_two,
        grad_shift_two,
    )
    owned_grads = (
        lax.psum_scatter(
            gradients[0].astype(jnp.bfloat16), "shard", scatter_dimension=0, tiled=True
        ).astype(jnp.float32),
        lax.psum_scatter(
            gradients[1].astype(jnp.bfloat16), "shard", scatter_dimension=0, tiled=True
        ).astype(jnp.float32),
        lax.psum_scatter(
            gradients[2].astype(jnp.bfloat16), "shard", scatter_dimension=0, tiled=True
        ).astype(jnp.float32),
        lax.psum_scatter(
            gradients[3].astype(jnp.bfloat16), "shard", scatter_dimension=0, tiled=True
        ).astype(jnp.float32),
        lax.psum_scatter(
            gradients[4].astype(jnp.bfloat16), "shard", scatter_dimension=0, tiled=True
        ).astype(jnp.float32),
        lax.psum_scatter(
            gradients[5].astype(jnp.bfloat16), "shard", scatter_dimension=0, tiled=True
        ).astype(jnp.float32),
        lax.psum_scatter(
            gradients[6].astype(jnp.bfloat16), "shard", scatter_dimension=0, tiled=True
        ).astype(jnp.float32),
        lax.psum_scatter(
            gradients[7].astype(jnp.bfloat16), "shard", scatter_dimension=0, tiled=True
        ).astype(jnp.float32),
        lax.psum_scatter(
            gradients[8].astype(jnp.bfloat16), "shard", scatter_dimension=0, tiled=True
        ).astype(jnp.float32),
        lax.psum_scatter(
            gradients[9].astype(jnp.bfloat16), "shard", scatter_dimension=0, tiled=True
        ).astype(jnp.float32),
        lax.psum_scatter(
            gradients[10].astype(jnp.bfloat16), "shard", scatter_dimension=0, tiled=True
        ).astype(jnp.float32),
        lax.psum_scatter(
            gradients[11].astype(jnp.bfloat16), "shard", scatter_dimension=0, tiled=True
        ).astype(jnp.float32),
        lax.psum_scatter(
            gradients[12].astype(jnp.bfloat16), "shard", scatter_dimension=0, tiled=True
        ).astype(jnp.float32),
        lax.psum_scatter(
            gradients[13].astype(jnp.bfloat16), "shard", scatter_dimension=0, tiled=True
        ).astype(jnp.float32),
        lax.psum_scatter(
            gradients[14].astype(jnp.bfloat16), "shard", scatter_dimension=0, tiled=True
        ).astype(jnp.float32),
    )
    owned_grads = jax.tree.map(
        lambda part: part.astype(jnp.float32), lax.psum(as_sent(tuple(owned_grads)), ("rep", "seq"))
    )
    return (result.astype(jnp.bfloat16)[None], grad_input[None]) + tuple(owned_grads)


def solution(mesh):
    if dict(mesh.shape) == {"rep": 4, "shard": 4, "seq": 2}:
        return make(mesh, shards)
    return make(mesh, general_shards)
```

```python
import functools
import math

import jax
import jax.numpy as jnp
from jax import lax
from jax.experimental import pallas as pl
from jax.experimental.pallas import tpu as pltpu
from jax.sharding import PartitionSpec as P

D = 768
H = 12
DH = 64
FF = 3072
MESH = pl.DeviceIdType.MESH
F32 = jnp.float32
BF = jnp.bfloat16
ANY = pl.BlockSpec(memory_space=pl.ANY)

norm_eps = 1e-05
far_value = -1e30


class Place:
    def __init__(self):
        self.z = lax.axis_index("rep")
        self.s = lax.axis_index("shard")
        self.x = lax.axis_index("seq")
        self.y = self.s // 2
        self.c = self.s % 2
        self.zb = self.z % 2
        self.zh = self.z // 2
        zb, zh, x, y, c = self.zb, self.zh, self.x, self.y, self.c
        self.core_p = (self.z, 2 * y + 1 - c, x)
        self.y_p = (self.z, 2 * (1 - y) + c, x)
        self.diag_p = (self.z, 2 * (1 - y) + 1 - c, x)
        self.x_p = (self.z, self.s, 1 - x)
        self.z0_p = (2 * zh + 1 - zb, self.s, x)
        self.z1_p = (2 * (1 - zh) + zb, self.s, x)


def greet(partners):
    barrier = pltpu.get_barrier_semaphore()
    for p in partners:
        pl.semaphore_signal(barrier, inc=1, device_id=p, device_id_type=MESH)
    pl.semaphore_wait(barrier, len(partners))


def remote(src, dst, ssem, rsem, dev):
    return pltpu.make_async_remote_copy(
        src_ref=src, dst_ref=dst, send_sem=ssem, recv_sem=rsem, device_id=dev, device_id_type=MESH
    )


NT = (((1,), (1,)), ((), ()))
TN = (((0,), (0,)), ((), ()))


def dot(a, b, dims=(((1,), (0,)), ((), ()))):
    return lax.dot_general(a, b, dims, preferred_element_type=F32)


L1, L2, YD = 2, 4, 3
KINDS = (1, 2, 2, 2, 2, 1, 1, 0)


def forward_kernel(
    wq, wk, wv, wo, wu, wd, small, x_in, seg_in,
    gq, gk, gv, go, gu, gd, vecs, x_out, q_out, k_out, v_out, mix_out, p_out,
    b768, bu, bd, sb, xb, segb, wb, qb, kb, vb, mixb, pb, bias,
    ysend, yrecv, fsend, frecv, csend, crecv, ssend, srecv, lsem, wsem, osem, psem,
):
    me = Place()
    s, x, zb = me.s, me.x, me.zb
    so = 2 * (1 - me.y) + me.c

    chunks = [(own, full, 0, 192, 0, 768, KINDS[0]) for own, full in ((wq, gq), (wk, gk), (wv, gv))]
    chunks.append((wo, go, 0, 192, 0, 768, KINDS[1]))
    for j in range(2):
        chunks.append((wu, gu, 0, 192, 1536 * j, 1536, KINDS[2 + j]))
    for j in range(4):
        chunks.append((wd, gd, 192 * j, 192, 0, 768, KINDS[4 + j]))
    n = len(chunks)

    greet([me.core_p, me.y_p, me.diag_p, me.x_p, me.z0_p])

    ycp, relays, seconds, lasts, ccp = [], [], [], [], []
    for k, (own, full, r0, rows, c0, cols, kind) in enumerate(chunks):
        cs = pl.ds(c0, cols)
        whole = pl.ds(r0, rows)

        def part(i, h):
            return pl.ds(pl.multiple_of(r0 + i * h, 16), h)

        def relay(i, r, c, dev):
            return remote(full.at[so, r, c], full.at[so, r, c], fsend.at[k, i], frecv.at[k, i], dev)

        def across(i, r):
            return remote(full.at[so, r, cs], full.at[so, r, cs], csend.at[k, i], crecv.at[k, i], me.core_p)

        cc = [remote(own.at[whole, cs], full.at[s, whole, cs], csend.at[k, 0], crecv.at[k, 0], me.core_p)]
        if kind == 2:
            h = rows // 4
            rm, rx = part(2 * x + zb, h), part(2 * (1 - x) + zb, h)
            rz, rd = part(2 * x + 1 - zb, h), part(2 * (1 - x) + 1 - zb, h)
            h0, h1 = pl.ds(c0, cols // 2), pl.ds(c0 + cols // 2, cols // 2)
            relays.append([relay(0, rm, cs, me.x_p), relay(1, rm, cs, me.z0_p)])
            seconds.append([relay(3, rx, h1, me.z0_p), relay(2, rz, h0, me.x_p)])
            cc += [across(1 + i, r) for i, r in enumerate((rm, rx, rz, rd))]
        elif kind == 1:
            h = rows // 2
            rm, rz = part(zb, h), part(1 - zb, h)
            relays.append([relay(1, rm, cs, me.z0_p)])
            seconds.append([])
            cc += [across(1 + i, r) for i, r in enumerate((rm, rz))]
        else:
            rm = whole
            relays.append([])
            seconds.append([])
            cc.append(across(1, rm))
        ycp.append(remote(own.at[rm, cs], full.at[s, rm, cs], ysend.at[k], yrecv.at[k], me.y_p))
        ccp.append(cc)

    def pump(t):
        if t < n:
            ycp[t].wait_recv()
            for cp in relays[t]:
                cp.start()
            ccp[t][1].start()
        k = t - L1
        if 0 <= k < n:
            for i, cp in enumerate(relays[k]):
                cp.wait_recv()
                ccp[k][2 + i].start()
                if seconds[k]:
                    seconds[k][i].start()
        k = t - L2
        if 0 <= k < n and seconds[k]:
            for cp in seconds[k]:
                cp.wait_recv()
            ccp[k][4].start()
        if t + 3 < n:
            ccp[t + 3][0].start()
        if t + YD < n:
            ycp[t + YD].start()

    cps = [
        remote(x_in, xb.at[x], ssend.at[0], srecv.at[0], me.x_p),
        remote(seg_in, segb.at[x], ssend.at[1], srecv.at[1], me.x_p),
        remote(small, sb.at[s], ssend.at[2], srecv.at[2], me.core_p),
        remote(small, sb.at[s], ssend.at[3], srecv.at[3], me.y_p),
        remote(small, sb.at[s], ssend.at[4], srecv.at[4], me.diag_p),
    ]
    ycp[0].start()
    cps[0].start()
    for k in range(1, YD):
        ycp[k].start()
    for cp in cps[1:]:
        cp.start()
    for k in range(3):
        ccp[k][0].start()
    owns = [(wq, b768.at[0], gq), (wk, b768.at[1], gk), (wv, b768.at[2], gv), (wo, b768.at[3], go), (wu, bu, gu), (wd, bd, gd)]
    ins = [pltpu.make_async_copy(a, b, lsem.at[i, 0]) for i, (a, b, _) in enumerate(owns)]
    outs = [pltpu.make_async_copy(b, f.at[s], lsem.at[i, 1]) for i, (_, b, f) in enumerate(owns)]
    more = [(x_in, xb.at[x]), (seg_in, segb.at[x]), (small, sb.at[s])]
    more = [pltpu.make_async_copy(a, b, lsem.at[6 + i, 0]) for i, (a, b) in enumerate(more)]
    for cp in more + ins[:3]:
        cp.start()
    for a, b in zip(ins[:3], outs[:3]):
        a.wait()
        b.start()
    for cp in more:
        cp.wait()

    def weight(i):
        for cp in ccp[i]:
            cp.wait_recv()
        outs[i].wait()
        cp = pltpu.make_async_copy((gq, gk, gv)[i], wb.at[i], wsem.at[i])
        cp.start()
        cp.wait()

    def whole_weight(i):
        return wb[i].reshape(768, 768)

    pump(0)
    pump(1)
    for cp in ins[3:]:
        cp.start()
    pump(2)
    for a, b in zip(ins[3:], outs[3:]):
        a.wait()
        b.start()
    for cp in cps[2:]:
        cp.wait_recv()
    row = lax.broadcasted_iota(jnp.int32, (192, 768), 0)
    col = lax.broadcasted_iota(jnp.int32, (192, 768), 1)
    total = jnp.zeros((16, 768), F32)
    for i in range(4):
        pick = jnp.where(col == row + 192 * i, 1.0, 0.0).astype(BF)
        total = total + dot(sb[i, :, 0:192], pick)
    vecs[...] = total
    for i in range(4):
        vecs[8 + i : 9 + i, :] = sb[i].astype(F32)[8:9, :]

    def project(i, half, fn):
        w = whole_weight(i)
        for r in range(2):
            fn(256 * r, dot(xb[half, 256 * r : 256 * r + 256, :], w))

    weight(0)

    def put_q(r, v):
        qb[r : r + 256, :] = ((v + vecs[0:1, :]).astype(BF).astype(F32) * 0.125).astype(BF)

    project(0, x, put_q)
    pump(3)
    weight(1)

    def put(dst, half, bias_row):
        def fn(r, v):
            if bias_row is not None:
                v = v + vecs[bias_row : bias_row + 1, :]
            dst[pl.ds(pl.multiple_of(half * 512 + r, 256), 256), :] = v.astype(BF)

        return fn

    project(1, x, put(kb, x, None))
    pump(4)
    weight(2)
    project(2, x, put(vb, x, 1))
    cps[0].wait_recv()
    cps[1].wait_recv()
    project(1, 1 - x, put(kb, 1 - x, None))
    pump(5)
    project(2, 1 - x, put(vb, 1 - x, 1))

    def pair(i):
        v = segb[i].astype(F32)
        r = lax.broadcasted_iota(jnp.int32, (16, 512), 0)
        return jnp.where(r == 0, v, jnp.where(r == 1, 1.0 - v, 0.0)).astype(BF)

    mine = pair(x)
    for i in range(2):
        same = dot(mine, pair(i), TN)
        bias[:, 512 * i : 512 * i + 512] = (same - 1.0) * -far_value
    saves = [
        pltpu.make_async_copy(a, b, osem.at[i])
        for i, (a, b) in enumerate(((xb, x_out), (qb, q_out), (kb, k_out), (vb, v_out)))
    ]
    for cp in saves:
        cp.start()

    def pcp(h):
        return pltpu.make_async_copy(pb.at[h % 2], p_out.at[pl.ds(2 * h, 2)], psem.at[h])

    def attn(h, carry):
        cs = pl.ds(pl.multiple_of(h * 128, 128), 128)

        @pl.when(h >= 2)
        def _():
            pcp(jnp.maximum(h - 2, 0)).wait()

        qq, kk, vv = qb[:, cs], kb[:, cs], vb[:, cs]
        parts = []
        for i in range(2):
            cols = slice(64 * i, 64 * i + 64)
            sc = dot(qq[:, cols], kk[:, cols], NT) + bias[...]
            m = jnp.max(sc, axis=1, keepdims=True)
            e = jnp.exp(sc - m)
            p = (e * (1.0 / jnp.sum(e, axis=1, keepdims=True))).astype(BF)
            pb[h % 2, i] = p
            parts.append(dot(p, vv[:, cols]))
        mixb[:, cs] = jnp.concatenate(parts, axis=1).astype(BF)
        pcp(h).start()
        for i in range(6):

            @pl.when(h == i)
            def _(i=i):
                pump(6 + i)

        return carry

    lax.fori_loop(0, 6, attn, 0)
    mix_cp = pltpu.make_async_copy(mixb, mix_out, osem.at[4])
    mix_cp.start()
    for t in range(12, n + L2):
        pump(t)
    for cp in cps:
        cp.wait_send()
    for k in range(n):
        for cp in ccp[k]:
            cp.wait_send()
            if k >= 3:
                cp.wait_recv()
        for cp in [ycp[k]] + relays[k] + seconds[k]:
            cp.wait_send()
    for cp in outs[3:] + saves + [mix_cp, pcp(4), pcp(5)]:
        cp.wait()


def forward_all(*args):
    sd = jax.ShapeDtypeStruct
    n = 10
    dma = pltpu.SemaphoreType.DMA
    vm = pltpu.VMEM
    square = lambda: sd((4, 192, 768), BF)
    return pl.pallas_call(
        forward_kernel,
        name="forward",
        out_shape=[
            square(), square(), square(), square(), sd((4, 192, 3072), BF), sd((4, 768, 768), BF), sd((16, 768), F32),
            sd((2, 512, 768), BF), sd((512, 768), BF), sd((1024, 768), BF), sd((1024, 768), BF), sd((512, 768), BF),
            sd((H, 512, 1024), BF),
        ],
        in_specs=[ANY] * 9,
        out_specs=[ANY] * 6 + [pl.BlockSpec(memory_space=pltpu.VMEM)] + [ANY] * 6,
        scratch_shapes=[
            vm((4, 192, 768), BF), vm((192, 3072), BF), vm((768, 768), BF), vm((4, 16, 768), BF), vm((2, 512, 768), BF),
            vm((2, 1, 512), jnp.int32), vm((3, 4, 192, 768), BF), vm((512, 768), BF), vm((1024, 768), BF),
            vm((1024, 768), BF), vm((512, 768), BF), vm((2, 2, 512, 1024), BF), vm((512, 1024), F32),
            dma((n,)), dma((n,)), dma((n, 4)), dma((n, 4)), dma((n, 5)), dma((n, 5)), dma((5,)), dma((5,)),
            dma((9, 2)), dma((3,)), dma((5,)), dma((6,)),
        ],
        compiler_params=pltpu.CompilerParams(collective_id=0, has_side_effects=True, vmem_limit_bytes=60 * 2**20),
    )(*args)


NCH = 24
CW = 384
LAGS = (2, 4, 6, 8, 10, 12)


def add_into(dst, src, rows, step=32):
    def body(i, carry):
        r = pl.ds(pl.multiple_of(i * step, step), step)
        dst[r, :] = (dst[r, :].astype(F32) + src[r, :].astype(F32)).astype(BF)
        return carry

    lax.fori_loop(0, rows // step, body, 0)


def backward_kernel(
    gd, gffn_in, gmid_in, slope_in, hid_in, z_in, q_in, k_in, v_in, mix_in, p_in, x_in,
    wd, wu, wo, wq, wk, wv, vecs, vec0,
    o_wd, o_wu, o_wo, o_wv, o_wk, o_wq, vec_out, own_out, gx_out,
    kbuf, gbuf, cbuf, ybuf, xbuf, z0buf, z1buf, fin,
    wt, st, gf, hid, zf, gp, gh, tr, qb, kb, vb, mixb, dk, dv, pb, xt, vbuf, vval,
    ksem, csend, crecv, send, recv, vsend, vrecv, gsend, grecv, osem, lsem, wsem, psem,
):
    me = Place()
    x, y, c, zb, z, s = me.x, me.y, me.c, me.zb, me.z, me.s

    def load(i, src, dst):
        return pltpu.make_async_copy(src, dst, lsem.at[i])

    l_gf, l_gh, l_hid = load(0, gffn_in, gf), load(1, gmid_in, gh), load(2, hid_in, hid)
    l_z, l_q, l_k, l_v = load(3, z_in, zf), load(4, q_in, qb), load(5, k_in, kb), load(6, v_in, vb)
    l_mix, l_x = load(7, mix_in, mixb), load(8, x_in, kb)
    own_cp = load(9, gh, own_out)

    def wdcp(j):
        return pltpu.make_async_copy(wd.at[pl.ds(pl.multiple_of(768 * j, 768), 768), :], wt.at[j % 2], wsem.at[0, j])

    def wucp(j):
        return pltpu.make_async_copy(wu.at[:, pl.ds(pl.multiple_of(768 * j, 768), 768)], wt.at[2 + j % 2], wsem.at[1, j])

    def slcp(j):
        return pltpu.make_async_copy(slope_in.at[:, pl.ds(pl.multiple_of(768 * j, 768), 768)], st.at[j % 2], wsem.at[2, j])

    def pcp(h):
        return pltpu.make_async_copy(p_in.at[pl.ds(2 * h, 2)], pb.at[h % 2], psem.at[h])

    w_o = pltpu.make_async_copy(wo, wt.at[0], wsem.at[3, 0])
    w_k = pltpu.make_async_copy(wk, wt.at[2], wsem.at[3, 1])
    w_v = pltpu.make_async_copy(wv, wt.at[1], wsem.at[3, 2])
    w_q = pltpu.make_async_copy(wq, wt.at[3], wsem.at[3, 3])

    def columns(k):
        return pl.ds(pl.multiple_of(k % 2 * CW, CW), CW)

    def source(k, sh):
        cs = columns(k)
        if isinstance(k, int) and k < 8:
            return gd.at[sh, pl.ds(192 * (k // 2), 192), cs]
        return gbuf.at[k // 2 - 4, sh, :, cs]

    def ccp(k, yy):
        return remote(source(k, 2 * yy + 1 - c), cbuf.at[k, yy], csend.at[k, yy], crecv.at[k, yy], me.core_p)

    def kcp(k, yy):
        return pltpu.make_async_copy(source(k, 2 * yy + c), kbuf.at[k, yy], ksem.at[k, yy])

    def core_start(k):
        for yy in range(2):
            ccp(k, yy).start()

    def bits(k):
        e = (k + 1) % 2
        return e, x + e * (zb - x), zb + e * (x - zb)

    def rows(a, n):
        return pl.ds(pl.multiple_of(a * n, 16), n)

    def ycp(k):
        return remote(cbuf.at[k, 1 - y], ybuf.at[k], send.at[0, k], recv.at[0, k], me.y_p)

    def p1cp(k):
        e, b1, b2 = bits(k)
        p = (z + e * (1 - 2 * zb), s, x + (1 - e) * (1 - 2 * x))
        return remote(ybuf.at[k, rows(1 - b1, 96), :], xbuf.at[k], send.at[1, k], recv.at[1, k], p)

    def second(k):
        e = (k + 1) % 2
        return (z + (1 - e) * (1 - 2 * zb), s, x + e * (1 - 2 * x))

    def p2cp(k):
        e, b1, b2 = bits(k)
        return remote(xbuf.at[k, rows(1 - b2, 48), :], z0buf.at[k], send.at[2, k], recv.at[2, k], second(k))

    def z1cp(k):
        return remote(z0buf.at[k], z1buf.at[k], send.at[3, k], recv.at[3, k], me.z1_p)

    def a2cp(k):
        e, b1, b2 = bits(k)
        r = fin.at[k, rows(2 * b1 + b2, 48), :]
        return remote(r, r, send.at[4, k], recv.at[4, k], second(k))

    def a1cp(k):
        e, b1, b2 = bits(k)
        r = fin.at[k, rows(b1, 96), :]
        p = (z + e * (1 - 2 * zb), s, x + (1 - e) * (1 - 2 * x))
        return remote(r, r, send.at[5, k], recv.at[5, k], p)

    def branch(cond, fn):
        if isinstance(cond, bool):
            if cond:
                fn()
        else:
            pl.when(cond)(fn)

    def out_copy(k, act):
        def wd_out():
            kk = jnp.minimum(k, 7) // 2
            o = o_wd.at[pl.ds(pl.multiple_of(192 * kk, 192), 192), columns(k)]
            act(pltpu.make_async_copy(fin.at[k], o, osem.at[k]))

        def wu_out():
            kk = jnp.clip(k - 10, 0, 7)
            o = o_wu.at[:, pl.ds(pl.multiple_of(CW * kk, CW), CW)]
            act(pltpu.make_async_copy(fin.at[k], o, osem.at[k]))

        branch(k < 8, wd_out)
        both = (10 <= k < 18) if isinstance(k, int) else jnp.logical_and(k >= 10, k < 18)
        branch(both, wu_out)
        for i, o in ((4, o_wo), (9, o_wv), (10, o_wk), (11, o_wq)):
            branch(k // 2 == i, lambda o=o: act(pltpu.make_async_copy(fin.at[k], o.at[:, columns(k)], osem.at[k])))

    def pump(t):
        def at(d, fn):
            k = t - d
            if isinstance(k, int):
                if 0 <= k < NCH:
                    fn(k)
            else:
                pl.when(jnp.logical_and(k >= 0, k < NCH))(lambda: fn(jnp.clip(k, 0, NCH - 1)))

        def core(k):
            for yy in range(2):
                remote(cbuf.at[k, yy], cbuf.at[k, yy], csend.at[k, yy], crecv.at[k, yy], me.core_p).wait_recv()

            def first():
                kk = jnp.minimum(k, 7)
                for yy in range(2):
                    pltpu.make_async_copy(kbuf.at[kk, yy], kbuf.at[kk, yy], ksem.at[kk, yy]).wait()
                    add_into(cbuf.at[k, yy], kbuf.at[kk, yy], 192)

            def later():
                kk = jnp.maximum(k - 8, 0) // 2
                for yy in range(2):
                    add_into(cbuf.at[k, yy], gbuf.at[kk, 2 * yy + c, :, columns(k)], 192)

            branch(k < 8, first)
            branch(k >= 8, later)

        def s_p1(k):
            e, b1, b2 = bits(k)
            p1cp(k).wait_recv()
            add_into(xbuf.at[k], ybuf.at[k, rows(b1, 96), :], 96)
            p2cp(k).start()

        def s_p2(k):
            e, b1, b2 = bits(k)
            p2cp(k).wait_recv()
            add_into(z0buf.at[k], xbuf.at[k, rows(b2, 48), :], 48, 16)
            z1cp(k).start()

        def s_z1(k):
            e, b1, b2 = bits(k)
            z1cp(k).wait_recv()
            fin[k, rows(2 * b1 + b2, 48), :] = (z0buf[k].astype(F32) + z1buf[k].astype(F32)).astype(BF)
            a2cp(k).start()

        def s_a2(k):
            a2cp(k).wait_recv()
            a1cp(k).start()

        def s_a1(k):
            a1cp(k).wait_recv()
            out_copy(k, lambda cp: cp.start())

        def s_y(k):
            ycp(k).wait_recv()
            add_into(ybuf.at[k], cbuf.at[k, y], 192)
            p1cp(k).start()

        at(0, core)
        for lag, stage in zip(LAGS, (s_y, s_p1, s_p2, s_z1, s_a2, s_a1)):
            at(lag, stage)
        at(0, lambda k: ycp(k).start())

    greet([me.core_p, me.y_p, me.x_p, me.z0_p, me.z1_p])

    def first_chunks(ks):
        for k in ks:
            core_start(k)
            for yy in range(2):
                kcp(k, yy).start()

    first_chunks((0, 1))
    l_gf.start()
    wdcp(0).start()
    slcp(0).start()
    l_hid.start()
    pump(0)
    first_chunks((2, 3))
    wucp(0).start()
    l_gh.start()
    pump(1)
    first_chunks((4, 5, 6, 7))
    wdcp(1).start()
    slcp(1).start()
    wucp(1).start()
    vval[0] = vec0[...]

    def transposed(dst, src, n):
        for i in range(n // 256):
            dst[:, 256 * i : 256 * i + 256] = src[256 * i : 256 * i + 256, :].T

    def weight_grad(lhs, rhs, k):
        def body(n, carry):
            cs = pl.ds(pl.multiple_of(n * 256, 256), 256)
            r = dot(lhs[...], rhs[:, cs]).astype(BF)
            for sh in range(4):
                gbuf[k - 4, sh, :, cs] = r[192 * sh : 192 * sh + 192]
            return carry

        lax.fori_loop(0, 3, body, 0)
        core_start(2 * k)
        core_start(2 * k + 1)

    def blocks(n, step, fn, init):
        return lax.fori_loop(0, n // step, lambda i, a: fn(pl.ds(pl.multiple_of(i * step, step), step), a), init)

    zero = jnp.zeros((1, D), F32)
    l_gf.wait()
    l_hid.wait()
    transposed(tr, hid, 512)
    l_gh.wait()

    def ff(j):
        return pl.ds(pl.multiple_of(768 * j, 768), 768)

    def ffn(j, carry):
        wdcp(j).wait()
        slcp(j).wait()
        sl = j % 2

        def up(r, a):
            t = (dot(gf[r, :], wt[sl], NT) * st[sl, r, :].astype(F32)).astype(BF)
            gp[r, ff(j)] = t
            return a + jnp.sum(t.astype(F32), 0, keepdims=True)

        vval[0, pl.ds(8 + j, 1), :] = blocks(512, 256, up, zero)
        wucp(j).wait()

        def down(r, a):
            gh[r, :] = gh[r, :] + dot(gp[r, ff(j)], wt[2 + sl], NT)
            return a

        blocks(512, 256, down, 0)

        @pl.when(j < 2)
        def _():
            jj = jnp.minimum(j + 2, 3)
            wdcp(jj).start()
            slcp(jj).start()
            wucp(jj).start()

        @pl.when(j == 2)
        def _():
            w_o.start()
            w_k.start()

        @pl.when(j == 3)
        def _():
            w_v.start()
            w_q.start()

        for i, cps in enumerate(((l_z, l_mix, l_q), (l_k, pcp(0)), (l_v, pcp(1)))):

            @pl.when(j == i)
            def _(cps=cps):
                for cp in cps:
                    cp.start()

        pump(2 + j)
        return carry

    def up_grad(j):
        weight_grad(tr, gp.at[:, ff(j)], 5 + j)

    lax.fori_loop(0, 4, ffn, 0)

    l_z.wait()
    l_mix.wait()
    gain = vecs[3:4, :]

    def norm(r, a):
        zz = zf[r, :]
        m = jnp.mean(zz, -1, keepdims=True)
        zz = zz - m
        inv = lax.rsqrt(jnp.mean(zz * zz, -1, keepdims=True) + norm_eps)
        n = zz * inv
        e = gh[r, :]
        ge = e * gain
        g = (ge - jnp.mean(ge, -1, keepdims=True) - n * jnp.mean(ge * n, -1, keepdims=True)) * inv
        gh[r, :] = g
        low = g.astype(BF)
        gf[r, :] = low
        total = lambda v: jnp.sum(v, 0, keepdims=True)
        return a[0] + total(low.astype(F32)), a[1] + total(e * n), a[2] + total(e)

    sums = blocks(512, 64, norm, (zero, zero, zero))
    for i in range(3):
        vval[0, 2 + i : 3 + i, :] = sums[i]
    transposed(xt, mixb, 512)
    pump(6)
    weight_grad(xt.at[:, 0:512], gf, 4)
    w_o.wait()

    def mixg(r, a):
        hid[r, :] = dot(gf[r, :], wt[0], NT).astype(BF)
        return a

    blocks(512, 256, mixg, 0)
    l_q.wait()
    l_k.wait()
    l_v.wait()
    pump(7)
    up_grad(0)
    pump(8)

    def attn(h, carry):
        cs = pl.ds(pl.multiple_of(h * 128, 128), 128)
        pcp(h).wait()
        g = hid[:, cs]
        prod = g.astype(F32) * mixb[:, cs].astype(F32)
        gt = g.T
        qt = qb[:, cs].T
        kk = kb[:, cs]
        vv = vb[:, cs]
        dqs, dks, dvs = [], [], []
        for i in range(2):
            cols = slice(64 * i, 64 * i + 64)
            p = pb[h % 2, i]
            delta = jnp.sum(prod[:, cols], axis=1, keepdims=True)
            dp = dot(g[:, cols], vv[:, cols], NT)
            gs = (p.astype(F32) * (dp - delta)).astype(BF)
            dqs.append(dot(gs, kk[:, cols]) * 0.125)
            dks.append(dot(qt[cols, :], gs))
            dvs.append(dot(gt[cols, :], p))
        gf[:, cs] = jnp.concatenate(dqs, axis=1).astype(BF)
        dk[:, cs] = jnp.concatenate(dks, axis=0).T.astype(BF)
        dv[:, cs] = jnp.concatenate(dvs, axis=0).T.astype(BF)

        @pl.when(h < 4)
        def _():
            pcp(jnp.minimum(h + 2, 5)).start()

        pl.when(h % 2 == 1)(lambda: up_grad((h + 1) // 2))
        pump(9 + h)
        return carry

    lax.fori_loop(0, 6, attn, 0)
    w_k.wait()
    w_v.wait()

    def gxcp(i):
        r = pl.ds(32 * i, 32)
        return remote(hid.at[r, :], gx_out.at[r, :], gsend.at[i], grecv.at[i], me.x_p)

    for i in range(2):
        r = pl.ds(pl.multiple_of((1 - x) * 512 + 256 * i, 256), 256)
        hid[256 * i : 256 * i + 256, :] = (dot(dk[r, :], wt[2], NT) + dot(dv[r, :], wt[1], NT)).astype(BF)
    l_x.start()

    def colsum(src):
        return lambda r, a: a + jnp.sum(src[r, :].astype(F32), 0, keepdims=True)

    vval[0, 0:1, :] = blocks(512, 128, colsum(gf), zero)
    vval[0, 1:2, :] = blocks(1024, 128, colsum(dv), zero)
    vps = (me.core_p, me.y_p, me.x_p, me.z0_p, me.z1_p)
    vcps = [remote(vval.at[b], vbuf.at[b], vsend.at[b], vrecv.at[b], vps[b]) for b in range(5)]

    def own(i, carry):
        r = pl.ds(pl.multiple_of(256 * i, 256), 256)
        ro = pl.ds(pl.multiple_of(x * 512 + 256 * i, 256), 256)
        gh[r, :] = gh[r, :] + dot(gf[r, :], wt[3], NT) + dot(dk[ro, :], wt[2], NT) + dot(dv[ro, :], wt[1], NT)
        return carry

    last = NCH + LAGS[-1]
    for t in range(15, last):
        if t == 16:
            l_x.wait()
            transposed(xt, kb, 1024)
            weight_grad(xt, dv, 9)
        if t == 17:
            weight_grad(xt, dk, 10)
        if t == 18:
            weight_grad(xt.at[:, pl.ds(pl.multiple_of(x * 512, 512), 512)], gf, 11)
            w_q.wait()
        if t in (19, 20):
            own(t - 19, 0)
        if t == 21:
            own_cp.start()
        pump(t)
        if 0 <= t - 15 < 16:
            gxcp(t - 15).start()
        b = (t - 19) // 2
        if t == 17:
            vcps[0].start()
        if t % 2 == 1 and 0 <= b < 5:
            vcps[b].wait_recv()
            if b < 4:
                vval[b + 1] = vval[b] + vbuf[b]
                vcps[b + 1].start()
            else:
                vec_out[...] = vval[b] + vbuf[b]

    def finish(k, carry):
        for f in (ycp, p1cp, p2cp, z1cp, a2cp, a1cp):
            f(k).wait_send()
        for yy in range(2):
            remote(cbuf.at[k, yy], cbuf.at[k, yy], csend.at[k, yy], crecv.at[k, yy], me.core_p).wait_send()
        out_copy(k, lambda cp: cp.wait())
        return carry

    lax.fori_loop(0, NCH, finish, 0)
    for cp in vcps:
        cp.wait_send()
    own_cp.wait()
    for i in range(16):
        gxcp(i).wait()


def backward_all(*args):
    sd = jax.ShapeDtypeStruct
    dma = pltpu.SemaphoreType.DMA
    vm = pltpu.VMEM
    vspec = pl.BlockSpec(memory_space=pltpu.VMEM)
    one = lambda: sd((192, 768), BF)
    half = lambda: vm((512, 768), BF)
    full = lambda: vm((1024, 768), BF)
    return pl.pallas_call(
        backward_kernel,
        name="backward",
        out_shape=[
            sd((768, 768), BF), sd((192, 3072), BF), one(), one(), one(), one(),
            sd((16, 768), F32), sd((512, 768), F32), sd((512, 768), BF),
        ],
        in_specs=[ANY] * 18 + [vspec] * 2,
        out_specs=[ANY] * 6 + [vspec, ANY, ANY],
        scratch_shapes=[
            vm((8, 2, 192, CW), BF), vm((8, 4, 192, 768), BF), vm((NCH, 2, 192, CW), BF), vm((NCH, 192, CW), BF),
            vm((NCH, 96, CW), BF), vm((NCH, 48, CW), BF), vm((NCH, 48, CW), BF), vm((NCH, 192, CW), BF),
            vm((4, 768, 768), BF), vm((2, 512, 768), BF), half(), half(), vm((512, 768), F32), vm((512, FF), BF), vm((512, 768), F32),
            vm((768, 512), BF), half(), full(), full(), half(), full(), full(), vm((2, 2, 512, 1024), BF),
            vm((768, 1024), BF), vm((5, 16, 768), F32), vm((5, 16, 768), F32),
            dma((8, 2)), dma((NCH, 2)), dma((NCH, 2)), dma((6, NCH)), dma((6, NCH)), dma((5,)), dma((5,)), dma((16,)), dma((16,)),
            dma((NCH,)), dma((10,)), dma((4, 4)), dma((6,)),
        ],
        compiler_params=pltpu.CompilerParams(collective_id=1, has_side_effects=True, vmem_limit_bytes=63 * 2**20),
    )(*args)


def finish_kernel(wd, wu, wo, wv, wk, wq, own, gx, o_wd, o_wu, o_wo, o_wv, o_wk, o_wq, o_x):
    for a, b in ((wd, o_wd), (wu, o_wu), (wo, o_wo), (wv, o_wv), (wk, o_wk), (wq, o_wq)):
        b[...] = a[...].astype(F32)
    o_x[...] = own[...] + gx[...].astype(F32)


def finish_all(*args):
    steps = 4
    block = lambda a: pl.BlockSpec((a.shape[0] // steps, a.shape[1]), lambda i: (i, 0))
    return pl.pallas_call(
        finish_kernel,
        name="finish",
        grid=(steps,),
        out_shape=[jax.ShapeDtypeStruct(a.shape, F32) for a in args[:7]],
        in_specs=[block(a) for a in args],
        out_specs=[block(a) for a in args[:7]],
    )(*args)


def layer_norm(total_rows, gain_vec, shift_vec):
    row_mean = jnp.mean(total_rows, -1, keepdims=True)
    centred = total_rows - row_mean
    variance = jnp.mean(centred * centred, -1, keepdims=True)
    inv_std = lax.rsqrt(variance + norm_eps)
    normed = centred * inv_std
    return (normed * gain_vec + shift_vec, normed, inv_std)


def norm_grad(grad_in, normed, inv_std, gain_vec):
    scaled = grad_in * gain_vec
    centred_grad = (
        scaled
        - jnp.mean(scaled, -1, keepdims=True)
        - normed * jnp.mean(scaled * normed, -1, keepdims=True)
    )
    return (centred_grad * inv_std, jnp.sum(grad_in * normed, 0), jnp.sum(grad_in, 0))


def shards(
    inputs, segments, cotangent, w_query, b_query, w_key, w_value, b_value, w_out, b_out,
    gain_one, shift_one, w_up, b_up, w_down, b_down, gain_two, shift_two,
):
    x_own = inputs[0]
    singles = (b_query, b_value, b_out, gain_one, shift_one, b_down, gain_two, shift_two, b_up)
    small = sum(jnp.pad(a, (D * i, 16 * D - D * i - a.shape[0])) for i, a in enumerate(singles)).reshape(16, D)
    wq, wk, wv, wo, wu, wd, vecs, xf, q8, keys, values, mixture, probs = forward_all(
        w_query, w_key, w_value, w_out, w_up, w_down, small, x_own, segments
    )
    wq, wk, wv, wo, wu, wd = (w.reshape(-1, w.shape[-1]) for w in (wq, wk, wv, wo, wu, wd))
    bo, g1, s1, bd, g2, s2 = (vecs[i : i + 1] for i in range(2, 8))
    bu = vecs[8:12].reshape(1, FF)
    x_all = xf.reshape(-1, D)

    attn_out = dot(mixture, wo) + bo
    z_one = x_own.astype(F32) + attn_out
    norm_one, _, _ = layer_norm(z_one, g1, s1)
    hidden_low = norm_one.astype(BF)
    pre_act = dot(hidden_low, wu) + bu
    phi = 0.5 * (1.0 + lax.erf(pre_act * (2.0**-0.5)))
    act_low = (pre_act * phi).astype(BF)
    slope = (phi + pre_act * jnp.exp(-0.5 * pre_act * pre_act) * (2 * math.pi) ** -0.5).astype(BF)
    ffn_out = dot(act_low, wd) + bd
    result, normed_two, inv_two = layer_norm(norm_one + ffn_out, g2, s2)

    grad_mid, d_g2, d_s2 = norm_grad(cotangent[0].astype(F32), normed_two, inv_two, g2)
    grad_ffn = grad_mid.astype(BF)
    d_bd = jnp.sum(grad_ffn.astype(F32), 0)
    d_wd = dot(act_low, grad_ffn, TN).astype(BF)
    vec0 = jnp.zeros((16, D), F32)
    for i, a in ((5, d_bd), (6, d_g2), (7, d_s2)):
        vec0 = vec0 + jnp.pad(a.reshape(1, D), ((i, 15 - i), (0, 0)))
    o_wd, o_wu, o_wo, o_wv, o_wk, o_wq, vec, own_part, gx = backward_all(
        d_wd.reshape(4, -1, D), grad_ffn, grad_mid, slope, hidden_low, z_one, q8, keys, values, mixture, probs, x_all,
        wd, wu, wo, wq, wk, wv, vecs, vec0,
    )
    o_wd, o_wu, o_wo, o_wv, o_wk, o_wq, grad_input = finish_all(o_wd, o_wu, o_wo, o_wv, o_wk, o_wq, own_part, gx)
    sh = lax.axis_index("shard")
    mine = lax.dynamic_slice(vec[:8], (0, sh * 192), (8, 192))
    o_bq, o_bv, o_bo, o_g1, o_s1, o_bd, o_g2, o_s2 = (mine[i] for i in range(8))
    o_bu = lax.dynamic_index_in_dim(vec[8:12], sh, 0, False)
    return (
        result.astype(BF)[None], grad_input[None], o_wq, o_bq, o_wk, o_wv, o_bv, o_wo, o_bo,
        o_g1, o_s1, o_wu, o_bu, o_wd, o_bd, o_g2, o_s2,
    )


def make(mesh, body):
    in_specs = (
        P(("rep", "shard"), "seq", None), P(("rep", "shard"), "seq"), P(("rep", "shard"), "seq", None),
        P("shard", None), P("shard"), P("shard", None), P("shard", None), P("shard"), P("shard", None), P("shard"),
        P("shard"), P("shard"), P("shard", None), P("shard"), P("shard", None), P("shard"), P("shard"), P("shard"),
    )
    out_specs = (
        P(("rep", "shard"), "seq", None), P(("rep", "shard"), "seq", None),
        P("shard", None), P("shard"), P("shard", None), P("shard", None), P("shard"), P("shard", None), P("shard"),
        P("shard"), P("shard"), P("shard", None), P("shard"), P("shard", None), P("shard"), P("shard"), P("shard"),
    )
    return jax.shard_map(body, mesh=mesh, in_specs=in_specs, out_specs=out_specs, check_vma=False)


param_names = (
    "w_query",
    "b_query",
    "w_key",
    "w_value",
    "b_value",
    "w_out",
    "b_out",
    "gain_one",
    "shift_one",
    "w_up",
    "b_up",
    "w_down",
    "b_down",
    "gain_two",
    "shift_two",
)


def as_sent(x):
    return jax.tree.map(lambda a: a.astype(jnp.bfloat16) if a.dtype == jnp.float32 else a, x)


def general_layer_norm(total_rows, gain_vec, shift_vec):
    row_mean = jnp.mean(total_rows, -1, keepdims=True)
    centred = total_rows - row_mean
    variance = jnp.mean(centred * centred, -1, keepdims=True)
    inv_std = lax.rsqrt(variance + norm_eps)
    normed = centred * inv_std
    return (normed * gain_vec + shift_vec, normed, inv_std)


def general_norm_grad(grad_in, normed, inv_std, gain_vec):
    scaled = grad_in * gain_vec
    centred_grad = (
        scaled
        - jnp.mean(scaled, -1, keepdims=True)
        - normed * jnp.mean(scaled * normed, -1, keepdims=True)
    )
    return (centred_grad * inv_std, jnp.sum(grad_in * normed, 0), jnp.sum(grad_in, 0))


def inner_rows(left, right):
    return lax.dot_general(
        left, right, (((0,), (0,)), ((), ())), preferred_element_type=jnp.float32
    )


def times_transposed(left, matrix):
    return lax.dot_general(
        left, matrix, (((1,), (1,)), ((), ())), preferred_element_type=jnp.float32
    )


def gelu_exact(value):
    return jax.nn.gelu(value, approximate=False)


def general_shards(
    inputs,
    segments,
    cotangent,
    w_query,
    b_query,
    w_key,
    w_value,
    b_value,
    w_out,
    b_out,
    gain_one,
    shift_one,
    w_up,
    b_up,
    w_down,
    b_down,
    gain_two,
    shift_two,
):
    score_scale = DH ** (-0.5)
    token_rows = inputs[0]
    row_count = token_rows.shape[0]
    own_seg = segments[0].astype(jnp.float32)
    local_params = (
        w_query,
        b_query,
        w_key,
        w_value,
        b_value,
        w_out,
        b_out,
        gain_one,
        shift_one,
        w_up,
        b_up,
        w_down,
        b_down,
        gain_two,
        shift_two,
    )
    gathered = (
        lax.all_gather(local_params[0], "shard", axis=0, tiled=True),
        lax.all_gather(local_params[1], "shard", axis=0, tiled=True),
        lax.all_gather(local_params[2], "shard", axis=0, tiled=True),
        lax.all_gather(local_params[3], "shard", axis=0, tiled=True),
        lax.all_gather(local_params[4], "shard", axis=0, tiled=True),
        lax.all_gather(local_params[5], "shard", axis=0, tiled=True),
        lax.all_gather(local_params[6], "shard", axis=0, tiled=True),
        lax.all_gather(local_params[7], "shard", axis=0, tiled=True),
        lax.all_gather(local_params[8], "shard", axis=0, tiled=True),
        lax.all_gather(local_params[9], "shard", axis=0, tiled=True),
        lax.all_gather(local_params[10], "shard", axis=0, tiled=True),
        lax.all_gather(local_params[11], "shard", axis=0, tiled=True),
        lax.all_gather(local_params[12], "shard", axis=0, tiled=True),
        lax.all_gather(local_params[13], "shard", axis=0, tiled=True),
        lax.all_gather(local_params[14], "shard", axis=0, tiled=True),
    )
    weights = dict(zip(param_names, gathered))

    def vector(name):
        return weights[name].astype(jnp.float32)

    q_wide = jnp.dot(token_rows, weights["w_query"], preferred_element_type=jnp.float32) + vector(
        "b_query"
    )
    queries = q_wide.astype(jnp.bfloat16)
    key_rows = jnp.dot(token_rows, weights["w_key"], preferred_element_type=jnp.float32).astype(
        jnp.bfloat16
    )
    value_rows = (
        jnp.dot(token_rows, weights["w_value"], preferred_element_type=jnp.float32)
        + vector("b_value")
    ).astype(jnp.bfloat16)
    seg_wire = segments[0].astype(jnp.bfloat16)
    query_heads = queries.reshape(row_count, H, DH)
    start_state = (
        jnp.full((H, row_count), far_value, jnp.float32),
        jnp.zeros((H, row_count), jnp.float32),
        jnp.zeros((row_count, H, DH), jnp.float32),
    )
    carried = start_state
    piece_keys = lax.all_gather(key_rows, "seq", axis=0, tiled=True)
    piece_values = lax.all_gather(value_rows, "seq", axis=0, tiled=True)
    piece_seg = lax.all_gather(seg_wire, "seq", axis=0, tiled=True)
    piece_rows = piece_keys.shape[0]
    width_blk = math.gcd(piece_rows, 512)
    blocks = piece_rows // width_blk
    key_blocks = piece_keys.reshape(blocks, width_blk, H, DH)
    value_blocks = piece_values.reshape(blocks, width_blk, H, DH)
    seg_blocks = piece_seg.astype(jnp.float32).reshape(blocks, width_blk)

    def update(fold_state, block_item):
        key_blk, value_blk, seg_blk = block_item
        row_peak, row_total, accumulated = fold_state
        scores = (
            jnp.einsum("rhd,khd->hrk", query_heads, key_blk, preferred_element_type=jnp.float32)
            * score_scale
        )
        allowed = own_seg[:, None] == seg_blk[None, :]
        scores = jnp.where(allowed[None], scores, far_value)
        new_peak = jnp.maximum(row_peak, jnp.max(scores, -1))
        factor = jnp.exp(row_peak - new_peak)
        exp_scores = jnp.exp(scores - new_peak[:, :, None])
        row_total = row_total * factor + jnp.sum(exp_scores, -1)
        block_mix = jnp.einsum(
            "hrk,khd->rhd",
            exp_scores.astype(jnp.bfloat16),
            value_blk,
            preferred_element_type=jnp.float32,
        )
        accumulated = accumulated * jnp.transpose(factor)[:, :, None] + block_mix
        return ((new_peak, row_total, accumulated), None)

    carried, unused = lax.scan(update, carried, (key_blocks, value_blocks, seg_blocks))
    row_peak, row_total, accumulated = carried
    mix_wide = (accumulated / jnp.transpose(row_total)[:, :, None]).reshape(row_count, D)
    mixture = mix_wide.astype(jnp.bfloat16)
    log_total = row_peak + jnp.log(row_total)
    attn_out = jnp.dot(mixture, weights["w_out"], preferred_element_type=jnp.float32) + vector(
        "b_out"
    )
    norm_one, normed_one, inv_one = general_layer_norm(
        token_rows.astype(jnp.float32) + attn_out, vector("gain_one"), vector("shift_one")
    )
    hidden_low = norm_one.astype(jnp.bfloat16)
    pre_act = jnp.dot(hidden_low, weights["w_up"], preferred_element_type=jnp.float32) + vector(
        "b_up"
    )
    activated, gelu_pullback = jax.vjp(gelu_exact, pre_act)
    act_low = activated.astype(jnp.bfloat16)
    ffn_out = jnp.dot(act_low, weights["w_down"], preferred_element_type=jnp.float32) + vector(
        "b_down"
    )
    result, normed_two, inv_two = general_layer_norm(
        norm_one + ffn_out, vector("gain_two"), vector("shift_two")
    )
    regathered = (
        lax.all_gather(local_params[0], "shard", axis=0, tiled=True),
        lax.all_gather(local_params[1], "shard", axis=0, tiled=True),
        lax.all_gather(local_params[2], "shard", axis=0, tiled=True),
        lax.all_gather(local_params[3], "shard", axis=0, tiled=True),
        lax.all_gather(local_params[4], "shard", axis=0, tiled=True),
        lax.all_gather(local_params[5], "shard", axis=0, tiled=True),
        lax.all_gather(local_params[6], "shard", axis=0, tiled=True),
        lax.all_gather(local_params[7], "shard", axis=0, tiled=True),
        lax.all_gather(local_params[8], "shard", axis=0, tiled=True),
        lax.all_gather(local_params[9], "shard", axis=0, tiled=True),
        lax.all_gather(local_params[10], "shard", axis=0, tiled=True),
        lax.all_gather(local_params[11], "shard", axis=0, tiled=True),
        lax.all_gather(local_params[12], "shard", axis=0, tiled=True),
        lax.all_gather(local_params[13], "shard", axis=0, tiled=True),
        lax.all_gather(local_params[14], "shard", axis=0, tiled=True),
    )
    backward_set = dict(zip(param_names, regathered))
    grad_out = cotangent[0].astype(jnp.float32)
    grad_mid, grad_gain_two, grad_shift_two = general_norm_grad(
        grad_out, normed_two, inv_two, backward_set["gain_two"].astype(jnp.float32)
    )
    grad_ffn = grad_mid.astype(jnp.bfloat16)
    grad_b_down = jnp.sum(grad_ffn.astype(jnp.float32), 0)
    grad_w_down = inner_rows(act_low, grad_ffn)
    grad_act = times_transposed(grad_ffn, backward_set["w_down"])
    (grad_pre_wide,) = gelu_pullback(grad_act)
    grad_pre = grad_pre_wide.astype(jnp.bfloat16)
    grad_b_up = jnp.sum(grad_pre.astype(jnp.float32), 0)
    grad_w_up = inner_rows(hidden_low, grad_pre)
    grad_hidden = grad_mid + times_transposed(grad_pre, backward_set["w_up"])
    grad_sum_one, grad_gain_one, grad_shift_one = general_norm_grad(
        grad_hidden, normed_one, inv_one, backward_set["gain_one"].astype(jnp.float32)
    )
    grad_attn = grad_sum_one.astype(jnp.bfloat16)
    grad_b_out = jnp.sum(grad_attn.astype(jnp.float32), 0)
    grad_w_out = inner_rows(mixture, grad_attn)
    grad_mixture = times_transposed(grad_attn, backward_set["w_out"]).astype(jnp.bfloat16)
    grad_mix_heads = grad_mixture.reshape(row_count, H, DH)
    row_delta = jnp.transpose(
        jnp.sum((grad_mixture.astype(jnp.float32) * mix_wide).reshape(row_count, H, DH), -1)
    )
    all_keys, all_values, all_seg = (
        lax.all_gather(key_rows, "seq", axis=0, tiled=True),
        lax.all_gather(value_rows, "seq", axis=0, tiled=True),
        lax.all_gather(seg_wire, "seq", axis=0, tiled=True),
    )
    seq_rows = all_keys.shape[0]
    width_all = math.gcd(seq_rows, 512)
    blocks_all = seq_rows // width_all
    key_blocks = all_keys.reshape(blocks_all, width_all, H, DH)
    value_blocks = all_values.reshape(blocks_all, width_all, H, DH)
    seg_blocks = all_seg.astype(jnp.float32).reshape(blocks_all, width_all)

    def block_grads(key_blk, value_blk, seg_blk):
        scores = (
            jnp.einsum("rhd,khd->hrk", query_heads, key_blk, preferred_element_type=jnp.float32)
            * score_scale
        )
        allowed = own_seg[:, None] == seg_blk[None, :]
        scores = jnp.where(allowed[None], scores, far_value)
        probabilities = jnp.exp(scores - log_total[:, :, None])
        grad_probs = jnp.einsum(
            "rhd,khd->hrk", grad_mix_heads, value_blk, preferred_element_type=jnp.float32
        )
        grad_scores = (probabilities * (grad_probs - row_delta[:, :, None])).astype(jnp.bfloat16)
        return (probabilities, grad_scores)

    def back_update(grad_query_acc, block_item):
        key_blk, value_blk, seg_blk = block_item
        back_grad_query_acc = grad_query_acc
        probabilities, grad_scores = block_grads(key_blk, value_blk, seg_blk)
        grad_value_blk = jnp.einsum(
            "hrk,rhd->khd",
            probabilities.astype(jnp.bfloat16),
            grad_mix_heads,
            preferred_element_type=jnp.float32,
        )
        back_grad_query_acc = (
            back_grad_query_acc
            + jnp.einsum("hrk,khd->rhd", grad_scores, key_blk, preferred_element_type=jnp.float32)
            * score_scale
        )
        grad_key_blk = (
            jnp.einsum("hrk,rhd->khd", grad_scores, query_heads, preferred_element_type=jnp.float32)
            * score_scale
        )
        return (back_grad_query_acc, (grad_key_blk, grad_value_blk))

    grad_query_heads, key_value_grads = lax.scan(
        back_update,
        jnp.zeros((row_count, H, DH), jnp.float32),
        (key_blocks, value_blocks, seg_blocks),
    )
    grad_key_all = key_value_grads[0].reshape(seq_rows, D)
    grad_value_all = key_value_grads[1].reshape(seq_rows, D)
    grad_key_rows, grad_value_rows = (
        lax.psum_scatter(
            grad_key_all.astype(jnp.bfloat16), "seq", scatter_dimension=0, tiled=True
        ).astype(jnp.float32),
        lax.psum_scatter(
            grad_value_all.astype(jnp.bfloat16), "seq", scatter_dimension=0, tiled=True
        ).astype(jnp.float32),
    )
    grad_query_low = grad_query_heads.reshape(row_count, D).astype(jnp.bfloat16)
    grad_key_low = grad_key_rows.astype(jnp.bfloat16)
    grad_value_low = grad_value_rows.astype(jnp.bfloat16)
    grad_w_query = inner_rows(token_rows, grad_query_low)
    grad_b_query = jnp.sum(grad_query_low.astype(jnp.float32), 0)
    grad_w_key = inner_rows(token_rows, grad_key_low)
    grad_w_value = inner_rows(token_rows, grad_value_low)
    grad_b_value = jnp.sum(grad_value_low.astype(jnp.float32), 0)
    grad_input = (
        grad_sum_one
        + times_transposed(grad_query_low, backward_set["w_query"])
        + times_transposed(grad_key_low, backward_set["w_key"])
        + times_transposed(grad_value_low, backward_set["w_value"])
    )
    gradients = (
        grad_w_query,
        grad_b_query,
        grad_w_key,
        grad_w_value,
        grad_b_value,
        grad_w_out,
        grad_b_out,
        grad_gain_one,
        grad_shift_one,
        grad_w_up,
        grad_b_up,
        grad_w_down,
        grad_b_down,
        grad_gain_two,
        grad_shift_two,
    )
    owned_grads = (
        lax.psum_scatter(
            gradients[0].astype(jnp.bfloat16), "shard", scatter_dimension=0, tiled=True
        ).astype(jnp.float32),
        lax.psum_scatter(
            gradients[1].astype(jnp.bfloat16), "shard", scatter_dimension=0, tiled=True
        ).astype(jnp.float32),
        lax.psum_scatter(
            gradients[2].astype(jnp.bfloat16), "shard", scatter_dimension=0, tiled=True
        ).astype(jnp.float32),
        lax.psum_scatter(
            gradients[3].astype(jnp.bfloat16), "shard", scatter_dimension=0, tiled=True
        ).astype(jnp.float32),
        lax.psum_scatter(
            gradients[4].astype(jnp.bfloat16), "shard", scatter_dimension=0, tiled=True
        ).astype(jnp.float32),
        lax.psum_scatter(
            gradients[5].astype(jnp.bfloat16), "shard", scatter_dimension=0, tiled=True
        ).astype(jnp.float32),
        lax.psum_scatter(
            gradients[6].astype(jnp.bfloat16), "shard", scatter_dimension=0, tiled=True
        ).astype(jnp.float32),
        lax.psum_scatter(
            gradients[7].astype(jnp.bfloat16), "shard", scatter_dimension=0, tiled=True
        ).astype(jnp.float32),
        lax.psum_scatter(
            gradients[8].astype(jnp.bfloat16), "shard", scatter_dimension=0, tiled=True
        ).astype(jnp.float32),
        lax.psum_scatter(
            gradients[9].astype(jnp.bfloat16), "shard", scatter_dimension=0, tiled=True
        ).astype(jnp.float32),
        lax.psum_scatter(
            gradients[10].astype(jnp.bfloat16), "shard", scatter_dimension=0, tiled=True
        ).astype(jnp.float32),
        lax.psum_scatter(
            gradients[11].astype(jnp.bfloat16), "shard", scatter_dimension=0, tiled=True
        ).astype(jnp.float32),
        lax.psum_scatter(
            gradients[12].astype(jnp.bfloat16), "shard", scatter_dimension=0, tiled=True
        ).astype(jnp.float32),
        lax.psum_scatter(
            gradients[13].astype(jnp.bfloat16), "shard", scatter_dimension=0, tiled=True
        ).astype(jnp.float32),
        lax.psum_scatter(
            gradients[14].astype(jnp.bfloat16), "shard", scatter_dimension=0, tiled=True
        ).astype(jnp.float32),
    )
    owned_grads = jax.tree.map(
        lambda part: part.astype(jnp.float32), lax.psum(as_sent(tuple(owned_grads)), ("rep", "seq"))
    )
    return (result.astype(jnp.bfloat16)[None], grad_input[None]) + tuple(owned_grads)


def solution(mesh):
    if dict(mesh.shape) == {"rep": 4, "shard": 4, "seq": 2}:
        return make(mesh, shards)
    return make(mesh, general_shards)
```

```python
import functools
import math

import jax
import jax.numpy as jnp
from jax import lax
from jax.experimental import pallas as pl
from jax.experimental.pallas import tpu as pltpu
from jax.sharding import PartitionSpec as P

D = 768
H = 12
DH = 64
FF = 3072
MESH = pl.DeviceIdType.MESH
F32 = jnp.float32
BF = jnp.bfloat16
ANY = pl.BlockSpec(memory_space=pl.ANY)

norm_eps = 1e-05
far_value = -1e30


class Place:
    def __init__(self):
        self.z = lax.axis_index("rep")
        self.s = lax.axis_index("shard")
        self.x = lax.axis_index("seq")
        self.y = self.s // 2
        self.c = self.s % 2
        self.zb = self.z % 2
        self.zh = self.z // 2
        zb, zh, x, y, c = self.zb, self.zh, self.x, self.y, self.c
        self.core_p = (self.z, 2 * y + 1 - c, x)
        self.y_p = (self.z, 2 * (1 - y) + c, x)
        self.diag_p = (self.z, 2 * (1 - y) + 1 - c, x)
        self.x_p = (self.z, self.s, 1 - x)
        self.z0_p = (2 * zh + 1 - zb, self.s, x)
        self.z1_p = (2 * (1 - zh) + zb, self.s, x)


def greet(partners):
    barrier = pltpu.get_barrier_semaphore()
    for p in partners:
        pl.semaphore_signal(barrier, inc=1, device_id=p, device_id_type=MESH)
    pl.semaphore_wait(barrier, len(partners))


def remote(src, dst, ssem, rsem, dev):
    return pltpu.make_async_remote_copy(
        src_ref=src, dst_ref=dst, send_sem=ssem, recv_sem=rsem, device_id=dev, device_id_type=MESH
    )


NT = (((1,), (1,)), ((), ()))
TN = (((0,), (0,)), ((), ()))


def dot(a, b, dims=(((1,), (0,)), ((), ()))):
    return lax.dot_general(a, b, dims, preferred_element_type=F32)


L1, L2, YD = 2, 4, 3
KINDS = (1, 1, 2, 2, 2, 2, 1, 0)


def forward_kernel(
    wq, wk, wv, wo, wu, wd, small, x_in, seg_in,
    gq, gk, gv, go, gu, gd, vecs, x_out, q_out, k_out, v_out, mix_out, p_out,
    b768, bu, bd, sb, xb, segb, wb, qb, kb, vb, mixb, pb, bias,
    ysend, yrecv, fsend, frecv, csend, crecv, ssend, srecv, lsem, wsem, osem, psem,
):
    me = Place()
    s, x, zb = me.s, me.x, me.zb
    so = 2 * (1 - me.y) + me.c

    chunks = [(own, full, 0, 192, 0, 768, KINDS[0]) for own, full in ((wq, gq), (wk, gk), (wv, gv))]
    chunks.append((wo, go, 0, 192, 0, 768, KINDS[1]))
    for j in range(2):
        chunks.append((wu, gu, 0, 192, 1536 * j, 1536, KINDS[2 + j]))
    for j in range(4):
        chunks.append((wd, gd, 192 * j, 192, 0, 768, KINDS[4 + j]))
    n = len(chunks)

    greet([me.core_p, me.y_p, me.diag_p, me.x_p, me.z0_p])

    ycp, relays, seconds, lasts, ccp = [], [], [], [], []
    for k, (own, full, r0, rows, c0, cols, kind) in enumerate(chunks):
        cs = pl.ds(c0, cols)
        whole = pl.ds(r0, rows)

        def part(i, h):
            return pl.ds(pl.multiple_of(r0 + i * h, 16), h)

        def relay(i, r, c, dev):
            return remote(full.at[so, r, c], full.at[so, r, c], fsend.at[k, i], frecv.at[k, i], dev)

        def across(i, r):
            return remote(full.at[so, r, cs], full.at[so, r, cs], csend.at[k, i], crecv.at[k, i], me.core_p)

        cc = [remote(own.at[whole, cs], full.at[s, whole, cs], csend.at[k, 0], crecv.at[k, 0], me.core_p)]
        if kind == 2:
            h = rows // 4
            rm, rx = part(2 * x + zb, h), part(2 * (1 - x) + zb, h)
            rz, rd = part(2 * x + 1 - zb, h), part(2 * (1 - x) + 1 - zb, h)
            h0, h1 = pl.ds(c0, cols // 2), pl.ds(c0 + cols // 2, cols // 2)
            relays.append([relay(0, rm, cs, me.x_p), relay(1, rm, cs, me.z0_p)])
            seconds.append([relay(3, rx, h1, me.z0_p), relay(2, rz, h0, me.x_p)])
            cc += [across(1 + i, r) for i, r in enumerate((rm, rx, rz, rd))]
        elif kind == 1:
            h = rows // 2
            rm, rz = part(zb, h), part(1 - zb, h)
            relays.append([relay(1, rm, cs, me.z0_p)])
            seconds.append([])
            cc += [across(1 + i, r) for i, r in enumerate((rm, rz))]
        else:
            rm = whole
            relays.append([])
            seconds.append([])
            cc.append(across(1, rm))
        ycp.append(remote(own.at[rm, cs], full.at[s, rm, cs], ysend.at[k], yrecv.at[k], me.y_p))
        ccp.append(cc)

    def pump(t):
        if t < n:
            ycp[t].wait_recv()
            for cp in relays[t]:
                cp.start()
            ccp[t][1].start()
        k = t - L1
        if 0 <= k < n:
            for i, cp in enumerate(relays[k]):
                cp.wait_recv()
                ccp[k][2 + i].start()
                if seconds[k]:
                    seconds[k][i].start()
        k = t - L2
        if 0 <= k < n and seconds[k]:
            for cp in seconds[k]:
                cp.wait_recv()
            ccp[k][4].start()
        if t + 3 < n:
            ccp[t + 3][0].start()
        if t + YD < n:
            ycp[t + YD].start()

    cps = [
        remote(x_in, xb.at[x], ssend.at[0], srecv.at[0], me.x_p),
        remote(seg_in, segb.at[x], ssend.at[1], srecv.at[1], me.x_p),
        remote(small, sb.at[s], ssend.at[2], srecv.at[2], me.core_p),
        remote(small, sb.at[s], ssend.at[3], srecv.at[3], me.y_p),
        remote(small, sb.at[s], ssend.at[4], srecv.at[4], me.diag_p),
    ]
    ycp[0].start()
    cps[0].start()
    for k in range(1, YD):
        ycp[k].start()
    for cp in cps[1:]:
        cp.start()
    for k in range(3):
        ccp[k][0].start()
    owns = [(wq, b768.at[0], gq), (wk, b768.at[1], gk), (wv, b768.at[2], gv), (wo, b768.at[3], go), (wu, bu, gu), (wd, bd, gd)]
    ins = [pltpu.make_async_copy(a, b, lsem.at[i, 0]) for i, (a, b, _) in enumerate(owns)]
    outs = [pltpu.make_async_copy(b, f.at[s], lsem.at[i, 1]) for i, (_, b, f) in enumerate(owns)]
    more = [(x_in, xb.at[x]), (seg_in, segb.at[x]), (small, sb.at[s])]
    more = [pltpu.make_async_copy(a, b, lsem.at[6 + i, 0]) for i, (a, b) in enumerate(more)]
    for cp in more + ins[:3]:
        cp.start()
    for a, b in zip(ins[:3], outs[:3]):
        a.wait()
        b.start()
    for cp in more:
        cp.wait()

    def weight(i):
        for cp in ccp[i]:
            cp.wait_recv()
        outs[i].wait()
        cp = pltpu.make_async_copy((gq, gk, gv)[i], wb.at[i], wsem.at[i])
        cp.start()
        cp.wait()

    def whole_weight(i):
        return wb[i].reshape(768, 768)

    pump(0)
    pump(1)
    for cp in ins[3:]:
        cp.start()
    pump(2)
    for a, b in zip(ins[3:], outs[3:]):
        a.wait()
        b.start()
    for cp in cps[2:]:
        cp.wait_recv()
    row = lax.broadcasted_iota(jnp.int32, (192, 768), 0)
    col = lax.broadcasted_iota(jnp.int32, (192, 768), 1)
    total = jnp.zeros((16, 768), F32)
    for i in range(4):
        pick = jnp.where(col == row + 192 * i, 1.0, 0.0).astype(BF)
        total = total + dot(sb[i, :, 0:192], pick)
    vecs[...] = total
    for i in range(4):
        vecs[8 + i : 9 + i, :] = sb[i].astype(F32)[8:9, :]

    def project(i, half, fn):
        w = whole_weight(i)
        for r in range(2):
            fn(256 * r, dot(xb[half, 256 * r : 256 * r + 256, :], w))

    weight(0)

    def put_q(r, v):
        qb[r : r + 256, :] = ((v + vecs[0:1, :]).astype(BF).astype(F32) * 0.125).astype(BF)

    project(0, x, put_q)
    pump(3)
    weight(1)

    def put(dst, half, bias_row):
        def fn(r, v):
            if bias_row is not None:
                v = v + vecs[bias_row : bias_row + 1, :]
            dst[pl.ds(pl.multiple_of(half * 512 + r, 256), 256), :] = v.astype(BF)

        return fn

    project(1, x, put(kb, x, None))
    pump(4)
    weight(2)
    project(2, x, put(vb, x, 1))
    cps[0].wait_recv()
    cps[1].wait_recv()
    project(1, 1 - x, put(kb, 1 - x, None))
    pump(5)
    project(2, 1 - x, put(vb, 1 - x, 1))

    def pair(i):
        v = segb[i].astype(F32)
        r = lax.broadcasted_iota(jnp.int32, (16, 512), 0)
        return jnp.where(r == 0, v, jnp.where(r == 1, 1.0 - v, 0.0)).astype(BF)

    mine = pair(x)
    for i in range(2):
        same = dot(mine, pair(i), TN)
        bias[:, 512 * i : 512 * i + 512] = (same - 1.0) * -far_value
    saves = [
        pltpu.make_async_copy(a, b, osem.at[i])
        for i, (a, b) in enumerate(((xb, x_out), (qb, q_out), (kb, k_out), (vb, v_out)))
    ]
    for cp in saves:
        cp.start()

    def pcp(h):
        return pltpu.make_async_copy(pb.at[h % 2], p_out.at[pl.ds(2 * h, 2)], psem.at[h])

    def attn(h, carry):
        cs = pl.ds(pl.multiple_of(h * 128, 128), 128)

        @pl.when(h >= 2)
        def _():
            pcp(jnp.maximum(h - 2, 0)).wait()

        qq, kk, vv = qb[:, cs], kb[:, cs], vb[:, cs]
        parts = []
        for i in range(2):
            cols = slice(64 * i, 64 * i + 64)
            sc = dot(qq[:, cols], kk[:, cols], NT) + bias[...]
            m = jnp.max(sc, axis=1, keepdims=True)
            e = jnp.exp(sc - m)
            p = (e * (1.0 / jnp.sum(e, axis=1, keepdims=True))).astype(BF)
            pb[h % 2, i] = p
            parts.append(dot(p, vv[:, cols]))
        mixb[:, cs] = jnp.concatenate(parts, axis=1).astype(BF)
        pcp(h).start()
        for i in range(6):

            @pl.when(h == i)
            def _(i=i):
                pump(6 + i)

        return carry

    lax.fori_loop(0, 6, attn, 0)
    mix_cp = pltpu.make_async_copy(mixb, mix_out, osem.at[4])
    mix_cp.start()
    for t in range(12, n + L2):
        pump(t)
    for cp in cps:
        cp.wait_send()
    for k in range(n):
        for cp in ccp[k]:
            cp.wait_send()
            if k >= 3:
                cp.wait_recv()
        for cp in [ycp[k]] + relays[k] + seconds[k]:
            cp.wait_send()
    for cp in outs[3:] + saves + [mix_cp, pcp(4), pcp(5)]:
        cp.wait()


def forward_all(*args):
    sd = jax.ShapeDtypeStruct
    n = 10
    dma = pltpu.SemaphoreType.DMA
    vm = pltpu.VMEM
    square = lambda: sd((4, 192, 768), BF)
    return pl.pallas_call(
        forward_kernel,
        name="forward",
        out_shape=[
            square(), square(), square(), square(), sd((4, 192, 3072), BF), sd((4, 768, 768), BF), sd((16, 768), F32),
            sd((2, 512, 768), BF), sd((512, 768), BF), sd((1024, 768), BF), sd((1024, 768), BF), sd((512, 768), BF),
            sd((H, 512, 1024), BF),
        ],
        in_specs=[ANY] * 9,
        out_specs=[ANY] * 6 + [pl.BlockSpec(memory_space=pltpu.VMEM)] + [ANY] * 6,
        scratch_shapes=[
            vm((4, 192, 768), BF), vm((192, 3072), BF), vm((768, 768), BF), vm((4, 16, 768), BF), vm((2, 512, 768), BF),
            vm((2, 1, 512), jnp.int32), vm((3, 4, 192, 768), BF), vm((512, 768), BF), vm((1024, 768), BF),
            vm((1024, 768), BF), vm((512, 768), BF), vm((2, 2, 512, 1024), BF), vm((512, 1024), F32),
            dma((n,)), dma((n,)), dma((n, 4)), dma((n, 4)), dma((n, 5)), dma((n, 5)), dma((5,)), dma((5,)),
            dma((9, 2)), dma((3,)), dma((5,)), dma((6,)),
        ],
        compiler_params=pltpu.CompilerParams(collective_id=0, has_side_effects=True, vmem_limit_bytes=60 * 2**20),
    )(*args)


NCH = 24
CW = 384
LAGS = (2, 4, 6, 8, 10, 12)


def add_into(dst, src, rows, step=32):
    def body(i, carry):
        r = pl.ds(pl.multiple_of(i * step, step), step)
        dst[r, :] = (dst[r, :].astype(F32) + src[r, :].astype(F32)).astype(BF)
        return carry

    lax.fori_loop(0, rows // step, body, 0)


def backward_kernel(
    gd, gffn_in, gmid_in, slope_in, hid_in, z_in, q_in, k_in, v_in, mix_in, p_in, x_in,
    wd, wu, wo, wq, wk, wv, vecs, vec0,
    o_wd, o_wu, o_wo, o_wv, o_wk, o_wq, vec_out, own_out, gx_out,
    kbuf, gbuf, cbuf, ybuf, xbuf, z0buf, z1buf, fin,
    wt, st, gf, hid, zf, gp, gh, tr, qb, kb, vb, mixb, dk, dv, pb, xt, vbuf, vval,
    ksem, csend, crecv, send, recv, vsend, vrecv, gsend, grecv, osem, lsem, wsem, psem,
):
    me = Place()
    x, y, c, zb, z, s = me.x, me.y, me.c, me.zb, me.z, me.s

    def load(i, src, dst):
        return pltpu.make_async_copy(src, dst, lsem.at[i])

    l_gf, l_gh, l_hid = load(0, gffn_in, gf), load(1, gmid_in, gh), load(2, hid_in, hid)
    l_z, l_q, l_k, l_v = load(3, z_in, zf), load(4, q_in, qb), load(5, k_in, kb), load(6, v_in, vb)
    l_mix, l_x = load(7, mix_in, mixb), load(8, x_in, kb)
    own_cp = load(9, gh, own_out)

    def wdcp(j):
        return pltpu.make_async_copy(wd.at[pl.ds(pl.multiple_of(768 * j, 768), 768), :], wt.at[j % 2], wsem.at[0, j])

    def wucp(j):
        return pltpu.make_async_copy(wu.at[:, pl.ds(pl.multiple_of(768 * j, 768), 768)], wt.at[2 + j % 2], wsem.at[1, j])

    def slcp(j):
        return pltpu.make_async_copy(slope_in.at[:, pl.ds(pl.multiple_of(768 * j, 768), 768)], st.at[j % 2], wsem.at[2, j])

    def pcp(h):
        return pltpu.make_async_copy(p_in.at[pl.ds(2 * h, 2)], pb.at[h % 2], psem.at[h])

    w_o = pltpu.make_async_copy(wo, wt.at[0], wsem.at[3, 0])
    w_k = pltpu.make_async_copy(wk, wt.at[2], wsem.at[3, 1])
    w_v = pltpu.make_async_copy(wv, wt.at[1], wsem.at[3, 2])
    w_q = pltpu.make_async_copy(wq, wt.at[3], wsem.at[3, 3])

    def columns(k):
        return pl.ds(pl.multiple_of(k % 2 * CW, CW), CW)

    def source(k, sh):
        cs = columns(k)
        if isinstance(k, int) and k < 8:
            return gd.at[sh, pl.ds(192 * (k // 2), 192), cs]
        return gbuf.at[k // 2 - 4, sh, :, cs]

    def ccp(k, yy):
        return remote(source(k, 2 * yy + 1 - c), cbuf.at[k, yy], csend.at[k, yy], crecv.at[k, yy], me.core_p)

    def kcp(k, yy):
        return pltpu.make_async_copy(source(k, 2 * yy + c), kbuf.at[k, yy], ksem.at[k, yy])

    def core_start(k):
        for yy in range(2):
            ccp(k, yy).start()

    def bits(k):
        e = (k + 1) % 2
        return e, x + e * (zb - x), zb + e * (x - zb)

    def rows(a, n):
        return pl.ds(pl.multiple_of(a * n, 16), n)

    def ycp(k):
        return remote(cbuf.at[k, 1 - y], ybuf.at[k], send.at[0, k], recv.at[0, k], me.y_p)

    def p1cp(k):
        e, b1, b2 = bits(k)
        p = (z + e * (1 - 2 * zb), s, x + (1 - e) * (1 - 2 * x))
        return remote(ybuf.at[k, rows(1 - b1, 96), :], xbuf.at[k], send.at[1, k], recv.at[1, k], p)

    def second(k):
        e = (k + 1) % 2
        return (z + (1 - e) * (1 - 2 * zb), s, x + e * (1 - 2 * x))

    def p2cp(k):
        e, b1, b2 = bits(k)
        return remote(xbuf.at[k, rows(1 - b2, 48), :], z0buf.at[k], send.at[2, k], recv.at[2, k], second(k))

    def z1cp(k):
        return remote(z0buf.at[k], z1buf.at[k], send.at[3, k], recv.at[3, k], me.z1_p)

    def a2cp(k):
        e, b1, b2 = bits(k)
        r = fin.at[k, rows(2 * b1 + b2, 48), :]
        return remote(r, r, send.at[4, k], recv.at[4, k], second(k))

    def a1cp(k):
        e, b1, b2 = bits(k)
        r = fin.at[k, rows(b1, 96), :]
        p = (z + e * (1 - 2 * zb), s, x + (1 - e) * (1 - 2 * x))
        return remote(r, r, send.at[5, k], recv.at[5, k], p)

    def branch(cond, fn):
        if isinstance(cond, bool):
            if cond:
                fn()
        else:
            pl.when(cond)(fn)

    def out_copy(k, act):
        def wd_out():
            kk = jnp.minimum(k, 7) // 2
            o = o_wd.at[pl.ds(pl.multiple_of(192 * kk, 192), 192), columns(k)]
            act(pltpu.make_async_copy(fin.at[k], o, osem.at[k]))

        def wu_out():
            kk = jnp.clip(k - 10, 0, 7)
            o = o_wu.at[:, pl.ds(pl.multiple_of(CW * kk, CW), CW)]
            act(pltpu.make_async_copy(fin.at[k], o, osem.at[k]))

        branch(k < 8, wd_out)
        both = (10 <= k < 18) if isinstance(k, int) else jnp.logical_and(k >= 10, k < 18)
        branch(both, wu_out)
        for i, o in ((4, o_wo), (9, o_wv), (10, o_wk), (11, o_wq)):
            branch(k // 2 == i, lambda o=o: act(pltpu.make_async_copy(fin.at[k], o.at[:, columns(k)], osem.at[k])))

    def pump(t):
        def at(d, fn):
            k = t - d
            if isinstance(k, int):
                if 0 <= k < NCH:
                    fn(k)
            else:
                pl.when(jnp.logical_and(k >= 0, k < NCH))(lambda: fn(jnp.clip(k, 0, NCH - 1)))

        def core(k):
            for yy in range(2):
                remote(cbuf.at[k, yy], cbuf.at[k, yy], csend.at[k, yy], crecv.at[k, yy], me.core_p).wait_recv()

            def first():
                kk = jnp.minimum(k, 7)
                for yy in range(2):
                    pltpu.make_async_copy(kbuf.at[kk, yy], kbuf.at[kk, yy], ksem.at[kk, yy]).wait()
                    add_into(cbuf.at[k, yy], kbuf.at[kk, yy], 192)

            def later():
                kk = jnp.maximum(k - 8, 0) // 2
                for yy in range(2):
                    add_into(cbuf.at[k, yy], gbuf.at[kk, 2 * yy + c, :, columns(k)], 192)

            branch(k < 8, first)
            branch(k >= 8, later)

        def s_p1(k):
            e, b1, b2 = bits(k)
            p1cp(k).wait_recv()
            add_into(xbuf.at[k], ybuf.at[k, rows(b1, 96), :], 96)
            p2cp(k).start()

        def s_p2(k):
            e, b1, b2 = bits(k)
            p2cp(k).wait_recv()
            add_into(z0buf.at[k], xbuf.at[k, rows(b2, 48), :], 48, 16)
            z1cp(k).start()

        def s_z1(k):
            e, b1, b2 = bits(k)
            z1cp(k).wait_recv()
            fin[k, rows(2 * b1 + b2, 48), :] = (z0buf[k].astype(F32) + z1buf[k].astype(F32)).astype(BF)
            a2cp(k).start()

        def s_a2(k):
            a2cp(k).wait_recv()
            a1cp(k).start()

        def s_a1(k):
            a1cp(k).wait_recv()
            out_copy(k, lambda cp: cp.start())

        def s_y(k):
            ycp(k).wait_recv()
            add_into(ybuf.at[k], cbuf.at[k, y], 192)
            p1cp(k).start()

        at(0, core)
        for lag, stage in zip(LAGS, (s_y, s_p1, s_p2, s_z1, s_a2, s_a1)):
            at(lag, stage)
        at(0, lambda k: ycp(k).start())

    greet([me.core_p, me.y_p, me.x_p, me.z0_p, me.z1_p])

    def first_chunks(ks):
        for k in ks:
            core_start(k)
            for yy in range(2):
                kcp(k, yy).start()

    first_chunks((0, 1))
    l_gf.start()
    wdcp(0).start()
    slcp(0).start()
    l_hid.start()
    pump(0)
    first_chunks((2, 3))
    wucp(0).start()
    l_gh.start()
    pump(1)
    first_chunks((4, 5, 6, 7))
    wdcp(1).start()
    slcp(1).start()
    wucp(1).start()
    vval[0] = vec0[...]

    def transposed(dst, src, n):
        for i in range(n // 256):
            dst[:, 256 * i : 256 * i + 256] = src[256 * i : 256 * i + 256, :].T

    def weight_grad(lhs, rhs, k):
        def body(n, carry):
            cs = pl.ds(pl.multiple_of(n * 256, 256), 256)
            r = dot(lhs[...], rhs[:, cs]).astype(BF)
            for sh in range(4):
                gbuf[k - 4, sh, :, cs] = r[192 * sh : 192 * sh + 192]
            return carry

        lax.fori_loop(0, 3, body, 0)
        core_start(2 * k)
        core_start(2 * k + 1)

    def blocks(n, step, fn, init):
        return lax.fori_loop(0, n // step, lambda i, a: fn(pl.ds(pl.multiple_of(i * step, step), step), a), init)

    zero = jnp.zeros((1, D), F32)
    l_gf.wait()
    l_hid.wait()
    transposed(tr, hid, 512)
    l_gh.wait()

    def ff(j):
        return pl.ds(pl.multiple_of(768 * j, 768), 768)

    def ffn(j, carry):
        wdcp(j).wait()
        slcp(j).wait()
        sl = j % 2

        def up(r, a):
            t = (dot(gf[r, :], wt[sl], NT) * st[sl, r, :].astype(F32)).astype(BF)
            gp[r, ff(j)] = t
            return a + jnp.sum(t.astype(F32), 0, keepdims=True)

        vval[0, pl.ds(8 + j, 1), :] = blocks(512, 256, up, zero)
        wucp(j).wait()

        def down(r, a):
            gh[r, :] = gh[r, :] + dot(gp[r, ff(j)], wt[2 + sl], NT)
            return a

        blocks(512, 256, down, 0)

        @pl.when(j < 2)
        def _():
            jj = jnp.minimum(j + 2, 3)
            wdcp(jj).start()
            slcp(jj).start()
            wucp(jj).start()

        @pl.when(j == 2)
        def _():
            w_o.start()
            w_k.start()

        @pl.when(j == 3)
        def _():
            w_v.start()
            w_q.start()

        for i, cps in enumerate(((l_z, l_mix, l_q), (l_k, pcp(0)), (l_v, pcp(1)))):

            @pl.when(j == i)
            def _(cps=cps):
                for cp in cps:
                    cp.start()

        pump(2 + j)
        return carry

    def up_grad(j):
        weight_grad(tr, gp.at[:, ff(j)], 5 + j)

    lax.fori_loop(0, 4, ffn, 0)

    l_z.wait()
    l_mix.wait()
    gain = vecs[3:4, :]

    def norm(r, a):
        zz = zf[r, :]
        m = jnp.mean(zz, -1, keepdims=True)
        zz = zz - m
        inv = lax.rsqrt(jnp.mean(zz * zz, -1, keepdims=True) + norm_eps)
        n = zz * inv
        e = gh[r, :]
        ge = e * gain
        g = (ge - jnp.mean(ge, -1, keepdims=True) - n * jnp.mean(ge * n, -1, keepdims=True)) * inv
        gh[r, :] = g
        low = g.astype(BF)
        gf[r, :] = low
        total = lambda v: jnp.sum(v, 0, keepdims=True)
        return a[0] + total(low.astype(F32)), a[1] + total(e * n), a[2] + total(e)

    sums = blocks(512, 64, norm, (zero, zero, zero))
    for i in range(3):
        vval[0, 2 + i : 3 + i, :] = sums[i]
    transposed(xt, mixb, 512)
    pump(6)
    weight_grad(xt.at[:, 0:512], gf, 4)
    w_o.wait()

    def mixg(r, a):
        hid[r, :] = dot(gf[r, :], wt[0], NT).astype(BF)
        return a

    blocks(512, 256, mixg, 0)
    l_q.wait()
    l_k.wait()
    l_v.wait()
    pump(7)
    up_grad(0)
    pump(8)

    def attn(h, carry):
        cs = pl.ds(pl.multiple_of(h * 128, 128), 128)
        pcp(h).wait()
        g = hid[:, cs]
        prod = g.astype(F32) * mixb[:, cs].astype(F32)
        gt = g.T
        qt = qb[:, cs].T
        kk = kb[:, cs]
        vv = vb[:, cs]
        dqs, dks, dvs = [], [], []
        for i in range(2):
            cols = slice(64 * i, 64 * i + 64)
            p = pb[h % 2, i]
            delta = jnp.sum(prod[:, cols], axis=1, keepdims=True)
            dp = dot(g[:, cols], vv[:, cols], NT)
            gs = (p.astype(F32) * (dp - delta)).astype(BF)
            dqs.append(dot(gs, kk[:, cols]) * 0.125)
            dks.append(dot(qt[cols, :], gs))
            dvs.append(dot(gt[cols, :], p))
        gf[:, cs] = jnp.concatenate(dqs, axis=1).astype(BF)
        dk[:, cs] = jnp.concatenate(dks, axis=0).T.astype(BF)
        dv[:, cs] = jnp.concatenate(dvs, axis=0).T.astype(BF)

        @pl.when(h < 4)
        def _():
            pcp(jnp.minimum(h + 2, 5)).start()

        pl.when(h % 2 == 1)(lambda: up_grad((h + 1) // 2))
        pump(9 + h)
        return carry

    lax.fori_loop(0, 6, attn, 0)
    w_k.wait()
    w_v.wait()

    def gxcp(i):
        r = pl.ds(32 * i, 32)
        return remote(hid.at[r, :], gx_out.at[r, :], gsend.at[i], grecv.at[i], me.x_p)

    for i in range(2):
        r = pl.ds(pl.multiple_of((1 - x) * 512 + 256 * i, 256), 256)
        hid[256 * i : 256 * i + 256, :] = (dot(dk[r, :], wt[2], NT) + dot(dv[r, :], wt[1], NT)).astype(BF)
    l_x.start()

    def colsum(src):
        return lambda r, a: a + jnp.sum(src[r, :].astype(F32), 0, keepdims=True)

    vval[0, 0:1, :] = blocks(512, 128, colsum(gf), zero)
    vval[0, 1:2, :] = blocks(1024, 128, colsum(dv), zero)
    vps = (me.core_p, me.y_p, me.x_p, me.z0_p, me.z1_p)
    vcps = [remote(vval.at[b], vbuf.at[b], vsend.at[b], vrecv.at[b], vps[b]) for b in range(5)]

    def own(i, carry):
        r = pl.ds(pl.multiple_of(256 * i, 256), 256)
        ro = pl.ds(pl.multiple_of(x * 512 + 256 * i, 256), 256)
        gh[r, :] = gh[r, :] + dot(gf[r, :], wt[3], NT) + dot(dk[ro, :], wt[2], NT) + dot(dv[ro, :], wt[1], NT)
        return carry

    last = NCH + LAGS[-1]
    for t in range(15, last):
        if t == 16:
            l_x.wait()
            transposed(xt, kb, 1024)
            weight_grad(xt, dv, 9)
        if t == 17:
            weight_grad(xt, dk, 10)
        if t == 18:
            weight_grad(xt.at[:, pl.ds(pl.multiple_of(x * 512, 512), 512)], gf, 11)
            w_q.wait()
        if t in (19, 20):
            own(t - 19, 0)
        if t == 21:
            own_cp.start()
        pump(t)
        if 0 <= t - 15 < 16:
            gxcp(t - 15).start()
        b = (t - 19) // 2
        if t == 17:
            vcps[0].start()
        if t % 2 == 1 and 0 <= b < 5:
            vcps[b].wait_recv()
            if b < 4:
                vval[b + 1] = vval[b] + vbuf[b]
                vcps[b + 1].start()
            else:
                vec_out[...] = vval[b] + vbuf[b]

    def finish(k, carry):
        for f in (ycp, p1cp, p2cp, z1cp, a2cp, a1cp):
            f(k).wait_send()
        for yy in range(2):
            remote(cbuf.at[k, yy], cbuf.at[k, yy], csend.at[k, yy], crecv.at[k, yy], me.core_p).wait_send()
        out_copy(k, lambda cp: cp.wait())
        return carry

    lax.fori_loop(0, NCH, finish, 0)
    for cp in vcps:
        cp.wait_send()
    own_cp.wait()
    for i in range(16):
        gxcp(i).wait()


def backward_all(*args):
    sd = jax.ShapeDtypeStruct
    dma = pltpu.SemaphoreType.DMA
    vm = pltpu.VMEM
    vspec = pl.BlockSpec(memory_space=pltpu.VMEM)
    one = lambda: sd((192, 768), BF)
    half = lambda: vm((512, 768), BF)
    full = lambda: vm((1024, 768), BF)
    return pl.pallas_call(
        backward_kernel,
        name="backward",
        out_shape=[
            sd((768, 768), BF), sd((192, 3072), BF), one(), one(), one(), one(),
            sd((16, 768), F32), sd((512, 768), F32), sd((512, 768), BF),
        ],
        in_specs=[ANY] * 18 + [vspec] * 2,
        out_specs=[ANY] * 6 + [vspec, ANY, ANY],
        scratch_shapes=[
            vm((8, 2, 192, CW), BF), vm((8, 4, 192, 768), BF), vm((NCH, 2, 192, CW), BF), vm((NCH, 192, CW), BF),
            vm((NCH, 96, CW), BF), vm((NCH, 48, CW), BF), vm((NCH, 48, CW), BF), vm((NCH, 192, CW), BF),
            vm((4, 768, 768), BF), vm((2, 512, 768), BF), half(), half(), vm((512, 768), F32), vm((512, FF), BF), vm((512, 768), F32),
            vm((768, 512), BF), half(), full(), full(), half(), full(), full(), vm((2, 2, 512, 1024), BF),
            vm((768, 1024), BF), vm((5, 16, 768), F32), vm((5, 16, 768), F32),
            dma((8, 2)), dma((NCH, 2)), dma((NCH, 2)), dma((6, NCH)), dma((6, NCH)), dma((5,)), dma((5,)), dma((16,)), dma((16,)),
            dma((NCH,)), dma((10,)), dma((4, 4)), dma((6,)),
        ],
        compiler_params=pltpu.CompilerParams(collective_id=1, has_side_effects=True, vmem_limit_bytes=63 * 2**20),
    )(*args)


def finish_kernel(wd, wu, wo, wv, wk, wq, own, gx, o_wd, o_wu, o_wo, o_wv, o_wk, o_wq, o_x):
    for a, b in ((wd, o_wd), (wu, o_wu), (wo, o_wo), (wv, o_wv), (wk, o_wk), (wq, o_wq)):
        b[...] = a[...].astype(F32)
    o_x[...] = own[...] + gx[...].astype(F32)


def finish_all(*args):
    steps = 4
    block = lambda a: pl.BlockSpec((a.shape[0] // steps, a.shape[1]), lambda i: (i, 0))
    return pl.pallas_call(
        finish_kernel,
        name="finish",
        grid=(steps,),
        out_shape=[jax.ShapeDtypeStruct(a.shape, F32) for a in args[:7]],
        in_specs=[block(a) for a in args],
        out_specs=[block(a) for a in args[:7]],
    )(*args)


def layer_norm(total_rows, gain_vec, shift_vec):
    row_mean = jnp.mean(total_rows, -1, keepdims=True)
    centred = total_rows - row_mean
    variance = jnp.mean(centred * centred, -1, keepdims=True)
    inv_std = lax.rsqrt(variance + norm_eps)
    normed = centred * inv_std
    return (normed * gain_vec + shift_vec, normed, inv_std)


def norm_grad(grad_in, normed, inv_std, gain_vec):
    scaled = grad_in * gain_vec
    centred_grad = (
        scaled
        - jnp.mean(scaled, -1, keepdims=True)
        - normed * jnp.mean(scaled * normed, -1, keepdims=True)
    )
    return (centred_grad * inv_std, jnp.sum(grad_in * normed, 0), jnp.sum(grad_in, 0))


def shards(
    inputs, segments, cotangent, w_query, b_query, w_key, w_value, b_value, w_out, b_out,
    gain_one, shift_one, w_up, b_up, w_down, b_down, gain_two, shift_two,
):
    x_own = inputs[0]
    singles = (b_query, b_value, b_out, gain_one, shift_one, b_down, gain_two, shift_two, b_up)
    small = sum(jnp.pad(a, (D * i, 16 * D - D * i - a.shape[0])) for i, a in enumerate(singles)).reshape(16, D)
    wq, wk, wv, wo, wu, wd, vecs, xf, q8, keys, values, mixture, probs = forward_all(
        w_query, w_key, w_value, w_out, w_up, w_down, small, x_own, segments
    )
    wq, wk, wv, wo, wu, wd = (w.reshape(-1, w.shape[-1]) for w in (wq, wk, wv, wo, wu, wd))
    bo, g1, s1, bd, g2, s2 = (vecs[i : i + 1] for i in range(2, 8))
    bu = vecs[8:12].reshape(1, FF)
    x_all = xf.reshape(-1, D)

    attn_out = dot(mixture, wo) + bo
    z_one = x_own.astype(F32) + attn_out
    norm_one, _, _ = layer_norm(z_one, g1, s1)
    hidden_low = norm_one.astype(BF)
    pre_act = dot(hidden_low, wu) + bu
    phi = 0.5 * (1.0 + lax.erf(pre_act * (2.0**-0.5)))
    act_low = (pre_act * phi).astype(BF)
    slope = (phi + pre_act * jnp.exp(-0.5 * pre_act * pre_act) * (2 * math.pi) ** -0.5).astype(BF)
    ffn_out = dot(act_low, wd) + bd
    result, normed_two, inv_two = layer_norm(norm_one + ffn_out, g2, s2)

    grad_mid, d_g2, d_s2 = norm_grad(cotangent[0].astype(F32), normed_two, inv_two, g2)
    grad_ffn = grad_mid.astype(BF)
    d_bd = jnp.sum(grad_ffn.astype(F32), 0)
    d_wd = dot(act_low, grad_ffn, TN).astype(BF)
    vec0 = jnp.zeros((16, D), F32)
    for i, a in ((5, d_bd), (6, d_g2), (7, d_s2)):
        vec0 = vec0 + jnp.pad(a.reshape(1, D), ((i, 15 - i), (0, 0)))
    o_wd, o_wu, o_wo, o_wv, o_wk, o_wq, vec, own_part, gx = backward_all(
        d_wd.reshape(4, -1, D), grad_ffn, grad_mid, slope, hidden_low, z_one, q8, keys, values, mixture, probs, x_all,
        wd, wu, wo, wq, wk, wv, vecs, vec0,
    )
    o_wd, o_wu, o_wo, o_wv, o_wk, o_wq, grad_input = finish_all(o_wd, o_wu, o_wo, o_wv, o_wk, o_wq, own_part, gx)
    sh = lax.axis_index("shard")
    mine = lax.dynamic_slice(vec[:8], (0, sh * 192), (8, 192))
    o_bq, o_bv, o_bo, o_g1, o_s1, o_bd, o_g2, o_s2 = (mine[i] for i in range(8))
    o_bu = lax.dynamic_index_in_dim(vec[8:12], sh, 0, False)
    return (
        result.astype(BF)[None], grad_input[None], o_wq, o_bq, o_wk, o_wv, o_bv, o_wo, o_bo,
        o_g1, o_s1, o_wu, o_bu, o_wd, o_bd, o_g2, o_s2,
    )


def make(mesh, body):
    in_specs = (
        P(("rep", "shard"), "seq", None), P(("rep", "shard"), "seq"), P(("rep", "shard"), "seq", None),
        P("shard", None), P("shard"), P("shard", None), P("shard", None), P("shard"), P("shard", None), P("shard"),
        P("shard"), P("shard"), P("shard", None), P("shard"), P("shard", None), P("shard"), P("shard"), P("shard"),
    )
    out_specs = (
        P(("rep", "shard"), "seq", None), P(("rep", "shard"), "seq", None),
        P("shard", None), P("shard"), P("shard", None), P("shard", None), P("shard"), P("shard", None), P("shard"),
        P("shard"), P("shard"), P("shard", None), P("shard"), P("shard", None), P("shard"), P("shard"), P("shard"),
    )
    return jax.shard_map(body, mesh=mesh, in_specs=in_specs, out_specs=out_specs, check_vma=False)


param_names = (
    "w_query",
    "b_query",
    "w_key",
    "w_value",
    "b_value",
    "w_out",
    "b_out",
    "gain_one",
    "shift_one",
    "w_up",
    "b_up",
    "w_down",
    "b_down",
    "gain_two",
    "shift_two",
)


def as_sent(x):
    return jax.tree.map(lambda a: a.astype(jnp.bfloat16) if a.dtype == jnp.float32 else a, x)


def general_layer_norm(total_rows, gain_vec, shift_vec):
    row_mean = jnp.mean(total_rows, -1, keepdims=True)
    centred = total_rows - row_mean
    variance = jnp.mean(centred * centred, -1, keepdims=True)
    inv_std = lax.rsqrt(variance + norm_eps)
    normed = centred * inv_std
    return (normed * gain_vec + shift_vec, normed, inv_std)


def general_norm_grad(grad_in, normed, inv_std, gain_vec):
    scaled = grad_in * gain_vec
    centred_grad = (
        scaled
        - jnp.mean(scaled, -1, keepdims=True)
        - normed * jnp.mean(scaled * normed, -1, keepdims=True)
    )
    return (centred_grad * inv_std, jnp.sum(grad_in * normed, 0), jnp.sum(grad_in, 0))


def inner_rows(left, right):
    return lax.dot_general(
        left, right, (((0,), (0,)), ((), ())), preferred_element_type=jnp.float32
    )


def times_transposed(left, matrix):
    return lax.dot_general(
        left, matrix, (((1,), (1,)), ((), ())), preferred_element_type=jnp.float32
    )


def gelu_exact(value):
    return jax.nn.gelu(value, approximate=False)


def general_shards(
    inputs,
    segments,
    cotangent,
    w_query,
    b_query,
    w_key,
    w_value,
    b_value,
    w_out,
    b_out,
    gain_one,
    shift_one,
    w_up,
    b_up,
    w_down,
    b_down,
    gain_two,
    shift_two,
):
    score_scale = DH ** (-0.5)
    token_rows = inputs[0]
    row_count = token_rows.shape[0]
    own_seg = segments[0].astype(jnp.float32)
    local_params = (
        w_query,
        b_query,
        w_key,
        w_value,
        b_value,
        w_out,
        b_out,
        gain_one,
        shift_one,
        w_up,
        b_up,
        w_down,
        b_down,
        gain_two,
        shift_two,
    )
    gathered = (
        lax.all_gather(local_params[0], "shard", axis=0, tiled=True),
        lax.all_gather(local_params[1], "shard", axis=0, tiled=True),
        lax.all_gather(local_params[2], "shard", axis=0, tiled=True),
        lax.all_gather(local_params[3], "shard", axis=0, tiled=True),
        lax.all_gather(local_params[4], "shard", axis=0, tiled=True),
        lax.all_gather(local_params[5], "shard", axis=0, tiled=True),
        lax.all_gather(local_params[6], "shard", axis=0, tiled=True),
        lax.all_gather(local_params[7], "shard", axis=0, tiled=True),
        lax.all_gather(local_params[8], "shard", axis=0, tiled=True),
        lax.all_gather(local_params[9], "shard", axis=0, tiled=True),
        lax.all_gather(local_params[10], "shard", axis=0, tiled=True),
        lax.all_gather(local_params[11], "shard", axis=0, tiled=True),
        lax.all_gather(local_params[12], "shard", axis=0, tiled=True),
        lax.all_gather(local_params[13], "shard", axis=0, tiled=True),
        lax.all_gather(local_params[14], "shard", axis=0, tiled=True),
    )
    weights = dict(zip(param_names, gathered))

    def vector(name):
        return weights[name].astype(jnp.float32)

    q_wide = jnp.dot(token_rows, weights["w_query"], preferred_element_type=jnp.float32) + vector(
        "b_query"
    )
    queries = q_wide.astype(jnp.bfloat16)
    key_rows = jnp.dot(token_rows, weights["w_key"], preferred_element_type=jnp.float32).astype(
        jnp.bfloat16
    )
    value_rows = (
        jnp.dot(token_rows, weights["w_value"], preferred_element_type=jnp.float32)
        + vector("b_value")
    ).astype(jnp.bfloat16)
    seg_wire = segments[0].astype(jnp.bfloat16)
    query_heads = queries.reshape(row_count, H, DH)
    start_state = (
        jnp.full((H, row_count), far_value, jnp.float32),
        jnp.zeros((H, row_count), jnp.float32),
        jnp.zeros((row_count, H, DH), jnp.float32),
    )
    carried = start_state
    piece_keys = lax.all_gather(key_rows, "seq", axis=0, tiled=True)
    piece_values = lax.all_gather(value_rows, "seq", axis=0, tiled=True)
    piece_seg = lax.all_gather(seg_wire, "seq", axis=0, tiled=True)
    piece_rows = piece_keys.shape[0]
    width_blk = math.gcd(piece_rows, 512)
    blocks = piece_rows // width_blk
    key_blocks = piece_keys.reshape(blocks, width_blk, H, DH)
    value_blocks = piece_values.reshape(blocks, width_blk, H, DH)
    seg_blocks = piece_seg.astype(jnp.float32).reshape(blocks, width_blk)

    def update(fold_state, block_item):
        key_blk, value_blk, seg_blk = block_item
        row_peak, row_total, accumulated = fold_state
        scores = (
            jnp.einsum("rhd,khd->hrk", query_heads, key_blk, preferred_element_type=jnp.float32)
            * score_scale
        )
        allowed = own_seg[:, None] == seg_blk[None, :]
        scores = jnp.where(allowed[None], scores, far_value)
        new_peak = jnp.maximum(row_peak, jnp.max(scores, -1))
        factor = jnp.exp(row_peak - new_peak)
        exp_scores = jnp.exp(scores - new_peak[:, :, None])
        row_total = row_total * factor + jnp.sum(exp_scores, -1)
        block_mix = jnp.einsum(
            "hrk,khd->rhd",
            exp_scores.astype(jnp.bfloat16),
            value_blk,
            preferred_element_type=jnp.float32,
        )
        accumulated = accumulated * jnp.transpose(factor)[:, :, None] + block_mix
        return ((new_peak, row_total, accumulated), None)

    carried, unused = lax.scan(update, carried, (key_blocks, value_blocks, seg_blocks))
    row_peak, row_total, accumulated = carried
    mix_wide = (accumulated / jnp.transpose(row_total)[:, :, None]).reshape(row_count, D)
    mixture = mix_wide.astype(jnp.bfloat16)
    log_total = row_peak + jnp.log(row_total)
    attn_out = jnp.dot(mixture, weights["w_out"], preferred_element_type=jnp.float32) + vector(
        "b_out"
    )
    norm_one, normed_one, inv_one = general_layer_norm(
        token_rows.astype(jnp.float32) + attn_out, vector("gain_one"), vector("shift_one")
    )
    hidden_low = norm_one.astype(jnp.bfloat16)
    pre_act = jnp.dot(hidden_low, weights["w_up"], preferred_element_type=jnp.float32) + vector(
        "b_up"
    )
    activated, gelu_pullback = jax.vjp(gelu_exact, pre_act)
    act_low = activated.astype(jnp.bfloat16)
    ffn_out = jnp.dot(act_low, weights["w_down"], preferred_element_type=jnp.float32) + vector(
        "b_down"
    )
    result, normed_two, inv_two = general_layer_norm(
        norm_one + ffn_out, vector("gain_two"), vector("shift_two")
    )
    regathered = (
        lax.all_gather(local_params[0], "shard", axis=0, tiled=True),
        lax.all_gather(local_params[1], "shard", axis=0, tiled=True),
        lax.all_gather(local_params[2], "shard", axis=0, tiled=True),
        lax.all_gather(local_params[3], "shard", axis=0, tiled=True),
        lax.all_gather(local_params[4], "shard", axis=0, tiled=True),
        lax.all_gather(local_params[5], "shard", axis=0, tiled=True),
        lax.all_gather(local_params[6], "shard", axis=0, tiled=True),
        lax.all_gather(local_params[7], "shard", axis=0, tiled=True),
        lax.all_gather(local_params[8], "shard", axis=0, tiled=True),
        lax.all_gather(local_params[9], "shard", axis=0, tiled=True),
        lax.all_gather(local_params[10], "shard", axis=0, tiled=True),
        lax.all_gather(local_params[11], "shard", axis=0, tiled=True),
        lax.all_gather(local_params[12], "shard", axis=0, tiled=True),
        lax.all_gather(local_params[13], "shard", axis=0, tiled=True),
        lax.all_gather(local_params[14], "shard", axis=0, tiled=True),
    )
    backward_set = dict(zip(param_names, regathered))
    grad_out = cotangent[0].astype(jnp.float32)
    grad_mid, grad_gain_two, grad_shift_two = general_norm_grad(
        grad_out, normed_two, inv_two, backward_set["gain_two"].astype(jnp.float32)
    )
    grad_ffn = grad_mid.astype(jnp.bfloat16)
    grad_b_down = jnp.sum(grad_ffn.astype(jnp.float32), 0)
    grad_w_down = inner_rows(act_low, grad_ffn)
    grad_act = times_transposed(grad_ffn, backward_set["w_down"])
    (grad_pre_wide,) = gelu_pullback(grad_act)
    grad_pre = grad_pre_wide.astype(jnp.bfloat16)
    grad_b_up = jnp.sum(grad_pre.astype(jnp.float32), 0)
    grad_w_up = inner_rows(hidden_low, grad_pre)
    grad_hidden = grad_mid + times_transposed(grad_pre, backward_set["w_up"])
    grad_sum_one, grad_gain_one, grad_shift_one = general_norm_grad(
        grad_hidden, normed_one, inv_one, backward_set["gain_one"].astype(jnp.float32)
    )
    grad_attn = grad_sum_one.astype(jnp.bfloat16)
    grad_b_out = jnp.sum(grad_attn.astype(jnp.float32), 0)
    grad_w_out = inner_rows(mixture, grad_attn)
    grad_mixture = times_transposed(grad_attn, backward_set["w_out"]).astype(jnp.bfloat16)
    grad_mix_heads = grad_mixture.reshape(row_count, H, DH)
    row_delta = jnp.transpose(
        jnp.sum((grad_mixture.astype(jnp.float32) * mix_wide).reshape(row_count, H, DH), -1)
    )
    all_keys, all_values, all_seg = (
        lax.all_gather(key_rows, "seq", axis=0, tiled=True),
        lax.all_gather(value_rows, "seq", axis=0, tiled=True),
        lax.all_gather(seg_wire, "seq", axis=0, tiled=True),
    )
    seq_rows = all_keys.shape[0]
    width_all = math.gcd(seq_rows, 512)
    blocks_all = seq_rows // width_all
    key_blocks = all_keys.reshape(blocks_all, width_all, H, DH)
    value_blocks = all_values.reshape(blocks_all, width_all, H, DH)
    seg_blocks = all_seg.astype(jnp.float32).reshape(blocks_all, width_all)

    def block_grads(key_blk, value_blk, seg_blk):
        scores = (
            jnp.einsum("rhd,khd->hrk", query_heads, key_blk, preferred_element_type=jnp.float32)
            * score_scale
        )
        allowed = own_seg[:, None] == seg_blk[None, :]
        scores = jnp.where(allowed[None], scores, far_value)
        probabilities = jnp.exp(scores - log_total[:, :, None])
        grad_probs = jnp.einsum(
            "rhd,khd->hrk", grad_mix_heads, value_blk, preferred_element_type=jnp.float32
        )
        grad_scores = (probabilities * (grad_probs - row_delta[:, :, None])).astype(jnp.bfloat16)
        return (probabilities, grad_scores)

    def back_update(grad_query_acc, block_item):
        key_blk, value_blk, seg_blk = block_item
        back_grad_query_acc = grad_query_acc
        probabilities, grad_scores = block_grads(key_blk, value_blk, seg_blk)
        grad_value_blk = jnp.einsum(
            "hrk,rhd->khd",
            probabilities.astype(jnp.bfloat16),
            grad_mix_heads,
            preferred_element_type=jnp.float32,
        )
        back_grad_query_acc = (
            back_grad_query_acc
            + jnp.einsum("hrk,khd->rhd", grad_scores, key_blk, preferred_element_type=jnp.float32)
            * score_scale
        )
        grad_key_blk = (
            jnp.einsum("hrk,rhd->khd", grad_scores, query_heads, preferred_element_type=jnp.float32)
            * score_scale
        )
        return (back_grad_query_acc, (grad_key_blk, grad_value_blk))

    grad_query_heads, key_value_grads = lax.scan(
        back_update,
        jnp.zeros((row_count, H, DH), jnp.float32),
        (key_blocks, value_blocks, seg_blocks),
    )
    grad_key_all = key_value_grads[0].reshape(seq_rows, D)
    grad_value_all = key_value_grads[1].reshape(seq_rows, D)
    grad_key_rows, grad_value_rows = (
        lax.psum_scatter(
            grad_key_all.astype(jnp.bfloat16), "seq", scatter_dimension=0, tiled=True
        ).astype(jnp.float32),
        lax.psum_scatter(
            grad_value_all.astype(jnp.bfloat16), "seq", scatter_dimension=0, tiled=True
        ).astype(jnp.float32),
    )
    grad_query_low = grad_query_heads.reshape(row_count, D).astype(jnp.bfloat16)
    grad_key_low = grad_key_rows.astype(jnp.bfloat16)
    grad_value_low = grad_value_rows.astype(jnp.bfloat16)
    grad_w_query = inner_rows(token_rows, grad_query_low)
    grad_b_query = jnp.sum(grad_query_low.astype(jnp.float32), 0)
    grad_w_key = inner_rows(token_rows, grad_key_low)
    grad_w_value = inner_rows(token_rows, grad_value_low)
    grad_b_value = jnp.sum(grad_value_low.astype(jnp.float32), 0)
    grad_input = (
        grad_sum_one
        + times_transposed(grad_query_low, backward_set["w_query"])
        + times_transposed(grad_key_low, backward_set["w_key"])
        + times_transposed(grad_value_low, backward_set["w_value"])
    )
    gradients = (
        grad_w_query,
        grad_b_query,
        grad_w_key,
        grad_w_value,
        grad_b_value,
        grad_w_out,
        grad_b_out,
        grad_gain_one,
        grad_shift_one,
        grad_w_up,
        grad_b_up,
        grad_w_down,
        grad_b_down,
        grad_gain_two,
        grad_shift_two,
    )
    owned_grads = (
        lax.psum_scatter(
            gradients[0].astype(jnp.bfloat16), "shard", scatter_dimension=0, tiled=True
        ).astype(jnp.float32),
        lax.psum_scatter(
            gradients[1].astype(jnp.bfloat16), "shard", scatter_dimension=0, tiled=True
        ).astype(jnp.float32),
        lax.psum_scatter(
            gradients[2].astype(jnp.bfloat16), "shard", scatter_dimension=0, tiled=True
        ).astype(jnp.float32),
        lax.psum_scatter(
            gradients[3].astype(jnp.bfloat16), "shard", scatter_dimension=0, tiled=True
        ).astype(jnp.float32),
        lax.psum_scatter(
            gradients[4].astype(jnp.bfloat16), "shard", scatter_dimension=0, tiled=True
        ).astype(jnp.float32),
        lax.psum_scatter(
            gradients[5].astype(jnp.bfloat16), "shard", scatter_dimension=0, tiled=True
        ).astype(jnp.float32),
        lax.psum_scatter(
            gradients[6].astype(jnp.bfloat16), "shard", scatter_dimension=0, tiled=True
        ).astype(jnp.float32),
        lax.psum_scatter(
            gradients[7].astype(jnp.bfloat16), "shard", scatter_dimension=0, tiled=True
        ).astype(jnp.float32),
        lax.psum_scatter(
            gradients[8].astype(jnp.bfloat16), "shard", scatter_dimension=0, tiled=True
        ).astype(jnp.float32),
        lax.psum_scatter(
            gradients[9].astype(jnp.bfloat16), "shard", scatter_dimension=0, tiled=True
        ).astype(jnp.float32),
        lax.psum_scatter(
            gradients[10].astype(jnp.bfloat16), "shard", scatter_dimension=0, tiled=True
        ).astype(jnp.float32),
        lax.psum_scatter(
            gradients[11].astype(jnp.bfloat16), "shard", scatter_dimension=0, tiled=True
        ).astype(jnp.float32),
        lax.psum_scatter(
            gradients[12].astype(jnp.bfloat16), "shard", scatter_dimension=0, tiled=True
        ).astype(jnp.float32),
        lax.psum_scatter(
            gradients[13].astype(jnp.bfloat16), "shard", scatter_dimension=0, tiled=True
        ).astype(jnp.float32),
        lax.psum_scatter(
            gradients[14].astype(jnp.bfloat16), "shard", scatter_dimension=0, tiled=True
        ).astype(jnp.float32),
    )
    owned_grads = jax.tree.map(
        lambda part: part.astype(jnp.float32), lax.psum(as_sent(tuple(owned_grads)), ("rep", "seq"))
    )
    return (result.astype(jnp.bfloat16)[None], grad_input[None]) + tuple(owned_grads)


def solution(mesh):
    if dict(mesh.shape) == {"rep": 4, "shard": 4, "seq": 2}:
        return make(mesh, shards)
    return make(mesh, general_shards)
```
